128 devices in a mesh: tm: 8 (over z_hi, x), space: 16 (over y, z_lo, core).
Axes of the slice: x: 4, y: 4, z: 4 (z_hi: 2, z_lo: 2; z = z_hi * 2 + z_lo), core: 2. Of those that a mesh axis runs over, the one named last changes fastest.
Arguments:
- guess: float32 [16, 3, 192, 64, 128], P('tm', None, 'space'), may hold values from -6 to 6
- source: float32 [16, 3, 192, 64, 128], P('tm', None, 'space'), may hold values from -6 to 6
- regions: int32 [192, 64, 128], P('space'), may hold values from 0 to 3
- conductance: float32 [4], replicated, may hold values from 8 to 32
- reluct: float32 [4], replicated, may hold values from 0.25 to 2
Outputs:
- field: float32 [16, 3, 192, 64, 128], P('tm', None, 'space')
- coarse_residual: float32 [8, 3, 192, 64, 128], P('tm', None, 'space')
The draws below stay inside these ranges and needn't reach their ends.
Inputs may be any that keep to these rules, and one draw needn't show every extreme that they name: `regions`: a region id per cell.
All inputs are finite; a program needn't handle non-finite values.
Results may differ from the reference program's by a relative error of at most 0.0001.
Values sent between devices are 32-bit elements; how exact they have to be, the bound alone decides.
No kernel may reach another device: no remote copies, remote signals or barrier semaphores. Data moves between devices by JAX's collectives and lax.ppermute only.
A program may use at most 128 MiB of HBM per device.

```python
import math
import jax
import jax.numpy as jnp

NY = 64
NZ = 128
STEPS = 2
PICARD = 2
REGIONS = 4
NX = 192
NT = 16
N_TM = 8


def set_ends(result, rng, smallest, top_value):
    extent = result.shape
    place = [jax.random.randint(jax.random.fold_in(rng, axis), (), 0, extent[axis]) for axis in range(len(extent))]
    result = result.at[tuple(place)].set(smallest)
    longest = extent.index(max(extent))
    place[longest] = (place[longest] + 1) % extent[longest]
    return result.at[tuple(place)].set(top_value)


def block_scale(key, dims, split, least, largest):
    factor_of = 1.0
    for dim, parts in split:
        heights = jax.random.uniform(jax.random.fold_in(jax.random.fold_in(key, 6), dim), (parts,), jnp.float32, least / len(split), largest / len(split))
        factor_of = factor_of * jnp.repeat(jnp.exp(heights), dims[dim] // parts).reshape((-1,) + (1,) * (len(dims) - 1 - dim))
    return factor_of


def gaussian(stream_key, shape, spread, reach, cuts=(), held_as=jnp.bfloat16):
    result = spread * jax.random.normal(stream_key, shape, jnp.float32)
    if cuts:
        result = result * block_scale(stream_key, shape, cuts, -0.22, 0.18)
    return jnp.clip(result, -reach, reach).astype(held_as)


def setup_inputs(seed: int = 0) -> dict:
    keys = jax.random.split(jax.random.key(seed), 6)
    guess = gaussian(keys[0], (NT, 3, NX, NY, NZ), 1.0, 6.0, ((0, 8), (2, 16)), jnp.float32)
    source = gaussian(keys[1], (NT, 3, NX, NY, NZ), 1.0, 6.0, ((0, 8), (2, 16)), jnp.float32)
    regions = set_ends(jax.random.randint(keys[2], (NX, NY, NZ), 0, REGIONS), jax.random.fold_in(keys[2], 1), 0, REGIONS - 1).astype(jnp.int32)
    conductance = jnp.clip(jnp.exp(jax.random.uniform(keys[3], (REGIONS,), jnp.float32, math.log(8.0), math.log(32.0))), 8.0, 32.0)
    reluct = jnp.clip(jnp.exp(jax.random.uniform(keys[4], (REGIONS,), jnp.float32, math.log(0.25), math.log(2.0))), 0.25, 2.0)
    return {"guess": guess, "source": source, "regions": regions, "conductance": conductance, "reluct": reluct}


def material(regions, table):
    ids = jnp.arange(table.shape[0]).astype(jnp.int32).reshape(-1, 1, 1, 1)
    return jnp.sum(jnp.where(regions[None] == ids, table.reshape(-1, 1, 1, 1), jnp.float32(0.0)), axis=0)


def neighbour_sum(field):
    widths = [(0, 0)] * (field.ndim - 3) + [(1, 1)] * 3
    padded = jnp.pad(field, widths)
    first = padded[..., 2:, 1:-1, 1:-1] + padded[..., :-2, 1:-1, 1:-1]
    second = padded[..., 1:-1, 2:, 1:-1] + padded[..., 1:-1, :-2, 1:-1]
    third = padded[..., 1:-1, 1:-1, 2:] + padded[..., 1:-1, 1:-1, :-2]
    return (first + second) + third


def advance(old, force, cond, base_nu):
    state = old
    for sweep in range(PICARD):
        square = jnp.sum(state * state, axis=-4)
        nu = base_nu * (1.0 + 0.5 * square / (1.0 + square))
        nu = jnp.expand_dims(nu, -4)
        state = (cond * old + force + nu * neighbour_sum(state)) / (cond + 6.0 * nu)
    return state


def coarse_map(value, cond_coarse, base_nu):
    state = value
    for sweep in range(PICARD):
        state = (cond_coarse * value + base_nu * neighbour_sum(state)) / (cond_coarse + 6.0 * base_nu)
    return state


def reference(guess, source, regions, conductance, reluct):
    cond = material(regions, conductance)
    base_nu = material(regions, reluct)
    shape = (N_TM, STEPS) + guess.shape[1:]
    field_all = guess.reshape(shape)
    force_all = source.reshape(shape)
    points = [field_all[:, i] for i in range(STEPS)]
    forces = [force_all[:, i] for i in range(STEPS)]

    def relax_f(points):
        points = list(points)
        for i in range(1, STEPS):
            points[i] = advance(points[i - 1], forces[i], cond, base_nu)
        return points

    points = relax_f(points)
    points[0] = advance(jnp.roll(points[STEPS - 1], 1, axis=0), forces[0], cond, base_nu)
    points = relax_f(points)
    residual = advance(jnp.roll(points[STEPS - 1], 1, axis=0), forces[0], cond, base_nu) - points[0]
    cond_coarse = cond / STEPS
    correction = jnp.zeros_like(residual)
    for k in range(N_TM):
        correction = coarse_map(jnp.roll(correction, 1, axis=0), cond_coarse, base_nu) + residual
    points[0] = points[0] + correction
    points = relax_f(points)
    field = jnp.stack(points, axis=1).reshape(guess.shape)
    return field, residual
```

```python
import functools

import jax
import jax.numpy as jnp
from jax import lax
from jax.experimental import pallas as pl
from jax.experimental.pallas import tpu as pltpu
from jax.sharding import PartitionSpec as P

LX, NY, NZ = 12, 64, 128
F32 = jnp.float32
ANY = pl.BlockSpec(memory_space=pl.ANY)
SMEM = pl.BlockSpec(memory_space=pltpu.SMEM)


def planes(*lead):
    return jax.ShapeDtypeStruct(tuple(lead) + (NY, NZ), F32)


def vmem(*lead):
    return pltpu.VMEM(tuple(lead) + (NY, NZ), F32)


def copy_all(pairs, sems, base=0):
    copies = [
        pltpu.make_async_copy(src, dst, sems.at[base + n]) for n, (src, dst) in enumerate(pairs)
    ]
    for copy in copies:
        copy.start()
    return copies


def wait_all(copies):
    for copy in copies:
        copy.wait()


def run_copies(pairs, sems, base=0):
    wait_all(copy_all(pairs, sems, base))


def call(kernel, name, args, outs, scratch, n_sems, flops=0):
    in_specs = [SMEM if a.ndim == 1 else ANY for a in args]
    single = not isinstance(outs, (list, tuple))
    return pl.pallas_call(
        kernel,
        name=name,
        out_shape=outs,
        in_specs=in_specs,
        out_specs=ANY if single else [ANY] * len(outs),
        scratch_shapes=list(scratch) + [pltpu.SemaphoreType.DMA((n_sems,))],
        compiler_params=pltpu.CompilerParams(vmem_limit_bytes=40 * 1024 * 1024),
        cost_estimate=pl.CostEstimate(flops=flops, bytes_accessed=4 << 20, transcendentals=0),
    )(*args)


def neighbours(src, at):
    row = lax.broadcasted_iota(jnp.int32, (NY, NZ), 0)
    lane = lax.broadcasted_iota(jnp.int32, (NY, NZ), 1)
    zero = jnp.float32(0.0)
    def of(*lead_i):
        *lead, i = lead_i
        a = src[(*lead, i)]
        first = src[(*lead, i + 1)] + src[(*lead, i - 1)]
        up = jnp.where(row == 0, zero, pltpu.roll(a, 1, 0))
        down = jnp.where(row == NY - 1, zero, pltpu.roll(a, NY - 1, 0))
        left = jnp.where(lane == 0, zero, pltpu.roll(a, 1, 1))
        right = jnp.where(lane == NZ - 1, zero, pltpu.roll(a, NZ - 1, 1))
        return (first + (up + down)) + (left + right)
    return of(*at)


def fine_sweep(src, store, held, cond, nu, lo, hi, force=None):
    def body(i, carry):
        square = src[0, i] * src[0, i] + src[1, i] * src[1, i] + src[2, i] * src[2, i]
        base = nu[i]
        weight = cond[i]
        grown = 1.0 + square
        strong = base * (1.0 + 1.5 * square)
        scale = 1.0 / (weight * grown + 6.0 * strong)
        keep = grown * scale
        spread = strong * scale
        for c in range(3):
            if force is not None:
                fixed = weight * src[c, i] + force[c, i]
                held[c, i] = fixed
            else:
                fixed = held[c, i]
            store(c, i, fixed * keep + neighbours(src, (c, i)) * spread)
        return carry

    lax.fori_loop(lo, hi, body, 0)


def coarse_sweep(src, store, held, keep, spread, off, lo, hi, first, comps):
    def body(i, carry):
        k = keep[i + off]
        s = spread[i + off]
        for lead in comps:
            at = lead + (i,)
            if first:
                fixed = k * src[at]
                held[at] = fixed
            else:
                fixed = held[at]
            store(at, fixed + s * neighbours(src, at))
        return carry

    lax.fori_loop(lo, hi, body, 0)


def lookup(code, table):
    first = jnp.where(code == 1.0, table[0], table[1])
    second = jnp.where(code == 3.0, table[2], table[3])
    return jnp.where(code <= 2.0, first, second)


def materials(code, cond_t, nu_t):
    outside = code == 0.0
    return (
        jnp.where(outside, jnp.float32(1.0), lookup(code, cond_t)),
        jnp.where(outside, jnp.float32(0.0), lookup(code, nu_t)),
    )


def pack_kernel(odd_ref, guess, source, regions, code, a1, b1, a2, b2, reg, cod, sems):
    odd = odd_ref[0]
    run_copies([(regions, reg)], sems)

    def body(i, carry):
        cod[i] = (reg[i] + 1).astype(F32)
        return carry

    lax.fori_loop(0, LX, body, 0)
    pairs = [(cod, code)]
    for one, two, top in ((a1, a2, 1 - odd), (b1, b2, odd)):
        for c in range(3):
            pairs.append((guess.at[0, c, pl.ds(top * (LX - 2), 2)], one.at[pl.ds(2 * c, 2)]))
            pairs.append((source.at[1, c, pl.ds(top * (LX - 1), 1)], one.at[pl.ds(6 + c, 1)]))
            pairs.append((source.at[0, c, pl.ds(top * (LX - 3), 3)], two.at[pl.ds(3 * c, 3)]))
        pairs.append((cod.at[pl.ds(top * (LX - 1), 1)], one.at[pl.ds(9, 1)]))
        pairs.append((cod.at[pl.ds(top * (LX - 7), 7)], two.at[pl.ds(9, 7)]))
    run_copies(pairs, sems)


def first_middle_kernel(cond_t, nu_t, guess, source, code, out, x, y, held, f, cod, cond, nu, sems):
    pairs = [(code.at[pl.ds(2, 8)], cod)]
    pairs += [(guess.at[0, c, pl.ds(2, 8)], x.at[c]) for c in range(3)]
    pairs += [(source.at[1, c, pl.ds(2, 8)], f.at[c]) for c in range(3)]
    run_copies(pairs, sems)

    def body(i, carry):
        cond[i], nu[i] = materials(cod[i], cond_t, nu_t)
        return carry

    lax.fori_loop(1, 7, body, 0)

    def into(buf):
        def store(c, i, value):
            buf[c, i] = value
        return store

    fine_sweep(x, into(y), held, cond, nu, 1, 7, f)
    fine_sweep(y, into(x), held, cond, nu, 2, 6)
    run_copies([(x.at[:, pl.ds(2, 4)], out)], sems)


def first_kernel(odd_ref, cond_t, nu_t, guess, source, code, ra, rb, out_a, out_b, x, y, held, f, cod, cond, nu, sems):
    odd = odd_ref[0]
    n = LX + 4
    pairs = [(code, cod.at[pl.ds(2, LX)])]
    for c in range(3):
        pairs.append((guess.at[0, c], x.at[c, pl.ds(2, LX)]))
        pairs.append((source.at[1, c], f.at[c, pl.ds(2, LX)]))
    for pack, high in ((ra, 1 - odd), (rb, odd)):
        for c in range(3):
            pairs.append((pack.at[pl.ds(2 * c, 2)], x.at[c, pl.ds(high * (n - 2), 2)]))
            pairs.append((pack.at[pl.ds(6 + c, 1)], f.at[c, pl.ds(1 + high * (n - 3), 1)]))
        pairs.append((pack.at[pl.ds(9, 1)], cod.at[pl.ds(1 + high * (n - 3), 1)]))
    run_copies(pairs, sems)

    def body(i, carry):
        cond[i], nu[i] = materials(cod[i], cond_t, nu_t)
        return carry

    lax.fori_loop(1, n - 1, body, 0)

    def into(buf):
        def store(c, i, value):
            buf[c, i] = value
        return store

    fine_sweep(x, into(y), held, cond, nu, 1, 7, f)
    fine_sweep(x, into(y), held, cond, nu, 9, n - 1, f)
    fine_sweep(y, into(x), held, cond, nu, 2, 6)
    fine_sweep(y, into(x), held, cond, nu, 10, 14)
    run_copies(
        [
            (x.at[:, pl.ds(2 + (1 - odd) * 8, 4)], out_a),
            (x.at[:, pl.ds(2 + odd * 8, 4)], out_b),
        ],
        sems,
    )


def material_kernel(odd_ref, cond_t, nu_t, code, ra, rb, cond_o, nu_o, keep_o, spread_o, cod, cond, nu, keep, spread, sems):
    odd = odd_ref[0]
    run_copies(
        [
            (code, cod.at[pl.ds(7, LX)]),
            (ra.at[pl.ds(9, 7)], cod.at[pl.ds((1 - odd) * (LX + 7), 7)]),
            (rb.at[pl.ds(9, 7)], cod.at[pl.ds(odd * (LX + 7), 7)]),
        ],
        sems,
    )

    def body(i, carry):
        cv, nv = materials(cod[i], cond_t, nu_t)
        cond[i] = cv
        nu[i] = nv
        half = 0.5 * cv
        scale = 1.0 / (half + 6.0 * nv)
        keep[i] = half * scale
        spread[i] = nv * scale
        return carry

    lax.fori_loop(0, LX + 14, body, 0)
    run_copies(
        [
            (cond.at[pl.ds(4, LX + 6)], cond_o),
            (nu.at[pl.ds(4, LX + 6)], nu_o),
            (keep, keep_o),
            (spread, spread_o),
        ],
        sems,
    )


def extended_pairs(odd, pieces, halos, x):
    a, b, m = pieces
    ha, hb = halos
    return [
        (a, x.at[:, pl.ds(4 + (1 - odd) * 8, 4)]),
        (b, x.at[:, pl.ds(4 + odd * 8, 4)]),
        (m, x.at[:, pl.ds(8, 4)]),
        (ha, x.at[:, pl.ds((1 - odd) * 16, 4)]),
        (hb, x.at[:, pl.ds(odd * 16, 4)]),
    ]


def force_pairs(odd, source, which, width, packs, start, f):
    pairs = []
    for c in range(3):
        pairs.append((source.at[which, c], f.at[c, pl.ds(4, LX)]))
        for pack, high in ((packs[0], 1 - odd), (packs[1], odd)):
            pairs.append(
                (
                    pack.at[pl.ds(start + width * c, width)],
                    f.at[c, pl.ds(4 - width + high * (LX + width), width)],
                )
            )
    return pairs


def second_kernel(
    odd_ref, va, vb, vm, ha, hb, source, a1, b1, a2, b2, cond_i, nu_i,
    u0_o, oa, ob, om, x, y, held, f0, f1, cond, nu, sems,
):
    odd = odd_ref[0]
    pairs = extended_pairs(odd, (va, vb, vm), (ha, hb), x)
    pairs += force_pairs(odd, source, 0, 3, (a2, b2), 0, f0)
    pairs += force_pairs(odd, source, 1, 1, (a1, b1), 6, f1)
    pairs += [(cond_i, cond.at[pl.ds(1, LX + 6)]), (nu_i, nu.at[pl.ds(1, LX + 6)])]
    run_copies(pairs, sems)

    def into(buf):
        def store(c, i, value):
            buf[c, i] = value
        return store

    fine_sweep(x, into(y), held, cond, nu, 1, 19, f0)
    fine_sweep(y, into(x), held, cond, nu, 2, 18)
    kept = copy_all([(x.at[:, pl.ds(2, LX + 4)], u0_o)], sems, 30)
    fine_sweep(x, into(y), held, cond, nu, 3, 17, f1)
    wait_all(kept)
    fine_sweep(y, into(x), held, cond, nu, 4, 16)
    run_copies(
        [
            (x.at[:, pl.ds(4 + (1 - odd) * 8, 4)], oa),
            (x.at[:, pl.ds(4 + odd * 8, 4)], ob),
            (x.at[:, pl.ds(8, 4)], om),
        ],
        sems,
    )


def residual_kernel(
    odd_ref, va, vb, vm, ha, hb, source, a2, b2, cond_i, nu_i, keep_i, spread_i, u0_i,
    res_o, l0, l1, l2, x, y, held, f0, cond, nu, keep, spread, u0, sems,
):
    odd = odd_ref[0]
    pairs = extended_pairs(odd, (va, vb, vm), (ha, hb), x)
    pairs += force_pairs(odd, source, 0, 3, (a2, b2), 0, f0)
    pairs += [(cond_i, cond.at[pl.ds(1, LX + 6)]), (nu_i, nu.at[pl.ds(1, LX + 6)])]
    pairs += [(keep_i, keep), (spread_i, spread), (u0_i, u0.at[:, pl.ds(2, LX + 4)])]
    run_copies(pairs, sems)

    def into(buf):
        def store(c, i, value):
            buf[c, i] = value
        return store

    def less(c, i, value):
        x[c, i] = value - u0[c, i]

    def put(buf):
        def store(at, value):
            buf[at] = value
        return store

    comps = [(0,), (1,), (2,)]
    fine_sweep(x, into(y), held, cond, nu, 1, 19, f0)
    fine_sweep(y, less, held, cond, nu, 2, 18)
    kept = copy_all([(x.at[:, pl.ds(4, LX)], res_o.at[0])], sems, 30)
    coarse_sweep(x, put(y), held, keep, spread, 3, 3, 17, True, comps)
    wait_all(kept)
    coarse_sweep(y, put(x), held, keep, spread, 3, 4, 16, False, comps)
    run_copies([(x.at[c, pl.ds(4, LX)], o) for c, o in enumerate((l0, l1, l2))], sems)


def add_kernel(w, odd_ref, base, moved, total_o, sa, sb, x, y, sems):
    odd = odd_ref[0]
    run_copies([(base, x), (moved, y)], sems)

    def body(i, carry):
        x[i] = x[i] + y[i]
        return carry

    lax.fori_loop(0, LX, body, 0)
    run_copies(
        [
            (x, total_o),
            (x.at[pl.ds((1 - odd) * (LX - w), w)], sa),
            (x.at[pl.ds(odd * (LX - w), w)], sb),
        ],
        sems,
    )


def power_kernel(w, odd_ref, value, ha, hb, keep_i, spread_i, out, x, y, held, keep, spread, sems):
    odd = odd_ref[0]
    run_copies(
        [
            (value, x.at[pl.ds(w, LX)]),
            (ha, x.at[pl.ds((1 - odd) * (LX + w), w)]),
            (hb, x.at[pl.ds(odd * (LX + w), w)]),
            (keep_i, keep),
            (spread_i, spread),
        ],
        sems,
    )

    def put(buf):
        def store(at, value):
            buf[at] = value
        return store

    for step in range(w // 2):
        lo = 1 + 2 * step
        coarse_sweep(x, put(y), held, keep, spread, 7 - w, lo, LX + 2 * w - lo, True, [()])
        coarse_sweep(y, put(x), held, keep, spread, 7 - w, lo + 1, LX + 2 * w - lo - 1, False, [()])
    run_copies([(x.at[pl.ds(w, LX)], out)], sems)


def last_kernel(
    odd_ref, p0, p1, p2, a_0, a_1, a_2, b_0, b_1, b_2, source, a1, b1, cond_i, nu_i,
    field, x, y, held, f1, cond, nu, sems,
):
    odd = odd_ref[0]
    pairs = force_pairs(odd, source, 1, 1, (a1, b1), 6, f1)
    pairs += [(cond_i, cond.at[pl.ds(1, LX + 6)]), (nu_i, nu.at[pl.ds(1, LX + 6)])]
    for c, (p, a, b) in enumerate(((p0, a_0, b_0), (p1, a_1, b_1), (p2, a_2, b_2))):
        pairs.append((p, x.at[c, pl.ds(4, LX)]))
        pairs.append((a, x.at[c, pl.ds(2 + (1 - odd) * (LX + 2), 2)]))
        pairs.append((b, x.at[c, pl.ds(2 + odd * (LX + 2), 2)]))
    run_copies(pairs, sems)

    def into(buf):
        def store(c, i, value):
            buf[c, i] = value
        return store

    kept = copy_all([(x.at[:, pl.ds(4, LX)], field.at[0])], sems, 30)
    fine_sweep(x, into(y), held, cond, nu, 3, 17, f1)
    wait_all(kept)
    fine_sweep(y, into(x), held, cond, nu, 4, 16)
    run_copies([(x.at[:, pl.ds(4, LX)], field.at[1])], sems)


def body(guess, source, regions, conductance, reluct):
    slices = lax.axis_size("tm")
    slabs = lax.axis_size("space")
    odd = (lax.axis_index("space") % 2).astype(jnp.int32).reshape(1)
    on_chip = [(i, i ^ 1) for i in range(slabs)]
    off_chip = [(i, i + 1) for i in range(1, slabs - 1, 2)]
    off_chip += [(j, i) for i, j in off_chip]

    def from_a(x):
        return lax.ppermute(x, "space", on_chip)

    def from_b(x):
        return lax.ppermute(x, "space", off_chip)

    def later(x, distance):
        return lax.ppermute(x, "tm", [(i, (i + distance) % slices) for i in range(slices)])

    code, sa1, sb1, sa2, sb2 = call(
        pack_kernel, "pack", (odd, guess, source, regions),
        [planes(LX), planes(10), planes(10), planes(16), planes(16)],
        [pltpu.VMEM((LX, NY, NZ), jnp.int32), vmem(LX)], 32,
    )
    b1 = from_b(sb1)
    a1 = from_a(sa1)
    um = call(
        first_middle_kernel, "first_middle", (conductance, reluct, guess, source, code),
        planes(3, 4), [vmem(3, 8)] * 4 + [vmem(8)] * 3, 32,
    )
    vm = later(um, 1)
    b2 = from_b(sb2)
    a2 = from_a(sa2)
    ua, ub = call(
        first_kernel, "first", (odd, conductance, reluct, guess, source, code, a1, b1),
        [planes(3, 4), planes(3, 4)], [vmem(3, LX + 4)] * 4 + [vmem(LX + 4)] * 3, 32,
    )
    vb = later(ub, 1)
    va = later(ua, 1)
    cond, nu, keep, spread = call(
        material_kernel, "material", (odd, conductance, reluct, code, a2, b2),
        [planes(LX + 6), planes(LX + 6), planes(LX + 14), planes(LX + 14)],
        [vmem(LX + 14)] * 5, 32,
    )
    hb = from_b(vb)
    ha = from_a(va)
    n = LX + 8
    u0, ua, ub, um = call(
        second_kernel, "second",
        (odd, va, vb, vm, ha, hb, source, a1, b1, a2, b2, cond, nu),
        [planes(3, LX + 4), planes(3, 4), planes(3, 4), planes(3, 4)],
        [vmem(3, n)] * 5 + [vmem(n)] * 2, 32,
    )
    vb = later(ub, 1)
    va = later(ua, 1)
    vm = later(um, 1)
    hb = from_b(vb)
    ha = from_a(va)
    residual, *moving = call(
        residual_kernel, "residual",
        (odd, va, vb, vm, ha, hb, source, a2, b2, cond, nu, keep, spread, u0),
        [planes(1, 3, LX)] + [planes(LX)] * 3,
        [vmem(3, n)] * 4 + [vmem(n)] * 2 + [vmem(LX + 14)] * 2 + [vmem(3, n)], 32,
    )
    u0_own = [u0[c, 2:2 + LX] for c in range(3)]
    totals = [residual[0, c] for c in range(3)]
    for distance, width in ((1, 4), (2, 8), (4, 2)):
        moved = [later(m, distance) for m in moving]
        bases = u0_own if distance == 4 else totals
        if distance == 4:
            bases = [t + u for t, u in zip(totals, u0_own)]
        totals, moving, sides = [], [], []
        for c in range(3):
            total, sa, sb = call(
                functools.partial(add_kernel, width), "add%d" % width, (odd, bases[c], moved[c]),
                [planes(LX), planes(width), planes(width)], [vmem(LX)] * 2, 8,
            )
            hb = from_b(sb)
            ha = from_a(sa)
            totals.append(total)
            sides.append((ha, hb))
            if distance < 4:
                moving.append(
                    call(
                        functools.partial(power_kernel, width), "power%d" % width,
                        (odd, total, ha, hb, keep, spread), planes(LX),
                        [vmem(LX + 2 * width)] * 3 + [vmem(LX + 14)] * 2, 8,
                    )
                )
    field = call(
        last_kernel, "last",
        (odd, *totals, *[s[0] for s in sides], *[s[1] for s in sides], source, a1, b1, cond, nu),
        planes(2, 3, LX), [vmem(3, n)] * 4 + [vmem(n)] * 2, 32,
    )
    return field, residual


def solution(mesh):
    whole = P("tm", None, "space", None, None)
    return jax.shard_map(
        body, mesh=mesh, in_specs=(whole, whole, P("space", None, None), P(), P()),
        out_specs=(whole, whole), check_vma=False,
    )
```

```python
import functools

import jax
import jax.numpy as jnp
from jax import lax
from jax.experimental import pallas as pl
from jax.experimental.pallas import tpu as pltpu
from jax.sharding import PartitionSpec as P

LX, NY, NZ = 12, 64, 128
F32 = jnp.float32
ANY = pl.BlockSpec(memory_space=pl.ANY)
VMEM = pl.BlockSpec(memory_space=pltpu.VMEM)
SMEM = pl.BlockSpec(memory_space=pltpu.SMEM)


def planes(*lead):
    return jax.ShapeDtypeStruct(tuple(lead) + (NY, NZ), F32)


def vmem(*lead):
    return pltpu.VMEM(tuple(lead) + (NY, NZ), F32)


def copy_all(pairs, sems, base=0):
    copies = [
        pltpu.make_async_copy(src, dst, sems.at[base + n]) for n, (src, dst) in enumerate(pairs)
    ]
    for copy in copies:
        copy.start()
    return copies


def wait_all(copies):
    for copy in copies:
        copy.wait()


def run_copies(pairs, sems, base=0):
    wait_all(copy_all(pairs, sems, base))


def call(kernel, name, args, outs, scratch, n_sems, flops=0, place=ANY):
    in_specs = [SMEM if a.ndim == 1 else place for a in args]
    single = not isinstance(outs, (list, tuple))
    return pl.pallas_call(
        kernel,
        name=name,
        out_shape=outs,
        in_specs=in_specs,
        out_specs=place if single else [place] * len(outs),
        scratch_shapes=list(scratch) + [pltpu.SemaphoreType.DMA((n_sems,))] * (n_sems > 0),
        compiler_params=pltpu.CompilerParams(vmem_limit_bytes=40 * 1024 * 1024),
        cost_estimate=pl.CostEstimate(flops=flops, bytes_accessed=4 << 20, transcendentals=0),
    )(*args)


def over_layers(lo, hi, step, at_once):
    rounds = (hi - lo) // at_once

    def body(t, carry):
        for k in range(at_once):
            step(lo + t * at_once + k)
        return carry

    lax.fori_loop(0, rounds, body, 0)
    for i in range(lo + rounds * at_once, hi):
        step(i)


def neighbours(src, at):
    row = lax.broadcasted_iota(jnp.int32, (NY, NZ), 0)
    lane = lax.broadcasted_iota(jnp.int32, (NY, NZ), 1)
    zero = jnp.float32(0.0)
    def of(*lead_i):
        *lead, i = lead_i
        a = src[(*lead, i)]
        first = src[(*lead, i + 1)] + src[(*lead, i - 1)]
        up = jnp.where(row == 0, zero, pltpu.roll(a, 1, 0))
        down = jnp.where(row == NY - 1, zero, pltpu.roll(a, NY - 1, 0))
        left = jnp.where(lane == 0, zero, pltpu.roll(a, 1, 1))
        right = jnp.where(lane == NZ - 1, zero, pltpu.roll(a, NZ - 1, 1))
        return (first + (up + down)) + (left + right)
    return of(*at)


def fine_sweep(src, store, held, cond, nu, lo, hi, force=None):
    def step(i):
        square = src[0, i] * src[0, i] + src[1, i] * src[1, i] + src[2, i] * src[2, i]
        base = nu[i]
        weight = cond[i]
        grown = 1.0 + square
        strong = base * (1.0 + 1.5 * square)
        scale = 1.0 / (weight * grown + 6.0 * strong)
        keep = grown * scale
        spread = strong * scale
        for c in range(3):
            if force is not None:
                fixed = weight * src[c, i] + force[c, i]
                held[c, i] = fixed
            else:
                fixed = held[c, i]
            store(c, i, fixed * keep + neighbours(src, (c, i)) * spread)

    over_layers(lo, hi, step, 4)


def coarse_sweep(src, store, held, keep, spread, off, lo, hi, first, comps):
    def step(i):
        k = keep[i + off]
        s = spread[i + off]
        for lead in comps:
            at = lead + (i,)
            if first:
                fixed = k * src[at]
                held[at] = fixed
            else:
                fixed = held[at]
            store(at, fixed + s * neighbours(src, at))

    over_layers(lo, hi, step, 8 if len(comps) == 1 else 3)


def lookup(code, table):
    first = jnp.where(code == 1.0, table[0], table[1])
    second = jnp.where(code == 3.0, table[2], table[3])
    return jnp.where(code <= 2.0, first, second)


def materials(code, cond_t, nu_t):
    outside = code == 0.0
    return (
        jnp.where(outside, jnp.float32(1.0), lookup(code, cond_t)),
        jnp.where(outside, jnp.float32(0.0), lookup(code, nu_t)),
    )


def pack_kernel(odd_ref, guess, source, regions, code, a1, b1, a2, b2, reg, cod, sems):
    odd = odd_ref[0]
    run_copies([(regions, reg)], sems)

    def body(i, carry):
        cod[i] = (reg[i] + 1).astype(F32)
        return carry

    lax.fori_loop(0, LX, body, 0)
    pairs = [(cod, code)]
    for one, two, top in ((a1, a2, 1 - odd), (b1, b2, odd)):
        for c in range(3):
            pairs.append((guess.at[0, c, pl.ds(top * (LX - 2), 2)], one.at[pl.ds(2 * c, 2)]))
            pairs.append((source.at[1, c, pl.ds(top * (LX - 1), 1)], one.at[pl.ds(6 + c, 1)]))
            pairs.append((source.at[0, c, pl.ds(top * (LX - 3), 3)], two.at[pl.ds(3 * c, 3)]))
        pairs.append((cod.at[pl.ds(top * (LX - 1), 1)], one.at[pl.ds(9, 1)]))
        pairs.append((cod.at[pl.ds(top * (LX - 7), 7)], two.at[pl.ds(9, 7)]))
    run_copies(pairs, sems)


def first_middle_kernel(cond_t, nu_t, guess, source, code, out, x, y, held, f, cod, cond, nu, sems):
    pairs = [(code.at[pl.ds(2, 8)], cod)]
    pairs += [(guess.at[0, c, pl.ds(2, 8)], x.at[c]) for c in range(3)]
    pairs += [(source.at[1, c, pl.ds(2, 8)], f.at[c]) for c in range(3)]
    run_copies(pairs, sems)

    def body(i, carry):
        cond[i], nu[i] = materials(cod[i], cond_t, nu_t)
        return carry

    lax.fori_loop(1, 7, body, 0)

    def into(buf):
        def store(c, i, value):
            buf[c, i] = value
        return store

    fine_sweep(x, into(y), held, cond, nu, 1, 7, f)
    fine_sweep(y, into(x), held, cond, nu, 2, 6)
    run_copies([(x.at[:, pl.ds(2, 4)], out)], sems)


def first_kernel(odd_ref, cond_t, nu_t, guess, source, code, ra, rb, after, out_a, out_b, x, y, held, f, cod, cond, nu, sems):
    odd = odd_ref[0]
    n = LX + 4
    pairs = [(code, cod.at[pl.ds(2, LX)])]
    for c in range(3):
        pairs.append((guess.at[0, c], x.at[c, pl.ds(2, LX)]))
        pairs.append((source.at[1, c], f.at[c, pl.ds(2, LX)]))
    for pack, high in ((ra, 1 - odd), (rb, odd)):
        for c in range(3):
            pairs.append((pack.at[pl.ds(2 * c, 2)], x.at[c, pl.ds(high * (n - 2), 2)]))
            pairs.append((pack.at[pl.ds(6 + c, 1)], f.at[c, pl.ds(1 + high * (n - 3), 1)]))
        pairs.append((pack.at[pl.ds(9, 1)], cod.at[pl.ds(1 + high * (n - 3), 1)]))
    run_copies(pairs, sems)

    def body(i, carry):
        cond[i], nu[i] = materials(cod[i], cond_t, nu_t)
        return carry

    lax.fori_loop(1, n - 1, body, 0)

    def into(buf):
        def store(c, i, value):
            buf[c, i] = value
        return store

    fine_sweep(x, into(y), held, cond, nu, 1, 7, f)
    fine_sweep(x, into(y), held, cond, nu, 9, n - 1, f)
    fine_sweep(y, into(x), held, cond, nu, 2, 6)
    fine_sweep(y, into(x), held, cond, nu, 10, 14)
    run_copies(
        [
            (x.at[:, pl.ds(2 + (1 - odd) * 8, 4)], out_a),
            (x.at[:, pl.ds(2 + odd * 8, 4)], out_b),
        ],
        sems,
    )


def material_kernel(odd_ref, cond_t, nu_t, code, ra, rb, cond_o, nu_o, keep_o, spread_o, cod, cond, nu, keep, spread, sems):
    odd = odd_ref[0]
    run_copies(
        [
            (code, cod.at[pl.ds(7, LX)]),
            (ra.at[pl.ds(9, 7)], cod.at[pl.ds((1 - odd) * (LX + 7), 7)]),
            (rb.at[pl.ds(9, 7)], cod.at[pl.ds(odd * (LX + 7), 7)]),
        ],
        sems,
    )

    def body(i, carry):
        cv, nv = materials(cod[i], cond_t, nu_t)
        cond[i] = cv
        nu[i] = nv
        half = 0.5 * cv
        scale = 1.0 / (half + 6.0 * nv)
        keep[i] = half * scale
        spread[i] = nv * scale
        return carry

    lax.fori_loop(0, LX + 14, body, 0)
    run_copies(
        [
            (cond.at[pl.ds(4, LX + 6)], cond_o),
            (nu.at[pl.ds(4, LX + 6)], nu_o),
            (keep, keep_o),
            (spread, spread_o),
        ],
        sems,
    )


def extended_pairs(odd, pieces, halos, x):
    a, b, m = pieces
    ha, hb = halos
    return [
        (a, x.at[:, pl.ds(4 + (1 - odd) * 8, 4)]),
        (b, x.at[:, pl.ds(4 + odd * 8, 4)]),
        (m, x.at[:, pl.ds(8, 4)]),
        (ha, x.at[:, pl.ds((1 - odd) * 16, 4)]),
        (hb, x.at[:, pl.ds(odd * 16, 4)]),
    ]


def force_pairs(odd, source, which, width, packs, start, f):
    pairs = []
    for c in range(3):
        pairs.append((source.at[which, c], f.at[c, pl.ds(4, LX)]))
        for pack, high in ((packs[0], 1 - odd), (packs[1], odd)):
            pairs.append(
                (
                    pack.at[pl.ds(start + width * c, width)],
                    f.at[c, pl.ds(4 - width + high * (LX + width), width)],
                )
            )
    return pairs


def second_kernel(
    odd_ref, va, vb, vm, ha, hb, source, a1, b1, a2, b2, cond_i, nu_i,
    u0_o, oa, ob, om, x, y, held, f0, f1, cond, nu, sems,
):
    odd = odd_ref[0]
    pairs = extended_pairs(odd, (va, vb, vm), (ha, hb), x)
    pairs += force_pairs(odd, source, 0, 3, (a2, b2), 0, f0)
    pairs += force_pairs(odd, source, 1, 1, (a1, b1), 6, f1)
    pairs += [(cond_i, cond.at[pl.ds(1, LX + 6)]), (nu_i, nu.at[pl.ds(1, LX + 6)])]
    run_copies(pairs, sems)

    def into(buf):
        def store(c, i, value):
            buf[c, i] = value
        return store

    fine_sweep(x, into(y), held, cond, nu, 1, 19, f0)
    fine_sweep(y, into(x), held, cond, nu, 2, 18)
    kept = copy_all([(x.at[:, pl.ds(2, LX + 4)], u0_o)], sems, 30)
    fine_sweep(x, into(y), held, cond, nu, 3, 17, f1)
    wait_all(kept)
    fine_sweep(y, into(x), held, cond, nu, 4, 16)
    run_copies(
        [
            (x.at[:, pl.ds(4 + (1 - odd) * 8, 4)], oa),
            (x.at[:, pl.ds(4 + odd * 8, 4)], ob),
            (x.at[:, pl.ds(8, 4)], om),
        ],
        sems,
    )


def residual_kernel(
    odd_ref, va, vb, vm, ha, hb, source, a2, b2, cond_i, nu_i, keep_i, spread_i, u0_i,
    res_o, l0, l1, l2, x, y, held, f0, cond, nu, keep, spread, u0, sems,
):
    odd = odd_ref[0]
    pairs = extended_pairs(odd, (va, vb, vm), (ha, hb), x)
    pairs += force_pairs(odd, source, 0, 3, (a2, b2), 0, f0)
    pairs += [(cond_i, cond.at[pl.ds(1, LX + 6)]), (nu_i, nu.at[pl.ds(1, LX + 6)])]
    pairs += [(keep_i, keep), (spread_i, spread), (u0_i, u0.at[:, pl.ds(2, LX + 4)])]
    run_copies(pairs, sems)

    def into(buf):
        def store(c, i, value):
            buf[c, i] = value
        return store

    def less(c, i, value):
        x[c, i] = value - u0[c, i]

    def put(buf):
        def store(at, value):
            buf[at] = value
        return store

    comps = [(0,), (1,), (2,)]
    fine_sweep(x, into(y), held, cond, nu, 1, 19, f0)
    fine_sweep(y, less, held, cond, nu, 2, 18)
    kept = copy_all([(x.at[:, pl.ds(4, LX)], res_o.at[0])], sems, 30)
    coarse_sweep(x, put(y), held, keep, spread, 3, 3, 17, True, comps)
    wait_all(kept)
    coarse_sweep(y, put(x), held, keep, spread, 3, 4, 16, False, comps)
    run_copies([(x.at[c, pl.ds(4, LX)], o) for c, o in enumerate((l0, l1, l2))], sems)


def add_kernel(w, odd_ref, base, moved, total_o, sa, sb):
    odd = odd_ref[0]
    for i in range(LX):
        total_o[i] = base[i] + moved[i]
    for side, top in ((sa, 1 - odd), (sb, odd)):
        for i in range(w):
            side[i] = total_o[i + top * (LX - w)]


def power_kernel(w, odd_ref, value, ha, hb, keep, spread, out, x, y, held):
    odd = odd_ref[0]
    for i in range(LX):
        x[i + w] = value[i]
    for side, high in ((ha, 1 - odd), (hb, odd)):
        for i in range(w):
            x[i + high * (LX + w)] = side[i]

    def put(buf, shift=0):
        def store(at, value):
            buf[at[0] - shift] = value
        return store

    for step in range(w // 2):
        lo = 1 + 2 * step
        last = put(out, w) if step == w // 2 - 1 else put(x)
        coarse_sweep(x, put(y), held, keep, spread, 7 - w, lo, LX + 2 * w - lo, True, [()])
        coarse_sweep(y, last, held, keep, spread, 7 - w, lo + 1, LX + 2 * w - lo - 1, False, [()])


def last_kernel(
    odd_ref, p0, p1, p2, a_0, a_1, a_2, b_0, b_1, b_2, source, a1, b1, cond_i, nu_i,
    field, x, y, held, f1, cond, nu, sems,
):
    odd = odd_ref[0]
    pairs = force_pairs(odd, source, 1, 1, (a1, b1), 6, f1)
    pairs += [(cond_i, cond.at[pl.ds(1, LX + 6)]), (nu_i, nu.at[pl.ds(1, LX + 6)])]
    for c, (p, a, b) in enumerate(((p0, a_0, b_0), (p1, a_1, b_1), (p2, a_2, b_2))):
        pairs.append((p, x.at[c, pl.ds(4, LX)]))
        pairs.append((a, x.at[c, pl.ds(2 + (1 - odd) * (LX + 2), 2)]))
        pairs.append((b, x.at[c, pl.ds(2 + odd * (LX + 2), 2)]))
    run_copies(pairs, sems)

    def into(buf):
        def store(c, i, value):
            buf[c, i] = value
        return store

    kept = copy_all([(x.at[:, pl.ds(4, LX)], field.at[0])], sems, 30)
    fine_sweep(x, into(y), held, cond, nu, 3, 17, f1)
    wait_all(kept)
    fine_sweep(y, into(x), held, cond, nu, 4, 16)
    run_copies([(x.at[:, pl.ds(4, LX)], field.at[1])], sems)


def body(guess, source, regions, conductance, reluct):
    slices = lax.axis_size("tm")
    slabs = lax.axis_size("space")
    odd = (lax.axis_index("space") % 2).astype(jnp.int32).reshape(1)
    on_chip = [(i, i ^ 1) for i in range(slabs)]
    off_chip = [(i, i + 1) for i in range(1, slabs - 1, 2)]
    off_chip += [(j, i) for i, j in off_chip]

    def from_a(x):
        return lax.ppermute(x, "space", on_chip)

    def from_b(x):
        return lax.ppermute(x, "space", off_chip)

    def later(x, distance):
        return lax.ppermute(x, "tm", [(i, (i + distance) % slices) for i in range(slices)])

    code, sa1, sb1, sa2, sb2 = call(
        pack_kernel, "pack", (odd, guess, source, regions),
        [planes(LX), planes(10), planes(10), planes(16), planes(16)],
        [pltpu.VMEM((LX, NY, NZ), jnp.int32), vmem(LX)], 32,
    )
    b1 = from_b(sb1)
    a1 = from_a(sa1)
    um = call(
        first_middle_kernel, "first_middle", (conductance, reluct, guess, source, code),
        planes(3, 4), [vmem(3, 8)] * 4 + [vmem(8)] * 3, 32,
    )
    vm = later(um, 1)
    b2 = from_b(sb2)
    a2 = from_a(sa2)
    ua, ub = call(
        first_kernel, "first", (odd, conductance, reluct, guess, source, code, a1, b1, um),
        [planes(3, 4), planes(3, 4)], [vmem(3, LX + 4)] * 4 + [vmem(LX + 4)] * 3, 32,
    )
    vb = later(ub, 1)
    va = later(ua, 1)
    cond, nu, keep, spread = call(
        material_kernel, "material", (odd, conductance, reluct, code, a2, b2),
        [planes(LX + 6), planes(LX + 6), planes(LX + 14), planes(LX + 14)],
        [vmem(LX + 14)] * 5, 32,
    )
    hb = from_b(vb)
    ha = from_a(va)
    n = LX + 8
    u0, ua, ub, um = call(
        second_kernel, "second",
        (odd, va, vb, vm, ha, hb, source, a1, b1, a2, b2, cond, nu),
        [planes(3, LX + 4), planes(3, 4), planes(3, 4), planes(3, 4)],
        [vmem(3, n)] * 5 + [vmem(n)] * 2, 32,
    )
    vb = later(ub, 1)
    va = later(ua, 1)
    vm = later(um, 1)
    hb = from_b(vb)
    ha = from_a(va)
    residual, *moving = call(
        residual_kernel, "residual",
        (odd, va, vb, vm, ha, hb, source, a2, b2, cond, nu, keep, spread, u0),
        [planes(1, 3, LX)] + [planes(LX)] * 3,
        [vmem(3, n)] * 4 + [vmem(n)] * 2 + [vmem(LX + 14)] * 2 + [vmem(3, n)], 32,
    )
    u0_own = [u0[c, 2:2 + LX] for c in range(3)]
    totals = [residual[0, c] for c in range(3)]
    for distance, width in ((1, 4), (2, 8), (4, 2)):
        moved = [later(m, distance) for m in moving]
        bases = u0_own if distance == 4 else totals
        if distance == 4:
            bases = [t + u for t, u in zip(totals, u0_own)]
        totals, moving, sides = [], [], []
        for c in range(3):
            total, sa, sb = call(
                functools.partial(add_kernel, width), "add%d" % width, (odd, bases[c], moved[c]),
                [planes(LX), planes(width), planes(width)], [], 0, place=VMEM,
            )
            hb = from_b(sb)
            ha = from_a(sa)
            totals.append(total)
            sides.append((ha, hb))
            if distance < 4:
                moving.append(
                    call(
                        functools.partial(power_kernel, width), "power%d" % width,
                        (odd, total, ha, hb, keep, spread), planes(LX),
                        [vmem(LX + 2 * width)] * 3, 0, place=VMEM,
                    )
                )
    field = call(
        last_kernel, "last",
        (odd, *totals, *[s[0] for s in sides], *[s[1] for s in sides], source, a1, b1, cond, nu),
        planes(2, 3, LX), [vmem(3, n)] * 4 + [vmem(n)] * 2, 32,
    )
    return field, residual


def solution(mesh):
    whole = P("tm", None, "space", None, None)
    return jax.shard_map(
        body, mesh=mesh, in_specs=(whole, whole, P("space", None, None), P(), P()),
        out_specs=(whole, whole), check_vma=False,
    )
```

```python
import functools

import jax
import jax.numpy as jnp
from jax import lax
from jax.experimental import pallas as pl
from jax.experimental.pallas import tpu as pltpu
from jax.sharding import PartitionSpec as P

LX, NY, NZ = 12, 64, 128
F32 = jnp.float32
ANY = pl.BlockSpec(memory_space=pl.ANY)
HBM = pl.BlockSpec(memory_space=pltpu.HBM)
VMEM = pl.BlockSpec(memory_space=pltpu.VMEM)
SMEM = pl.BlockSpec(memory_space=pltpu.SMEM)


def planes(*lead):
    return jax.ShapeDtypeStruct(tuple(lead) + (NY, NZ), F32)


def vmem(*lead):
    return pltpu.VMEM(tuple(lead) + (NY, NZ), F32)


def copy_all(pairs, sems, base=0):
    copies = [
        pltpu.make_async_copy(src, dst, sems.at[base + n]) for n, (src, dst) in enumerate(pairs)
    ]
    for copy in copies:
        copy.start()
    return copies


def wait_all(copies):
    for copy in copies:
        copy.wait()


def run_copies(pairs, sems, base=0):
    wait_all(copy_all(pairs, sems, base))


def call(kernel, name, args, outs, scratch, n_sems=0, out_specs=None, in_place=VMEM):
    in_specs = [SMEM if a.ndim == 1 else in_place for a in args]
    single = not isinstance(outs, (list, tuple))
    return pl.pallas_call(
        kernel,
        name=name,
        out_shape=outs,
        in_specs=in_specs,
        out_specs=out_specs or (VMEM if single else [VMEM] * len(outs)),
        scratch_shapes=list(scratch) + [pltpu.SemaphoreType.DMA((n_sems,))] * (n_sems > 0),
        compiler_params=pltpu.CompilerParams(vmem_limit_bytes=40 * 1024 * 1024),
        cost_estimate=pl.CostEstimate(flops=0, bytes_accessed=4 << 20, transcendentals=0),
    )(*args)


def over_layers(lo, hi, step, at_once):
    rounds = (hi - lo) // at_once

    def body(t, carry):
        for k in range(at_once):
            step(lo + t * at_once + k)
        return carry

    lax.fori_loop(0, rounds, body, 0)
    for i in range(lo + rounds * at_once, hi):
        step(i)


def neighbours(src, at):
    row = lax.broadcasted_iota(jnp.int32, (NY, NZ), 0)
    lane = lax.broadcasted_iota(jnp.int32, (NY, NZ), 1)
    zero = jnp.float32(0.0)
    def of(*lead_i):
        *lead, i = lead_i
        a = src[(*lead, i)]
        first = src[(*lead, i + 1)] + src[(*lead, i - 1)]
        up = jnp.where(row == 0, zero, pltpu.roll(a, 1, 0))
        down = jnp.where(row == NY - 1, zero, pltpu.roll(a, NY - 1, 0))
        left = jnp.where(lane == 0, zero, pltpu.roll(a, 1, 1))
        right = jnp.where(lane == NZ - 1, zero, pltpu.roll(a, NZ - 1, 1))
        return (first + (up + down)) + (left + right)
    return of(*at)


def fine_sweep(src, store, held, cond, nu, lo, hi, force=None, off=0):
    def step(i):
        square = src[0, i] * src[0, i] + src[1, i] * src[1, i] + src[2, i] * src[2, i]
        base = nu[i - off]
        weight = cond[i - off]
        grown = 1.0 + square
        strong = base * (1.0 + 1.5 * square)
        scale = 1.0 / (weight * grown + 6.0 * strong)
        keep = grown * scale
        spread = strong * scale
        for c in range(3):
            if force is not None:
                fixed = weight * src[c, i] + force[c, i]
                held[c, i] = fixed
            else:
                fixed = held[c, i]
            store(c, i, fixed * keep + neighbours(src, (c, i)) * spread)

    over_layers(lo, hi, step, 4)


def coarse_sweep(src, store, held, keep, spread, off, lo, hi, first, comps):
    def step(i):
        k = keep[i + off]
        s = spread[i + off]
        for lead in comps:
            at = lead + (i,)
            if first:
                fixed = k * src[at]
                held[at] = fixed
            else:
                fixed = held[at]
            store(at, fixed + s * neighbours(src, at))

    over_layers(lo, hi, step, 8 if len(comps) == 1 else 3)


def lookup(code, table):
    first = jnp.where(code == 1, table[0], table[1])
    second = jnp.where(code == 3, table[2], table[3])
    return jnp.where(code <= 2, first, second)


def materials(code, cond_t, nu_t):
    outside = code == 0
    return (
        jnp.where(outside, jnp.float32(1.0), lookup(code, cond_t)),
        jnp.where(outside, jnp.float32(0.0), lookup(code, nu_t)),
    )


def into(buf):
    def store(c, i, value):
        buf[c, i] = value
    return store


def put(buf, shift=0):
    def store(at, value):
        buf[at[:-1] + (at[-1] - shift,)] = value
    return store


def edges(odd, n, width):
    return (1 - odd) * (n - width), odd * (n - width)


def first_pack_kernel(odd_ref, guess, source, regions, a1, b1, reg, sems):
    odd = odd_ref[0]
    pairs = [(regions.at[pl.ds(0, 1)], reg.at[pl.ds(0, 1)]), (regions.at[pl.ds(LX - 1, 1)], reg.at[pl.ds(1, 1)])]
    for one, two_from, one_from in zip((a1, b1), edges(odd, LX, 2), edges(odd, LX, 1)):
        for c in range(3):
            pairs.append((guess.at[0, c, pl.ds(two_from, 2)], one.at[pl.ds(2 * c, 2)]))
            pairs.append((source.at[1, c, pl.ds(one_from, 1)], one.at[pl.ds(6 + c, 1)]))
    run_copies(pairs, sems)
    a1[9] = (reg[1 - odd] + 1).astype(F32)
    b1[9] = (reg[odd] + 1).astype(F32)


def second_pack_kernel(odd_ref, source, regions, a2, b2, a3, b3, reg, sems):
    odd = odd_ref[0]
    pairs = [(regions, reg)]
    for two, start in zip((a2, b2), edges(odd, LX, 3)):
        for c in range(3):
            pairs.append((source.at[0, c, pl.ds(start, 3)], two.at[pl.ds(3 * c, 3)]))
    run_copies(pairs, sems)
    for two, start in zip((a2, b2), edges(odd, LX, 3)):
        for k in range(3):
            two[9 + k] = (reg[start + k] + 1).astype(F32)
    for three, high in ((a3, 1 - odd), (b3, odd)):
        for k in range(4):
            three[k] = (reg[high * (LX - 7) + (1 - high) * 3 + k] + 1).astype(F32)


def first_middle_kernel(cond_t, nu_t, guess, source, regions, out, y, held, cond, nu):
    def prepare(i):
        cond[i], nu[i] = materials(regions[i] + 1, cond_t, nu_t)

    over_layers(3, 9, prepare, 6)
    fine_sweep(guess.at[0], into(y), held, cond, nu, 3, 9, source.at[1])

    def store(c, i, value):
        out[c, i - 4] = value

    fine_sweep(y, store, held, cond, nu, 4, 8)


def first_kernel(odd_ref, cond_t, nu_t, guess, source, regions, ra, rb, after, out_a, out_b, x, y, held, f, cond, nu):
    odd = odd_ref[0]
    n = LX + 4
    for c in range(3):
        for i in (0, 1, 2, 3, 4, 5, 6, 7, 8, 9, 10, 11):
            x[c, i + 2] = guess[0, c, i]
            f[c, i + 2] = source[1, c, i]
    for i in range(LX):
        cond[i + 2], nu[i + 2] = materials(regions[i] + 1, cond_t, nu_t)
    for pack, high in ((ra, 1 - odd), (rb, odd)):
        for c in range(3):
            for k in range(2):
                x[c, high * (n - 2) + k] = pack[2 * c + k]
            f[c, 1 + high * (n - 3)] = pack[6 + c]
        cond[1 + high * (n - 3)], nu[1 + high * (n - 3)] = materials(pack[9], cond_t, nu_t)
    fine_sweep(x, into(y), held, cond, nu, 1, 7, f)
    fine_sweep(x, into(y), held, cond, nu, 9, n - 1, f)
    fine_sweep(y, into(x), held, cond, nu, 2, 6)
    fine_sweep(y, into(x), held, cond, nu, 10, 14)
    for c in range(3):
        for k in range(4):
            out_a[c, k] = x[c, 2 + (1 - odd) * 8 + k]
            out_b[c, k] = x[c, 2 + odd * 8 + k]


def material_kernel(odd_ref, cond_t, nu_t, regions, ra, rb, cond, nu, keep, spread):
    odd = odd_ref[0]

    def fill(at, code):
        cv, nv = materials(code, cond_t, nu_t)
        cond[at] = cv
        nu[at] = nv
        half = 0.5 * cv
        scale = 1.0 / (half + 6.0 * nv)
        keep[at] = half * scale
        spread[at] = nv * scale

    for i in range(LX):
        fill(3 + i, regions[i] + 1)
    for pack, high in ((ra, 1 - odd), (rb, odd)):
        for k in range(3):
            fill(high * (LX + 3) + k, pack[9 + k])


def wide_kernel(odd_ref, cond_t, nu_t, keep_i, spread_i, ra, rb, keep, spread):
    odd = odd_ref[0]
    for i in range(LX + 6):
        keep[i + 4] = keep_i[i]
        spread[i + 4] = spread_i[i]
    for pack, high in ((ra, 1 - odd), (rb, odd)):
        for k in range(4):
            at = high * (LX + 10) + k
            cv, nv = materials(pack[k], cond_t, nu_t)
            half = 0.5 * cv
            scale = 1.0 / (half + 6.0 * nv)
            keep[at] = half * scale
            spread[at] = nv * scale


def extend(odd, pieces, halos, x):
    a, b, m = pieces
    ha, hb = halos
    for c in range(3):
        for k in range(4):
            x[c, 8 + k] = m[c, k]
            x[c, 4 + (1 - odd) * 8 + k] = a[c, k]
            x[c, 4 + odd * 8 + k] = b[c, k]
            x[c, (1 - odd) * 16 + k] = ha[c, k]
            x[c, odd * 16 + k] = hb[c, k]


def extend_force(odd, source, which, width, packs, start, f):
    for c in range(3):
        for i in range(LX):
            f[c, 4 + i] = source[which, c, i]
        for pack, high in ((packs[0], 1 - odd), (packs[1], odd)):
            for k in range(width):
                f[c, 4 - width + high * (LX + width) + k] = pack[start + width * c + k]


def second_kernel(
    odd_ref, hb, vb, ha, va, vm, source, a1, b1, a2, b2, cond, nu,
    u0, oa, ob, om, x, y, held, f0, f1,
):
    odd = odd_ref[0]
    extend(odd, (va, vb, vm), (ha, hb), x)
    extend_force(odd, source, 0, 3, (a2, b2), 0, f0)
    extend_force(odd, source, 1, 1, (a1, b1), 6, f1)

    def keep_u0(c, i, value):
        x[c, i] = value
        u0[c, i - 2] = value

    fine_sweep(x, into(y), held, cond, nu, 1, 19, f0, 1)
    fine_sweep(y, keep_u0, held, cond, nu, 2, 18, None, 1)
    fine_sweep(x, into(y), held, cond, nu, 3, 17, f1, 1)
    fine_sweep(y, into(x), held, cond, nu, 4, 16, None, 1)
    for c in range(3):
        for k in range(4):
            om[c, k] = x[c, 8 + k]
            oa[c, k] = x[c, 4 + (1 - odd) * 8 + k]
            ob[c, k] = x[c, 4 + odd * 8 + k]


def residual_kernel(
    odd_ref, hb, vb, ha, va, vm, source, a2, b2, cond, nu, keep, spread, u0,
    res_o, l0, l1, l2, r0, r1, r2, x, y, held, f0, sems,
):
    odd = odd_ref[0]
    extend(odd, (va, vb, vm), (ha, hb), x)
    extend_force(odd, source, 0, 3, (a2, b2), 0, f0)

    def less(c, i, value):
        x[c, i] = value - u0[c, i - 2]

    fine_sweep(x, into(y), held, cond, nu, 1, 19, f0, 1)
    fine_sweep(y, less, held, cond, nu, 2, 18, None, 1)
    kept = copy_all([(x.at[:, pl.ds(4, LX)], res_o.at[0])], sems)
    comps = [(0,), (1,), (2,)]
    coarse_sweep(x, put(y), held, keep, spread, -1, 3, 17, True, comps)
    for c, out in enumerate((r0, r1, r2)):
        for i in range(LX):
            out[i] = x[c, 4 + i]

    def store(at, value):
        (l0, l1, l2)[at[0]][at[1] - 4] = value

    coarse_sweep(y, store, held, keep, spread, -1, 4, 16, False, comps)
    wait_all(kept)


def add_kernel(w, odd_ref, *refs):
    odd = odd_ref[0]
    *terms, total, sa, sb = refs
    for i in range(LX):
        value = terms[0][i]
        for term in terms[1:]:
            value = value + term[i]
        total[i] = value
    for side, top in ((sa, 1 - odd), (sb, odd)):
        for i in range(w):
            side[i] = total[i + top * (LX - w)]


def power_kernel(w, odd_ref, value, ha, hb, keep, spread, out, x, y, held):
    odd = odd_ref[0]
    for i in range(LX):
        x[i + w] = value[i]
    for side, high in ((ha, 1 - odd), (hb, odd)):
        for i in range(w):
            x[i + high * (LX + w)] = side[i]

    for step in range(w // 2):
        lo = 1 + 2 * step
        last = put(out, w) if step == w // 2 - 1 else put(x)
        coarse_sweep(x, put(y), held, keep, spread, -1, lo, LX + 2 * w - lo, True, [()])
        coarse_sweep(y, last, held, keep, spread, -1, lo + 1, LX + 2 * w - lo - 1, False, [()])


def last_kernel(
    odd_ref, p0, p1, p2, a_0, a_1, a_2, b_0, b_1, b_2, source, a1, b1, cond, nu,
    field, x, y, held, f1, sems,
):
    odd = odd_ref[0]
    kept = copy_all([(p, field.at[0, c]) for c, p in enumerate((p0, p1, p2))], sems)
    extend_force(odd, source, 1, 1, (a1, b1), 6, f1)
    for c, (p, a, b) in enumerate(((p0, a_0, b_0), (p1, a_1, b_1), (p2, a_2, b_2))):
        for i in range(LX):
            x[c, 4 + i] = p[i]
        for k in range(2):
            x[c, 2 + (1 - odd) * (LX + 2) + k] = a[k]
            x[c, 2 + odd * (LX + 2) + k] = b[k]
    fine_sweep(x, into(y), held, cond, nu, 3, 17, f1, 1)
    fine_sweep(y, into(x), held, cond, nu, 4, 10, None, 1)
    kept += copy_all([(x.at[:, pl.ds(4, 6)], field.at[1, :, pl.ds(0, 6)])], sems, 3)
    fine_sweep(y, into(x), held, cond, nu, 10, 16, None, 1)
    kept += copy_all([(x.at[:, pl.ds(10, 6)], field.at[1, :, pl.ds(6, 6)])], sems, 4)
    wait_all(kept)


def body(guess, source, regions, conductance, reluct):
    slices = lax.axis_size("tm")
    slabs = lax.axis_size("space")
    odd = (lax.axis_index("space") % 2).astype(jnp.int32).reshape(1)
    on_chip = [(i, i ^ 1) for i in range(slabs)]
    off_chip = [(i, i + 1) for i in range(1, slabs - 1, 2)]
    off_chip += [(j, i) for i, j in off_chip]
    fence = lax.optimization_barrier

    def from_a(x):
        return lax.ppermute(x, "space", on_chip)

    def from_b(x):
        return lax.ppermute(x, "space", off_chip)

    def later(x, distance):
        return lax.ppermute(x, "tm", [(i, (i + distance) % slices) for i in range(slices)])

    tables = (conductance, reluct)
    sa1, sb1 = call(
        first_pack_kernel, "first_pack", (odd, guess, source, regions),
        [planes(10), planes(10)], [pltpu.VMEM((2, NY, NZ), jnp.int32)], 16, in_place=HBM,
    )
    b1 = from_b(sb1)
    a1 = from_a(sa1)
    um = call(
        first_middle_kernel, "first_middle", (*tables, guess, source, regions),
        planes(3, 4), [vmem(3, LX)] * 2 + [vmem(LX)] * 2,
    )
    sa2, sb2, sa3, sb3 = call(
        second_pack_kernel, "second_pack", (odd, source, regions),
        [planes(12), planes(12), planes(4), planes(4)], [pltpu.VMEM((LX, NY, NZ), jnp.int32)], 8, in_place=HBM,
    )
    vm = later(um, 1)
    sb2, sa2, b1 = fence((sb2, sa2, b1))
    b2 = from_b(sb2)
    a2 = from_a(sa2)
    ua, ub = call(
        first_kernel, "first", (odd, *tables, guess, source, regions, a1, b1, um),
        [planes(3, 4), planes(3, 4)], [vmem(3, LX + 4)] * 4 + [vmem(LX + 4)] * 2,
    )
    vb = later(ub, 1)
    va = later(ua, 1)
    cond, nu, keep, spread = call(
        material_kernel, "material", (odd, *tables, regions, a2, b2), [planes(LX + 6)] * 4, [],
    )
    vb, vm, cond = fence((vb, vm, cond))
    hb = from_b(vb)
    ha = from_a(va)
    sb3, sa3, vb = fence((sb3, sa3, vb))
    b3 = from_b(sb3)
    a3 = from_a(sa3)
    n = LX + 8
    u0, ua, ub, um = call(
        second_kernel, "second",
        (odd, hb, vb, ha, va, vm, source, a1, b1, a2, b2, cond, nu),
        [planes(3, LX + 4), planes(3, 4), planes(3, 4), planes(3, 4)], [vmem(3, n)] * 5,
    )
    vb = later(ub, 1)
    va = later(ua, 1)
    vm = later(um, 1)
    hb = from_b(vb)
    ha = from_a(va)
    wide_keep, wide_spread = call(
        wide_kernel, "wide", (odd, *tables, keep, spread, a3, b3), [planes(LX + 14)] * 2, [],
    )
    residual, *rest = call(
        residual_kernel, "residual",
        (odd, hb, vb, ha, va, vm, source, a2, b2, cond, nu, keep, spread, u0),
        [planes(1, 3, LX)] + [planes(LX)] * 6, [vmem(3, n)] * 4, 1, [ANY] + [VMEM] * 6,
    )
    moving, totals = rest[:3], rest[3:]
    u0_own = [u0[c, 2:2 + LX] for c in range(3)]
    for distance, width in ((1, 4), (2, 8), (4, 2)):
        moved = [later(m, distance) for m in moving]
        bases = [(t,) for t in totals]
        if distance == 4:
            bases = [(t, u) for t, u in zip(totals, u0_own)]
        totals, moving, sides = [], [], []
        for c in range(3):
            total, sa, sb = call(
                functools.partial(add_kernel, width), "add%d" % width, (odd, *bases[c], moved[c]),
                [planes(LX), planes(width), planes(width)], [],
            )
            hb = from_b(sb)
            ha = from_a(sa)
            totals.append(total)
            sides.append((ha, hb))
            if distance < 4:
                pair = (wide_keep, wide_spread) if width == 8 else (keep, spread)
                moving.append(
                    call(
                        functools.partial(power_kernel, width), "power%d" % width,
                        (odd, total, ha, hb, *pair), planes(LX), [vmem(LX + 2 * width)] * 3,
                    )
                )
    field = call(
        last_kernel, "last",
        (odd, *totals, *[s[0] for s in sides], *[s[1] for s in sides], source, a1, b1, cond, nu),
        planes(2, 3, LX), [vmem(3, n)] * 4, 5, ANY,
    )
    return field, residual


def solution(mesh):
    whole = P("tm", None, "space", None, None)
    return jax.shard_map(
        body, mesh=mesh, in_specs=(whole, whole, P("space", None, None), P(), P()),
        out_specs=(whole, whole), check_vma=False,
    )
```

```python
import functools

import jax
import jax.numpy as jnp
from jax import lax
from jax.experimental import pallas as pl
from jax.experimental.pallas import tpu as pltpu
from jax.sharding import PartitionSpec as P

LX, NY, NZ = 12, 64, 128
F32 = jnp.float32
ANY = pl.BlockSpec(memory_space=pl.ANY)
HBM = pl.BlockSpec(memory_space=pltpu.HBM)
VMEM = pl.BlockSpec(memory_space=pltpu.VMEM)
SMEM = pl.BlockSpec(memory_space=pltpu.SMEM)


def planes(*lead):
    return jax.ShapeDtypeStruct(tuple(lead) + (NY, NZ), F32)


def vmem(*lead):
    return pltpu.VMEM(tuple(lead) + (NY, NZ), F32)


def copy_all(pairs, sems, base=0):
    copies = [
        pltpu.make_async_copy(src, dst, sems.at[base + n]) for n, (src, dst) in enumerate(pairs)
    ]
    for copy in copies:
        copy.start()
    return copies


def wait_all(copies):
    for copy in copies:
        copy.wait()


def run_copies(pairs, sems, base=0):
    wait_all(copy_all(pairs, sems, base))


def call(kernel, name, args, outs, scratch, n_sems=0, out_specs=None, in_place=VMEM):
    in_specs = [SMEM if a.ndim == 1 else in_place for a in args]
    single = not isinstance(outs, (list, tuple))
    return pl.pallas_call(
        kernel,
        name=name,
        out_shape=outs,
        in_specs=in_specs,
        out_specs=out_specs or (VMEM if single else [VMEM] * len(outs)),
        scratch_shapes=list(scratch) + [pltpu.SemaphoreType.DMA((n_sems,))] * (n_sems > 0),
        compiler_params=pltpu.CompilerParams(vmem_limit_bytes=40 * 1024 * 1024),
        cost_estimate=pl.CostEstimate(flops=0, bytes_accessed=4 << 20, transcendentals=0),
    )(*args)


def over_layers(lo, hi, step, at_once):
    rounds = (hi - lo) // at_once

    def body(t, carry):
        for k in range(at_once):
            step(lo + t * at_once + k)
        return carry

    lax.fori_loop(0, rounds, body, 0)
    for i in range(lo + rounds * at_once, hi):
        step(i)


def neighbours(src, at):
    row = lax.broadcasted_iota(jnp.int32, (NY, NZ), 0)
    lane = lax.broadcasted_iota(jnp.int32, (NY, NZ), 1)
    zero = jnp.float32(0.0)
    def of(*lead_i):
        *lead, i = lead_i
        a = src[(*lead, i)]
        first = src[(*lead, i + 1)] + src[(*lead, i - 1)]
        up = jnp.where(row == 0, zero, pltpu.roll(a, 1, 0))
        down = jnp.where(row == NY - 1, zero, pltpu.roll(a, NY - 1, 0))
        left = jnp.where(lane == 0, zero, pltpu.roll(a, 1, 1))
        right = jnp.where(lane == NZ - 1, zero, pltpu.roll(a, NZ - 1, 1))
        return (first + (up + down)) + (left + right)
    return of(*at)


def fine_sweep(src, store, held, cond, nu, lo, hi, force=None, off=0):
    def step(i):
        square = src[0, i] * src[0, i] + src[1, i] * src[1, i] + src[2, i] * src[2, i]
        base = nu[i - off]
        weight = cond[i - off]
        grown = 1.0 + square
        strong = base * (1.0 + 1.5 * square)
        scale = 1.0 / (weight * grown + 6.0 * strong)
        keep = grown * scale
        spread = strong * scale
        for c in range(3):
            if force is not None:
                fixed = weight * src[c, i] + force[c, i]
                held[c, i] = fixed
            else:
                fixed = held[c, i]
            store(c, i, fixed * keep + neighbours(src, (c, i)) * spread)

    over_layers(lo, hi, step, 4)


def coarse_sweep(src, store, held, keep, spread, off, lo, hi, first, comps):
    def step(i):
        k = keep[i + off]
        s = spread[i + off]
        for lead in comps:
            at = lead + (i,)
            if first:
                fixed = k * src[at]
                held[at] = fixed
            else:
                fixed = held[at]
            store(at, fixed + s * neighbours(src, at))

    over_layers(lo, hi, step, 8 if len(comps) == 1 else 3)


def lookup(code, table):
    first = jnp.where(code == 1, table[0], table[1])
    second = jnp.where(code == 3, table[2], table[3])
    return jnp.where(code <= 2, first, second)


def materials(code, cond_t, nu_t):
    outside = code == 0
    return (
        jnp.where(outside, jnp.float32(1.0), lookup(code, cond_t)),
        jnp.where(outside, jnp.float32(0.0), lookup(code, nu_t)),
    )


def into(buf):
    def store(c, i, value):
        buf[c, i] = value
    return store


def put(buf, shift=0):
    def store(at, value):
        buf[at[:-1] + (at[-1] - shift,)] = value
    return store


def edges(odd, n, width):
    return (1 - odd) * (n - width), odd * (n - width)


def first_pack_kernel(odd_ref, guess, source, regions, a1, b1, reg, sems):
    odd = odd_ref[0]
    pairs = [(regions.at[pl.ds(0, 1)], reg.at[pl.ds(0, 1)]), (regions.at[pl.ds(LX - 1, 1)], reg.at[pl.ds(1, 1)])]
    for one, two_from, one_from in zip((a1, b1), edges(odd, LX, 2), edges(odd, LX, 1)):
        for c in range(3):
            pairs.append((guess.at[0, c, pl.ds(two_from, 2)], one.at[pl.ds(2 * c, 2)]))
            pairs.append((source.at[1, c, pl.ds(one_from, 1)], one.at[pl.ds(6 + c, 1)]))
    run_copies(pairs, sems)
    a1[9] = (reg[1 - odd] + 1).astype(F32)
    b1[9] = (reg[odd] + 1).astype(F32)


def second_pack_kernel(odd_ref, source, regions, a2, b2, a3, b3, reg, sems):
    odd = odd_ref[0]
    pairs = [(regions, reg)]
    for two, start in zip((a2, b2), edges(odd, LX, 3)):
        for c in range(3):
            pairs.append((source.at[0, c, pl.ds(start, 3)], two.at[pl.ds(3 * c, 3)]))
    run_copies(pairs, sems)
    for two, start in zip((a2, b2), edges(odd, LX, 3)):
        for k in range(3):
            two[9 + k] = (reg[start + k] + 1).astype(F32)
    for three, high in ((a3, 1 - odd), (b3, odd)):
        for k in range(4):
            three[k] = (reg[high * (LX - 7) + (1 - high) * 3 + k] + 1).astype(F32)


def first_middle_kernel(cond_t, nu_t, guess, source, regions, out, y, held, cond, nu):
    def prepare(i):
        cond[i], nu[i] = materials(regions[i] + 1, cond_t, nu_t)

    over_layers(3, 9, prepare, 6)
    fine_sweep(guess.at[0], into(y), held, cond, nu, 3, 9, source.at[1])

    def store(c, i, value):
        out[c, i - 4] = value

    fine_sweep(y, store, held, cond, nu, 4, 8)


def first_kernel(odd_ref, cond_t, nu_t, guess, source, regions, ra, rb, after, out_a, out_b, x, y, held, f, cond, nu):
    odd = odd_ref[0]
    n = LX + 4
    for c in range(3):
        for i in (0, 1, 2, 3, 4, 5, 6, 7, 8, 9, 10, 11):
            x[c, i + 2] = guess[0, c, i]
            f[c, i + 2] = source[1, c, i]
    for i in range(LX):
        cond[i + 2], nu[i + 2] = materials(regions[i] + 1, cond_t, nu_t)
    for pack, high in ((ra, 1 - odd), (rb, odd)):
        for c in range(3):
            for k in range(2):
                x[c, high * (n - 2) + k] = pack[2 * c + k]
            f[c, 1 + high * (n - 3)] = pack[6 + c]
        cond[1 + high * (n - 3)], nu[1 + high * (n - 3)] = materials(pack[9], cond_t, nu_t)
    fine_sweep(x, into(y), held, cond, nu, 1, 7, f)
    fine_sweep(x, into(y), held, cond, nu, 9, n - 1, f)
    fine_sweep(y, into(x), held, cond, nu, 2, 6)
    fine_sweep(y, into(x), held, cond, nu, 10, 14)
    for c in range(3):
        for k in range(4):
            out_a[c, k] = x[c, 2 + (1 - odd) * 8 + k]
            out_b[c, k] = x[c, 2 + odd * 8 + k]


def material_kernel(odd_ref, cond_t, nu_t, regions, ra, rb, cond, nu, keep, spread):
    odd = odd_ref[0]

    def fill(at, code):
        cv, nv = materials(code, cond_t, nu_t)
        cond[at] = cv
        nu[at] = nv
        half = 0.5 * cv
        scale = 1.0 / (half + 6.0 * nv)
        keep[at] = half * scale
        spread[at] = nv * scale

    for i in range(LX):
        fill(3 + i, regions[i] + 1)
    for pack, high in ((ra, 1 - odd), (rb, odd)):
        for k in range(3):
            fill(high * (LX + 3) + k, pack[9 + k])


def wide_kernel(odd_ref, cond_t, nu_t, keep_i, spread_i, ra, rb, keep, spread):
    odd = odd_ref[0]
    for i in range(LX + 6):
        keep[i + 4] = keep_i[i]
        spread[i + 4] = spread_i[i]
    for pack, high in ((ra, 1 - odd), (rb, odd)):
        for k in range(4):
            at = high * (LX + 10) + k
            cv, nv = materials(pack[k], cond_t, nu_t)
            half = 0.5 * cv
            scale = 1.0 / (half + 6.0 * nv)
            keep[at] = half * scale
            spread[at] = nv * scale


def extend(odd, pieces, halos, x):
    a, b, m = pieces
    ha, hb = halos
    for c in range(3):
        for k in range(4):
            x[c, 8 + k] = m[c, k]
            x[c, 4 + (1 - odd) * 8 + k] = a[c, k]
            x[c, 4 + odd * 8 + k] = b[c, k]
            x[c, (1 - odd) * 16 + k] = ha[c, k]
            x[c, odd * 16 + k] = hb[c, k]


def extend_force(odd, source, which, width, packs, start, f):
    for c in range(3):
        for i in range(LX):
            f[c, 4 + i] = source[which, c, i]
        for pack, high in ((packs[0], 1 - odd), (packs[1], odd)):
            for k in range(width):
                f[c, 4 - width + high * (LX + width) + k] = pack[start + width * c + k]


def second_kernel(
    odd_ref, hb, vb, ha, va, vm, source, a1, b1, a2, b2, cond, nu,
    u0, oa, ob, om, x, y, held, f0, f1,
):
    odd = odd_ref[0]
    extend(odd, (va, vb, vm), (ha, hb), x)
    extend_force(odd, source, 0, 3, (a2, b2), 0, f0)
    extend_force(odd, source, 1, 1, (a1, b1), 6, f1)

    def keep_u0(c, i, value):
        x[c, i] = value
        u0[c, i - 2] = value

    fine_sweep(x, into(y), held, cond, nu, 1, 19, f0, 1)
    fine_sweep(y, keep_u0, held, cond, nu, 2, 18, None, 1)
    fine_sweep(x, into(y), held, cond, nu, 3, 17, f1, 1)
    fine_sweep(y, into(x), held, cond, nu, 4, 16, None, 1)
    for c in range(3):
        for k in range(4):
            om[c, k] = x[c, 8 + k]
            oa[c, k] = x[c, 4 + (1 - odd) * 8 + k]
            ob[c, k] = x[c, 4 + odd * 8 + k]


def residual_kernel(
    odd_ref, hb, vb, ha, va, vm, source, a2, b2, cond, nu, keep, spread, u0,
    res_o, l0, l1, l2, r0, r1, r2, x, y, held, f0, sems,
):
    odd = odd_ref[0]
    extend(odd, (va, vb, vm), (ha, hb), x)
    extend_force(odd, source, 0, 3, (a2, b2), 0, f0)

    def less(c, i, value):
        x[c, i] = value - u0[c, i - 2]

    fine_sweep(x, into(y), held, cond, nu, 1, 19, f0, 1)
    fine_sweep(y, less, held, cond, nu, 2, 18, None, 1)
    kept = copy_all([(x.at[:, pl.ds(4, LX)], res_o.at[0])], sems)
    comps = [(0,), (1,), (2,)]
    coarse_sweep(x, put(y), held, keep, spread, -1, 3, 17, True, comps)
    for c, out in enumerate((r0, r1, r2)):
        for i in range(LX):
            out[i] = x[c, 4 + i]

    def store(at, value):
        (l0, l1, l2)[at[0]][at[1] - 4] = value

    coarse_sweep(y, store, held, keep, spread, -1, 4, 16, False, comps)
    wait_all(kept)


def add_kernel(w, odd_ref, *refs):
    odd = odd_ref[0]
    *terms, total, sa, sb = refs
    for i in range(LX):
        value = terms[0][i]
        for term in terms[1:]:
            value = value + term[i]
        total[i] = value
    for side, top in ((sa, 1 - odd), (sb, odd)):
        for i in range(w):
            side[i] = total[i + top * (LX - w)]


def power_kernel(w, odd_ref, value, ha, hb, keep, spread, out, x, y, held):
    odd = odd_ref[0]
    for i in range(LX):
        x[i + w] = value[i]
    for side, high in ((ha, 1 - odd), (hb, odd)):
        for i in range(w):
            x[i + high * (LX + w)] = side[i]

    for step in range(w // 2):
        lo = 1 + 2 * step
        last = put(out, w) if step == w // 2 - 1 else put(x)
        coarse_sweep(x, put(y), held, keep, spread, -1, lo, LX + 2 * w - lo, True, [()])
        coarse_sweep(y, last, held, keep, spread, -1, lo + 1, LX + 2 * w - lo - 1, False, [()])


def last_kernel(
    odd_ref, p0, p1, p2, a_0, a_1, a_2, b_0, b_1, b_2, source, a1, b1, cond, nu,
    field, x, y, held, f1, sems,
):
    odd = odd_ref[0]
    kept = copy_all([(p, field.at[0, c]) for c, p in enumerate((p0, p1, p2))], sems)
    extend_force(odd, source, 1, 1, (a1, b1), 6, f1)
    for c, (p, a, b) in enumerate(((p0, a_0, b_0), (p1, a_1, b_1), (p2, a_2, b_2))):
        for i in range(LX):
            x[c, 4 + i] = p[i]
        for k in range(2):
            x[c, 2 + (1 - odd) * (LX + 2) + k] = a[k]
            x[c, 2 + odd * (LX + 2) + k] = b[k]
    fine_sweep(x, into(y), held, cond, nu, 3, 17, f1, 1)
    fine_sweep(y, into(x), held, cond, nu, 4, 10, None, 1)
    kept += copy_all([(x.at[:, pl.ds(4, 6)], field.at[1, :, pl.ds(0, 6)])], sems, 3)
    fine_sweep(y, into(x), held, cond, nu, 10, 16, None, 1)
    kept += copy_all([(x.at[:, pl.ds(10, 6)], field.at[1, :, pl.ds(6, 6)])], sems, 4)
    wait_all(kept)


def body(guess, source, regions, conductance, reluct):
    slices = lax.axis_size("tm")
    slabs = lax.axis_size("space")
    odd = (lax.axis_index("space") % 2).astype(jnp.int32).reshape(1)
    on_chip = [(i, i ^ 1) for i in range(slabs)]
    off_chip = [(i, i + 1) for i in range(1, slabs - 1, 2)]
    off_chip += [(j, i) for i, j in off_chip]
    fence = lax.optimization_barrier

    def from_a(x):
        return lax.ppermute(x, "space", on_chip)

    def from_b(x):
        return lax.ppermute(x, "space", off_chip)

    half = slices // 2
    column = lax.axis_index("tm") % half

    def later(x, distance, route="direct"):
        def send(value, pairs):
            return lax.ppermute(value, "tm", pairs)

        if route == "direct" or distance == half:
            return send(x, [(i, (i + distance) % slices) for i in range(slices)])
        wrapping = [i for i in range(slices) if i % half + distance >= half]
        if route == "first":
            stops = [(i + half) % slices for i in wrapping]
        else:
            stops = [(i - 1 + half) % slices for i in wrapping]
        around = send(send(x, list(zip(wrapping, stops))), [(j, (i + distance) % slices) for i, j in zip(wrapping, stops)])
        plain = send(x, [(i, i + distance) for i in range(slices) if i not in wrapping])
        return jnp.where(column < distance, around, plain)

    tables = (conductance, reluct)
    sa1, sb1 = call(
        first_pack_kernel, "first_pack", (odd, guess, source, regions),
        [planes(10), planes(10)], [pltpu.VMEM((2, NY, NZ), jnp.int32)], 16, in_place=HBM,
    )
    b1 = from_b(sb1)
    a1 = from_a(sa1)
    um = call(
        first_middle_kernel, "first_middle", (*tables, guess, source, regions),
        planes(3, 4), [vmem(3, LX)] * 2 + [vmem(LX)] * 2,
    )
    sa2, sb2, sa3, sb3 = call(
        second_pack_kernel, "second_pack", (odd, source, regions),
        [planes(12), planes(12), planes(4), planes(4)], [pltpu.VMEM((LX, NY, NZ), jnp.int32)], 8, in_place=HBM,
    )
    vm = later(um, 1, "first")
    sb2, sa2, b1 = fence((sb2, sa2, b1))
    b2 = from_b(sb2)
    a2 = from_a(sa2)
    ua, ub = call(
        first_kernel, "first", (odd, *tables, guess, source, regions, a1, b1, um),
        [planes(3, 4), planes(3, 4)], [vmem(3, LX + 4)] * 4 + [vmem(LX + 4)] * 2,
    )
    vb = later(ub, 1)
    va = later(ua, 1, "middle")
    cond, nu, keep, spread = call(
        material_kernel, "material", (odd, *tables, regions, a2, b2), [planes(LX + 6)] * 4, [],
    )
    va, cond = fence((va, cond))
    hb = from_b(vb)
    ha = from_a(va)
    sb3, sa3, vb = fence((sb3, sa3, vb))
    b3 = from_b(sb3)
    a3 = from_a(sa3)
    n = LX + 8
    u0, ua, ub, um = call(
        second_kernel, "second",
        (odd, hb, vb, ha, va, vm, source, a1, b1, a2, b2, cond, nu),
        [planes(3, LX + 4), planes(3, 4), planes(3, 4), planes(3, 4)], [vmem(3, n)] * 5,
    )
    vb = later(ub, 1)
    va = later(ua, 1, "middle")
    vm = later(um, 1, "first")
    hb = from_b(vb)
    ha = from_a(va)
    wide_keep, wide_spread = call(
        wide_kernel, "wide", (odd, *tables, keep, spread, a3, b3), [planes(LX + 14)] * 2, [],
    )
    residual, *rest = call(
        residual_kernel, "residual",
        (odd, hb, vb, ha, va, vm, source, a2, b2, cond, nu, keep, spread, u0),
        [planes(1, 3, LX)] + [planes(LX)] * 6, [vmem(3, n)] * 4, 1, [ANY] + [VMEM] * 6,
    )
    moving, totals = rest[:3], rest[3:]
    u0_own = [u0[c, 2:2 + LX] for c in range(3)]
    for distance, width, routes in (
        (1, 4, ("direct", "first", "middle")),
        (2, 8, ("first", "direct", "first")),
        (4, 2, ("direct",) * 3),
    ):
        moved = [later(m, distance, r) for m, r in zip(moving, routes)]
        bases = [(t,) for t in totals]
        if distance == 4:
            bases = [(t, u) for t, u in zip(totals, u0_own)]
        totals, moving, sides = [], [], []
        for c in range(3):
            total, sa, sb = call(
                functools.partial(add_kernel, width), "add%d" % width, (odd, *bases[c], moved[c]),
                [planes(LX), planes(width), planes(width)], [],
            )
            hb = from_b(sb)
            ha = from_a(sa)
            totals.append(total)
            sides.append((ha, hb))
            if distance < 4:
                pair = (wide_keep, wide_spread) if width == 8 else (keep, spread)
                moving.append(
                    call(
                        functools.partial(power_kernel, width), "power%d" % width,
                        (odd, total, ha, hb, *pair), planes(LX), [vmem(LX + 2 * width)] * 3,
                    )
                )
    field = call(
        last_kernel, "last",
        (odd, *totals, *[s[0] for s in sides], *[s[1] for s in sides], source, a1, b1, cond, nu),
        planes(2, 3, LX), [vmem(3, n)] * 4, 5, ANY,
    )
    return field, residual


def solution(mesh):
    whole = P("tm", None, "space", None, None)
    return jax.shard_map(
        body, mesh=mesh, in_specs=(whole, whole, P("space", None, None), P(), P()),
        out_specs=(whole, whole), check_vma=False,
    )
```

```python
import jax
import jax.numpy as jnp
from jax import lax
from jax.experimental import pallas as pl
from jax.experimental.pallas import tpu as pltpu
from jax.sharding import PartitionSpec as P

LX, NY, NZ = 12, 64, 128
F32 = jnp.float32
ANY = pl.BlockSpec(memory_space=pl.ANY)
HBM = pl.BlockSpec(memory_space=pltpu.HBM)
VMEM = pl.BlockSpec(memory_space=pltpu.VMEM)
COMPS = [(0,), (1,), (2,)]
SMEM = pl.BlockSpec(memory_space=pltpu.SMEM)


def planes(*lead):
    return jax.ShapeDtypeStruct(tuple(lead) + (NY, NZ), F32)


def vmem(*lead):
    return pltpu.VMEM(tuple(lead) + (NY, NZ), F32)


def copy_all(pairs, sems, base=0):
    copies = [
        pltpu.make_async_copy(src, dst, sems.at[base + n]) for n, (src, dst) in enumerate(pairs)
    ]
    for copy in copies:
        copy.start()
    return copies


def wait_all(copies):
    for copy in copies:
        copy.wait()


def run_copies(pairs, sems, base=0):
    wait_all(copy_all(pairs, sems, base))


def call(kernel, name, args, outs, scratch, n_sems=0, out_specs=None, in_place=VMEM):
    in_specs = [SMEM if a.ndim == 1 else in_place for a in args]
    single = not isinstance(outs, (list, tuple))
    return pl.pallas_call(
        kernel,
        name=name,
        out_shape=outs,
        in_specs=in_specs,
        out_specs=out_specs or (VMEM if single else [VMEM] * len(outs)),
        scratch_shapes=list(scratch) + [pltpu.SemaphoreType.DMA((n_sems,))] * (n_sems > 0),
        compiler_params=pltpu.CompilerParams(vmem_limit_bytes=16 * 1024 * 1024),
        cost_estimate=pl.CostEstimate(flops=0, bytes_accessed=4 << 20, transcendentals=0),
    )(*args)


def over_layers(lo, hi, step, at_once):
    rounds = (hi - lo) // at_once

    def body(t, carry):
        for k in range(at_once):
            step(lo + t * at_once + k)
        return carry

    lax.fori_loop(0, rounds, body, 0)
    for i in range(lo + rounds * at_once, hi):
        step(i)


def neighbours(src, at):
    row = lax.broadcasted_iota(jnp.int32, (NY, NZ), 0)
    lane = lax.broadcasted_iota(jnp.int32, (NY, NZ), 1)
    zero = jnp.float32(0.0)
    def of(*lead_i):
        *lead, i = lead_i
        a = src[(*lead, i)]
        first = src[(*lead, i + 1)] + src[(*lead, i - 1)]
        up = jnp.where(row == 0, zero, pltpu.roll(a, 1, 0))
        down = jnp.where(row == NY - 1, zero, pltpu.roll(a, NY - 1, 0))
        left = jnp.where(lane == 0, zero, pltpu.roll(a, 1, 1))
        right = jnp.where(lane == NZ - 1, zero, pltpu.roll(a, NZ - 1, 1))
        return (first + (up + down)) + (left + right)
    return of(*at)


def fine_sweep(src, store, held, cond, nu, lo, hi, force=None, off=0):
    def step(i):
        square = src[0, i] * src[0, i] + src[1, i] * src[1, i] + src[2, i] * src[2, i]
        base = nu[i - off]
        weight = cond[i - off]
        grown = 1.0 + square
        strong = base * (1.0 + 1.5 * square)
        scale = 1.0 / (weight * grown + 6.0 * strong)
        keep = grown * scale
        spread = strong * scale
        for c in range(3):
            if force is not None:
                fixed = weight * src[c, i] + force[c, i]
                held[c, i] = fixed
            else:
                fixed = held[c, i]
            store(c, i, fixed * keep + neighbours(src, (c, i)) * spread)

    over_layers(lo, hi, step, 4)


def coarse_sweep(src, store, held, keep, spread, off, lo, hi, first, comps):
    def step(i):
        k = keep[i + off]
        s = spread[i + off]
        for lead in comps:
            at = lead + (i,)
            if first:
                fixed = k * src[at]
                held[at] = fixed
            else:
                fixed = held[at]
            store(at, fixed + s * neighbours(src, at))

    over_layers(lo, hi, step, 8 if len(comps) == 1 else 3)


def lookup(code, table):
    first = jnp.where(code == 1, table[0], table[1])
    second = jnp.where(code == 3, table[2], table[3])
    return jnp.where(code <= 2, first, second)


def materials(code, cond_t, nu_t):
    outside = code == 0
    return (
        jnp.where(outside, jnp.float32(1.0), lookup(code, cond_t)),
        jnp.where(outside, jnp.float32(0.0), lookup(code, nu_t)),
    )


def into(buf):
    def store(c, i, value):
        buf[c, i] = value
    return store


def put(buf, shift=0):
    def store(at, value):
        buf[at[:-1] + (at[-1] - shift,)] = value
    return store


def edges(odd, n, width):
    return (1 - odd) * (n - width), odd * (n - width)


def first_pack_kernel(odd_ref, guess, source, regions, a1, b1, reg, sems):
    odd = odd_ref[0]
    pairs = [(regions.at[pl.ds(0, 1)], reg.at[pl.ds(0, 1)]), (regions.at[pl.ds(LX - 1, 1)], reg.at[pl.ds(1, 1)])]
    for one, two_from, one_from in zip((a1, b1), edges(odd, LX, 2), edges(odd, LX, 1)):
        for c in range(3):
            pairs.append((guess.at[0, c, pl.ds(two_from, 2)], one.at[pl.ds(2 * c, 2)]))
            pairs.append((source.at[1, c, pl.ds(one_from, 1)], one.at[pl.ds(6 + c, 1)]))
    run_copies(pairs, sems)
    a1[9] = (reg[1 - odd] + 1).astype(F32)
    b1[9] = (reg[odd] + 1).astype(F32)


def second_pack_kernel(odd_ref, source, regions, a2, b2, a3, b3, reg, sems):
    odd = odd_ref[0]
    pairs = [(regions, reg)]
    for two, start in zip((a2, b2), edges(odd, LX, 3)):
        for c in range(3):
            pairs.append((source.at[0, c, pl.ds(start, 3)], two.at[pl.ds(3 * c, 3)]))
    run_copies(pairs, sems)
    for two, start in zip((a2, b2), edges(odd, LX, 3)):
        for k in range(3):
            two[9 + k] = (reg[start + k] + 1).astype(F32)
    for three, high in ((a3, 1 - odd), (b3, odd)):
        for k in range(4):
            three[k] = (reg[high * (LX - 7) + (1 - high) * 3 + k] + 1).astype(F32)


def first_middle_kernel(cond_t, nu_t, guess, source, regions, out, y, held, cond, nu):
    def prepare(i):
        cond[i], nu[i] = materials(regions[i] + 1, cond_t, nu_t)

    over_layers(3, 9, prepare, 6)
    fine_sweep(guess.at[0], into(y), held, cond, nu, 3, 9, source.at[1])

    def store(c, i, value):
        out[c, i - 4] = value

    fine_sweep(y, store, held, cond, nu, 4, 8)


def first_kernel(odd_ref, cond_t, nu_t, guess, source, regions, ra, rb, after, out_a, out_b, x, y, held, f, cond, nu):
    odd = odd_ref[0]
    n = LX + 4
    for c in range(3):
        for i in (0, 1, 2, 3, 4, 5, 6, 7, 8, 9, 10, 11):
            x[c, i + 2] = guess[0, c, i]
            f[c, i + 2] = source[1, c, i]
    for i in range(LX):
        cond[i + 2], nu[i + 2] = materials(regions[i] + 1, cond_t, nu_t)
    for pack, high in ((ra, 1 - odd), (rb, odd)):
        for c in range(3):
            for k in range(2):
                x[c, high * (n - 2) + k] = pack[2 * c + k]
            f[c, 1 + high * (n - 3)] = pack[6 + c]
        cond[1 + high * (n - 3)], nu[1 + high * (n - 3)] = materials(pack[9], cond_t, nu_t)
    fine_sweep(x, into(y), held, cond, nu, 1, 7, f)
    fine_sweep(x, into(y), held, cond, nu, 9, n - 1, f)
    fine_sweep(y, into(x), held, cond, nu, 2, 6)
    fine_sweep(y, into(x), held, cond, nu, 10, 14)
    for c in range(3):
        for k in range(4):
            out_a[c, k] = x[c, 2 + (1 - odd) * 8 + k]
            out_b[c, k] = x[c, 2 + odd * 8 + k]


def material_kernel(odd_ref, cond_t, nu_t, regions, ra, rb, cond, nu, keep, spread):
    odd = odd_ref[0]

    def fill(at, code):
        cv, nv = materials(code, cond_t, nu_t)
        cond[at] = cv
        nu[at] = nv
        half = 0.5 * cv
        scale = 1.0 / (half + 6.0 * nv)
        keep[at] = half * scale
        spread[at] = nv * scale

    for i in range(LX):
        fill(3 + i, regions[i] + 1)
    for pack, high in ((ra, 1 - odd), (rb, odd)):
        for k in range(3):
            fill(high * (LX + 3) + k, pack[9 + k])


def wide_kernel(odd_ref, cond_t, nu_t, keep_i, spread_i, ra, rb, keep, spread):
    odd = odd_ref[0]
    for i in range(LX + 6):
        keep[i + 4] = keep_i[i]
        spread[i + 4] = spread_i[i]
    for pack, high in ((ra, 1 - odd), (rb, odd)):
        for k in range(4):
            at = high * (LX + 10) + k
            cv, nv = materials(pack[k], cond_t, nu_t)
            half = 0.5 * cv
            scale = 1.0 / (half + 6.0 * nv)
            keep[at] = half * scale
            spread[at] = nv * scale


def extend(odd, pieces, halos, x):
    a, b, *m = pieces
    ha, hb = halos
    for c in range(3):
        for k in range(4):
            middle = m[0][c, k]
            for other in m[1:]:
                middle = middle + other[c, k]
            x[c, 8 + k] = middle
            x[c, 4 + (1 - odd) * 8 + k] = a[c, k]
            x[c, 4 + odd * 8 + k] = b[c, k]
            x[c, (1 - odd) * 16 + k] = ha[c, k]
            x[c, odd * 16 + k] = hb[c, k]


def extend_force(odd, source, which, width, packs, start, f):
    for c in range(3):
        for i in range(LX):
            f[c, 4 + i] = source[which, c, i]
        for pack, high in ((packs[0], 1 - odd), (packs[1], odd)):
            for k in range(width):
                f[c, 4 - width + high * (LX + width) + k] = pack[start + width * c + k]


def second_kernel(
    odd_ref, hb, vb, ha, va, vm, vn, source, a1, b1, a2, b2, cond, nu,
    u0, oa, ob, om, x, y, held, f0, f1,
):
    odd = odd_ref[0]
    extend(odd, (va, vb, vm, vn), (ha, hb), x)
    extend_force(odd, source, 0, 3, (a2, b2), 0, f0)
    extend_force(odd, source, 1, 1, (a1, b1), 6, f1)

    def keep_u0(c, i, value):
        x[c, i] = value
        u0[c, i - 2] = value

    fine_sweep(x, into(y), held, cond, nu, 1, 19, f0, 1)
    fine_sweep(y, keep_u0, held, cond, nu, 2, 18, None, 1)
    fine_sweep(x, into(y), held, cond, nu, 3, 17, f1, 1)
    fine_sweep(y, into(x), held, cond, nu, 4, 16, None, 1)
    for c in range(3):
        for k in range(4):
            om[c, k] = x[c, 8 + k]
            oa[c, k] = x[c, 4 + (1 - odd) * 8 + k]
            ob[c, k] = x[c, 4 + odd * 8 + k]


def split(odd, x, start, b, a, m):
    for c in range(3):
        for k in range(4):
            b[c, k] = x[c, start + odd * 8 + k]
            a[c, k] = x[c, start + (1 - odd) * 8 + k]
            m[c, k] = x[c, start + 4 + k]


def residual_kernel(
    odd_ref, hb, vb, ha, va, vm, vn, source, a2, b2, cond, nu, keep, spread, u0,
    res_o, lb, la, lm, rb, ra, rm, x, y, held, f0, sems,
):
    odd = odd_ref[0]
    extend(odd, (va, vb, vm, vn), (ha, hb), x)
    extend_force(odd, source, 0, 3, (a2, b2), 0, f0)

    def less(c, i, value):
        x[c, i] = value - u0[c, i - 2]

    fine_sweep(x, into(y), held, cond, nu, 1, 19, f0, 1)
    fine_sweep(y, less, held, cond, nu, 2, 18, None, 1)
    kept = copy_all([(x.at[:, pl.ds(4, LX)], res_o.at[0])], sems)
    split(odd, x, 4, rb, ra, rm)
    coarse_sweep(x, put(y), held, keep, spread, -1, 3, 17, True, COMPS)
    wait_all(kept)
    coarse_sweep(y, put(x), held, keep, spread, -1, 4, 16, False, COMPS)
    split(odd, x, 4, lb, la, lm)


def square_kernel(odd_ref, hb, sb, ha, sa, sm, keep, spread, ob, oa, om, x, y, held):
    odd = odd_ref[0]
    extend(odd, (sa, sb, sm), (ha, hb), x)
    for lo in (1, 3):
        coarse_sweep(x, put(y), held, keep, spread, -1, lo, 20 - lo, True, COMPS)
        coarse_sweep(y, put(x), held, keep, spread, -1, lo + 1, 19 - lo, False, COMPS)
    split(odd, x, 4, ob, oa, om)


def fourth_kernel(
    odd_ref, near_b, tb, far_b, tm, far_a, near_a, ta, u0, keep, spread,
    ob, oa, om, bb, ba, bm, x, y, held,
):
    odd = odd_ref[0]
    for c in range(3):
        for k in range(4):
            x[c, 8 + odd * 8 + k] = tb[c, k]
            x[c, 8 + (1 - odd) * 8 + k] = ta[c, k]
            x[c, 12 + k] = tm[c, k]
            x[c, 4 + odd * 16 + k] = near_b[c, k]
            x[c, 4 + (1 - odd) * 16 + k] = near_a[c, k]
            x[c, odd * 24 + k] = far_b[c, k]
            x[c, (1 - odd) * 24 + k] = far_a[c, k]
    for c in range(3):
        for k in range(4):
            bb[c, k] = tb[c, k] + u0[c, 2 + odd * 8 + k]
            ba[c, k] = ta[c, k] + u0[c, 2 + (1 - odd) * 8 + k]
            bm[c, k] = tm[c, k] + u0[c, 6 + k]
    for lo in (1, 3, 5, 7):
        coarse_sweep(x, put(y), held, keep, spread, -1, lo, 28 - lo, True, COMPS)
        coarse_sweep(y, put(x), held, keep, spread, -1, lo + 1, 27 - lo, False, COMPS)
    split(odd, x, 8, ob, oa, om)


def edge_kernel(odd_ref, base, moved, total, edge):
    odd = odd_ref[0]
    for c in range(3):
        for k in range(4):
            total[c, k] = base[c, k] + moved[c, k]
        for k in range(2):
            edge[c, k] = total[c, odd * 2 + k]


def last_kernel(
    odd_ref, hb, eb, ha, ea, em, source, a1, b1, cond, nu, field, x, y, held, f1, sems,
):
    odd = odd_ref[0]
    kept = copy_all(
        [
            (eb, field.at[0, :, pl.ds(odd * 8, 4)]),
            (ea, field.at[0, :, pl.ds((1 - odd) * 8, 4)]),
            (em, field.at[0, :, pl.ds(4, 4)]),
        ],
        sems,
    )
    extend_force(odd, source, 1, 1, (a1, b1), 6, f1)
    for c in range(3):
        for k in range(4):
            x[c, 4 + odd * 8 + k] = eb[c, k]
            x[c, 4 + (1 - odd) * 8 + k] = ea[c, k]
            x[c, 8 + k] = em[c, k]
        for k in range(2):
            x[c, 2 + odd * 14 + k] = hb[c, k]
            x[c, 2 + (1 - odd) * 14 + k] = ha[c, odd * 2 + k]
    fine_sweep(x, into(y), held, cond, nu, 3, 17, f1, 1)
    fine_sweep(y, into(x), held, cond, nu, 4, 10, None, 1)
    kept += copy_all([(x.at[:, pl.ds(4, 6)], field.at[1, :, pl.ds(0, 6)])], sems, 3)
    fine_sweep(y, into(x), held, cond, nu, 10, 16, None, 1)
    kept += copy_all([(x.at[:, pl.ds(10, 6)], field.at[1, :, pl.ds(6, 6)])], sems, 4)
    wait_all(kept)


def body(guess, source, regions, conductance, reluct):
    slices = lax.axis_size("tm")
    slabs = lax.axis_size("space")
    odd = (lax.axis_index("space") % 2).astype(jnp.int32).reshape(1)
    on_chip = [(i, i ^ 1) for i in range(slabs)]
    off_chip = [(i, i + 1) for i in range(1, slabs - 1, 2)]
    off_chip += [(j, i) for i, j in off_chip]
    fence = lax.optimization_barrier

    def from_a(x):
        return lax.ppermute(x, "space", on_chip)

    def from_b(x):
        return lax.ppermute(x, "space", off_chip)

    half = slices // 2

    def along(x, pairs):
        return lax.ppermute(x, "tm", pairs)

    def later(x, distance):
        return along(x, [(i, (i + distance) % slices) for i in range(slices)])

    def later_parts(x, distance):
        wrapping = [i for i in range(slices) if i % half + distance >= half]
        across = along(x, [(i, (i + half) % slices) for i in wrapping])
        around = along(across, [((i + half) % slices, (i + distance) % slices) for i in wrapping])
        plain = along(x, [(i, i + distance) for i in range(slices) if i not in wrapping])
        return around, plain

    tables = (conductance, reluct)
    sa1, sb1 = call(
        first_pack_kernel, "first_pack", (odd, guess, source, regions),
        [planes(10), planes(10)], [pltpu.VMEM((2, NY, NZ), jnp.int32)], 16, in_place=HBM,
    )
    b1 = from_b(sb1)
    a1 = from_a(sa1)
    um = call(
        first_middle_kernel, "first_middle", (*tables, guess, source, regions),
        planes(3, 4), [vmem(3, LX)] * 2 + [vmem(LX)] * 2,
    )
    sa2, sb2, sa3, sb3 = call(
        second_pack_kernel, "second_pack", (odd, source, regions),
        [planes(12), planes(12), planes(4), planes(4)], [pltpu.VMEM((LX, NY, NZ), jnp.int32)], 8, in_place=HBM,
    )
    vm = later_parts(um, 1)
    sb2, sa2, b1 = fence((sb2, sa2, b1))
    b2 = from_b(sb2)
    a2 = from_a(sa2)
    ua, ub = call(
        first_kernel, "first", (odd, *tables, guess, source, regions, a1, b1, um),
        [planes(3, 4), planes(3, 4)], [vmem(3, LX + 4)] * 4 + [vmem(LX + 4)] * 2,
    )
    vb = later(ub, 1)
    va = later(ua, 1)
    cond, nu, keep, spread = call(
        material_kernel, "material", (odd, *tables, regions, a2, b2), [planes(LX + 6)] * 4, [],
    )
    va, cond = fence((va, cond))
    hb = from_b(vb)
    ha = from_a(va)
    sb3, sa3, vb = fence((sb3, sa3, vb))
    b3 = from_b(sb3)
    a3 = from_a(sa3)
    n = LX + 8
    u0, ua, ub, um = call(
        second_kernel, "second",
        (odd, hb, vb, ha, va, *vm, source, a1, b1, a2, b2, cond, nu),
        [planes(3, LX + 4), planes(3, 4), planes(3, 4), planes(3, 4)], [vmem(3, n)] * 5,
    )
    vb = later(ub, 1)
    va = later(ua, 1)
    vm = later_parts(um, 1)
    hb = from_b(vb)
    ha = from_a(va)
    wide_keep, wide_spread = call(
        wide_kernel, "wide", (odd, *tables, keep, spread, a3, b3), [planes(LX + 14)] * 2, [],
    )
    residual, lb, la, lm, rb, ra, rm = call(
        residual_kernel, "residual",
        (odd, hb, vb, ha, va, *vm, source, a2, b2, cond, nu, keep, spread, u0),
        [planes(1, 3, LX)] + [planes(3, 4)] * 6, [vmem(3, n)] * 4, 1, [ANY] + [VMEM] * 6,
    )
    sb = rb + later(lb, 1)
    hb = from_b(sb)
    sa = ra + later(la, 1)
    ha = from_a(sa)
    around, plain = later_parts(lm, 1)
    sm = rm + (around + plain)
    lb, la, lm = call(
        square_kernel, "square", (odd, hb, sb, ha, sa, sm, keep, spread),
        [planes(3, 4)] * 3, [vmem(3, n)] * 3,
    )
    tb = sb + later(lb, 2)
    near_b = from_b(tb)
    tm = sm + later(lm, 2)
    far_b = from_b(tm)
    around, plain = later_parts(la, 2)
    ta = sa + (around + plain)
    near_a = from_a(ta)
    far_a = from_a(tm)
    lb, la, lm, bb, ba, bm = call(
        fourth_kernel, "fourth",
        (odd, near_b, tb, far_b, tm, far_a, near_a, ta, u0, wide_keep, wide_spread),
        [planes(3, 4)] * 6, [vmem(3, LX + 16)] * 3,
    )
    eb, edge = call(
        edge_kernel, "edge", (odd, bb, later(lb, half)), [planes(3, 4), planes(3, 2)], [],
    )
    hb = from_b(edge)
    ea, edge = lax.optimization_barrier((ba + later(la, half), edge))
    ha = from_a(ea)
    em = bm + later(lm, half)
    field = call(
        last_kernel, "last", (odd, hb, eb, ha, ea, em, source, a1, b1, cond, nu),
        planes(2, 3, LX), [vmem(3, n)] * 4, 5, ANY,
    )
    return field, residual


def solution(mesh):
    whole = P("tm", None, "space", None, None)
    return jax.shard_map(
        body, mesh=mesh, in_specs=(whole, whole, P("space", None, None), P(), P()),
        out_specs=(whole, whole), check_vma=False,
    )
```

```python
import jax
import jax.numpy as jnp
from jax import lax
from jax.experimental import pallas as pl
from jax.experimental.pallas import tpu as pltpu
from jax.sharding import PartitionSpec as P

LX, NY, NZ = 12, 64, 128
F32 = jnp.float32
ANY = pl.BlockSpec(memory_space=pl.ANY)
HBM = pl.BlockSpec(memory_space=pltpu.HBM)
VMEM = pl.BlockSpec(memory_space=pltpu.VMEM)
COMPS = [(0,), (1,), (2,)]
SMEM = pl.BlockSpec(memory_space=pltpu.SMEM)


def planes(*lead):
    return jax.ShapeDtypeStruct(tuple(lead) + (NY, NZ), F32)


def vmem(*lead):
    return pltpu.VMEM(tuple(lead) + (NY, NZ), F32)


def copy_all(pairs, sems, base=0):
    copies = [
        pltpu.make_async_copy(src, dst, sems.at[base + n]) for n, (src, dst) in enumerate(pairs)
    ]
    for copy in copies:
        copy.start()
    return copies


def wait_all(copies):
    for copy in copies:
        copy.wait()


def run_copies(pairs, sems, base=0):
    wait_all(copy_all(pairs, sems, base))


def call(kernel, name, args, outs, scratch, n_sems=0, out_specs=None, in_place=VMEM):
    in_specs = [SMEM if a.ndim == 1 else in_place for a in args]
    single = not isinstance(outs, (list, tuple))
    return pl.pallas_call(
        kernel,
        name=name,
        out_shape=outs,
        in_specs=in_specs,
        out_specs=out_specs or (VMEM if single else [VMEM] * len(outs)),
        scratch_shapes=list(scratch) + [pltpu.SemaphoreType.DMA((n_sems,))] * (n_sems > 0),
        compiler_params=pltpu.CompilerParams(vmem_limit_bytes=16 * 1024 * 1024),
        cost_estimate=pl.CostEstimate(flops=0, bytes_accessed=4 << 20, transcendentals=0),
    )(*args)


def over_layers(lo, hi, step, at_once):
    rounds = (hi - lo) // at_once

    def body(t, carry):
        for k in range(at_once):
            step(lo + t * at_once + k)
        return carry

    lax.fori_loop(0, rounds, body, 0)
    for i in range(lo + rounds * at_once, hi):
        step(i)


def neighbours(src, at):
    row = lax.broadcasted_iota(jnp.int32, (NY, NZ), 0)
    lane = lax.broadcasted_iota(jnp.int32, (NY, NZ), 1)
    zero = jnp.float32(0.0)
    def of(*lead_i):
        *lead, i = lead_i
        a = src[(*lead, i)]
        first = src[(*lead, i + 1)] + src[(*lead, i - 1)]
        up = jnp.where(row == 0, zero, pltpu.roll(a, 1, 0))
        down = jnp.where(row == NY - 1, zero, pltpu.roll(a, NY - 1, 0))
        left = jnp.where(lane == 0, zero, pltpu.roll(a, 1, 1))
        right = jnp.where(lane == NZ - 1, zero, pltpu.roll(a, NZ - 1, 1))
        return (first + (up + down)) + (left + right)
    return of(*at)


def fine_sweep(src, store, held, cond, nu, lo, hi, force=None, off=0):
    def step(i):
        square = src[0, i] * src[0, i] + src[1, i] * src[1, i] + src[2, i] * src[2, i]
        base = nu[i - off]
        weight = cond[i - off]
        grown = 1.0 + square
        strong = base * (1.0 + 1.5 * square)
        scale = 1.0 / (weight * grown + 6.0 * strong)
        keep = grown * scale
        spread = strong * scale
        for c in range(3):
            if force is not None:
                fixed = weight * src[c, i] + force[c, i]
                held[c, i] = fixed
            else:
                fixed = held[c, i]
            store(c, i, fixed * keep + neighbours(src, (c, i)) * spread)

    over_layers(lo, hi, step, 4)


def coarse_sweep(src, store, held, keep, spread, off, lo, hi, first, comps):
    def step(i):
        k = keep[i + off]
        s = spread[i + off]
        for lead in comps:
            at = lead + (i,)
            if first:
                fixed = k * src[at]
                held[at] = fixed
            else:
                fixed = held[at]
            store(at, fixed + s * neighbours(src, at))

    over_layers(lo, hi, step, 8 if len(comps) == 1 else 3)


def lookup(code, table):
    first = jnp.where(code == 1, table[0], table[1])
    second = jnp.where(code == 3, table[2], table[3])
    return jnp.where(code <= 2, first, second)


def materials(code, cond_t, nu_t):
    outside = code == 0
    return (
        jnp.where(outside, jnp.float32(1.0), lookup(code, cond_t)),
        jnp.where(outside, jnp.float32(0.0), lookup(code, nu_t)),
    )


def into(buf):
    def store(c, i, value):
        buf[c, i] = value
    return store


def put(buf, shift=0):
    def store(at, value):
        buf[at[:-1] + (at[-1] - shift,)] = value
    return store


def edges(odd, n, width):
    return (1 - odd) * (n - width), odd * (n - width)


def first_pack_kernel(odd_ref, g_low, g_high, s_low, s_high, r_low, r_high, a1, b1):
    odd = odd_ref[0]

    def fill(low, high):
        for c in range(3):
            for k in range(2):
                low[2 * c + k] = g_low[0, c, k]
                high[2 * c + k] = g_high[0, c, k]
            low[6 + c] = s_low[0, c, 0]
            high[6 + c] = s_high[0, c, 0]
        low[9] = (r_low[0] + 1).astype(F32)
        high[9] = (r_high[0] + 1).astype(F32)

    @pl.when(odd == 0)
    def even_slab():
        fill(b1, a1)

    @pl.when(odd == 1)
    def odd_slab():
        fill(a1, b1)


def second_pack_kernel(odd_ref, source, regions, a2, b2, a3, b3, reg, sems):
    odd = odd_ref[0]
    pairs = [(regions, reg)]
    for two, start in zip((a2, b2), edges(odd, LX, 3)):
        for c in range(3):
            pairs.append((source.at[0, c, pl.ds(start, 3)], two.at[pl.ds(3 * c, 3)]))
    run_copies(pairs, sems)
    for two, start in zip((a2, b2), edges(odd, LX, 3)):
        for k in range(3):
            two[9 + k] = (reg[start + k] + 1).astype(F32)
    for three, high in ((a3, 1 - odd), (b3, odd)):
        for k in range(4):
            three[k] = (reg[high * (LX - 7) + (1 - high) * 3 + k] + 1).astype(F32)


def first_middle_kernel(cond_t, nu_t, guess, source, regions, out, y, held, cond, nu):
    def prepare(i):
        cond[i], nu[i] = materials(regions[i] + 1, cond_t, nu_t)

    over_layers(3, 9, prepare, 6)
    fine_sweep(guess.at[0], into(y), held, cond, nu, 3, 9, source.at[1])

    def store(c, i, value):
        out[c, i - 4] = value

    fine_sweep(y, store, held, cond, nu, 4, 8)


def first_kernel(odd_ref, cond_t, nu_t, guess, source, regions, ra, rb, after, out_a, out_b, x, y, held, f, cond, nu):
    odd = odd_ref[0]
    n = LX + 4
    for c in range(3):
        for i in (0, 1, 2, 3, 4, 5, 6, 7, 8, 9, 10, 11):
            x[c, i + 2] = guess[0, c, i]
            f[c, i + 2] = source[1, c, i]
    for i in range(LX):
        cond[i + 2], nu[i + 2] = materials(regions[i] + 1, cond_t, nu_t)
    for pack, high in ((ra, 1 - odd), (rb, odd)):
        for c in range(3):
            for k in range(2):
                x[c, high * (n - 2) + k] = pack[2 * c + k]
            f[c, 1 + high * (n - 3)] = pack[6 + c]
        cond[1 + high * (n - 3)], nu[1 + high * (n - 3)] = materials(pack[9], cond_t, nu_t)
    fine_sweep(x, into(y), held, cond, nu, 1, 7, f)
    fine_sweep(x, into(y), held, cond, nu, 9, n - 1, f)
    fine_sweep(y, into(x), held, cond, nu, 2, 6)
    fine_sweep(y, into(x), held, cond, nu, 10, 14)
    for c in range(3):
        for k in range(4):
            out_a[c, k] = x[c, 2 + (1 - odd) * 8 + k]
            out_b[c, k] = x[c, 2 + odd * 8 + k]


def material_kernel(odd_ref, cond_t, nu_t, regions, ra, rb, cond, nu, keep, spread):
    odd = odd_ref[0]

    def fill(at, code):
        cv, nv = materials(code, cond_t, nu_t)
        cond[at] = cv
        nu[at] = nv
        half = 0.5 * cv
        scale = 1.0 / (half + 6.0 * nv)
        keep[at] = half * scale
        spread[at] = nv * scale

    for i in range(LX):
        fill(3 + i, regions[i] + 1)
    for pack, high in ((ra, 1 - odd), (rb, odd)):
        for k in range(3):
            fill(high * (LX + 3) + k, pack[9 + k])


def wide_kernel(odd_ref, cond_t, nu_t, keep_i, spread_i, ra, rb, keep, spread):
    odd = odd_ref[0]
    for i in range(LX + 6):
        keep[i + 4] = keep_i[i]
        spread[i + 4] = spread_i[i]
    for pack, high in ((ra, 1 - odd), (rb, odd)):
        for k in range(4):
            at = high * (LX + 10) + k
            cv, nv = materials(pack[k], cond_t, nu_t)
            half = 0.5 * cv
            scale = 1.0 / (half + 6.0 * nv)
            keep[at] = half * scale
            spread[at] = nv * scale


def extend(odd, pieces, halos, x):
    a, b, *m = pieces
    ha, hb = halos
    for c in range(3):
        for k in range(4):
            middle = m[0][c, k]
            for other in m[1:]:
                middle = middle + other[c, k]
            x[c, 8 + k] = middle
            x[c, 4 + (1 - odd) * 8 + k] = a[c, k]
            x[c, 4 + odd * 8 + k] = b[c, k]
            x[c, (1 - odd) * 16 + k] = ha[c, k]
            x[c, odd * 16 + k] = hb[c, k]


def extend_force(odd, source, which, width, packs, start, f):
    for c in range(3):
        for i in range(LX):
            f[c, 4 + i] = source[which, c, i]
        for pack, high in ((packs[0], 1 - odd), (packs[1], odd)):
            for k in range(width):
                f[c, 4 - width + high * (LX + width) + k] = pack[start + width * c + k]


def second_kernel(
    odd_ref, hb, vb, ha, va, vm, vn, source, a1, b1, a2, b2, cond, nu,
    u0, oa, ob, om, x, y, held, f0, f1,
):
    odd = odd_ref[0]
    extend(odd, (va, vb, vm, vn), (ha, hb), x)
    extend_force(odd, source, 0, 3, (a2, b2), 0, f0)
    extend_force(odd, source, 1, 1, (a1, b1), 6, f1)

    def keep_u0(c, i, value):
        x[c, i] = value
        u0[c, i - 2] = value

    fine_sweep(x, into(y), held, cond, nu, 1, 19, f0, 1)
    fine_sweep(y, keep_u0, held, cond, nu, 2, 18, None, 1)
    fine_sweep(x, into(y), held, cond, nu, 3, 17, f1, 1)
    fine_sweep(y, into(x), held, cond, nu, 4, 16, None, 1)
    for c in range(3):
        for k in range(4):
            om[c, k] = x[c, 8 + k]
            oa[c, k] = x[c, 4 + (1 - odd) * 8 + k]
            ob[c, k] = x[c, 4 + odd * 8 + k]


def split(odd, x, start, b, a, m):
    for c in range(3):
        for k in range(4):
            b[c, k] = x[c, start + odd * 8 + k]
            a[c, k] = x[c, start + (1 - odd) * 8 + k]
            m[c, k] = x[c, start + 4 + k]


def residual_kernel(
    odd_ref, hb, vb, ha, va, vm, vn, source, a2, b2, cond, nu, keep, spread, u0,
    res_o, lb, la, lm, rb, ra, rm, x, y, held, f0, sems,
):
    odd = odd_ref[0]
    extend(odd, (va, vb, vm, vn), (ha, hb), x)
    extend_force(odd, source, 0, 3, (a2, b2), 0, f0)

    def less(c, i, value):
        x[c, i] = value - u0[c, i - 2]

    fine_sweep(x, into(y), held, cond, nu, 1, 19, f0, 1)
    fine_sweep(y, less, held, cond, nu, 2, 18, None, 1)
    kept = copy_all([(x.at[:, pl.ds(4, LX)], res_o.at[0])], sems)
    split(odd, x, 4, rb, ra, rm)
    coarse_sweep(x, put(y), held, keep, spread, 3, 3, 17, True, COMPS)
    wait_all(kept)
    coarse_sweep(y, put(x), held, keep, spread, 3, 4, 16, False, COMPS)
    split(odd, x, 4, lb, la, lm)


def square_kernel(odd_ref, hb, sb, ha, sa, sm, keep, spread, ob, oa, om, x, y, held):
    odd = odd_ref[0]
    extend(odd, (sa, sb, sm), (ha, hb), x)
    for lo in (1, 3):
        coarse_sweep(x, put(y), held, keep, spread, -1, lo, 20 - lo, True, COMPS)
        coarse_sweep(y, put(x), held, keep, spread, -1, lo + 1, 19 - lo, False, COMPS)
    split(odd, x, 4, ob, oa, om)


def fourth_kernel(
    odd_ref, near_b, tb, far_b, tm, far_a, near_a, ta, u0, keep, spread,
    ob, oa, om, bb, ba, bm, x, y, held,
):
    odd = odd_ref[0]
    for c in range(3):
        for k in range(4):
            x[c, 8 + odd * 8 + k] = tb[c, k]
            x[c, 8 + (1 - odd) * 8 + k] = ta[c, k]
            x[c, 12 + k] = tm[c, k]
            x[c, 4 + odd * 16 + k] = near_b[c, k]
            x[c, 4 + (1 - odd) * 16 + k] = near_a[c, k]
            x[c, odd * 24 + k] = far_b[c, k]
            x[c, (1 - odd) * 24 + k] = far_a[c, k]
    for c in range(3):
        for k in range(4):
            bb[c, k] = tb[c, k] + u0[c, 2 + odd * 8 + k]
            ba[c, k] = ta[c, k] + u0[c, 2 + (1 - odd) * 8 + k]
            bm[c, k] = tm[c, k] + u0[c, 6 + k]
    for lo in (1, 3, 5, 7):
        coarse_sweep(x, put(y), held, keep, spread, -1, lo, 28 - lo, True, COMPS)
        coarse_sweep(y, put(x), held, keep, spread, -1, lo + 1, 27 - lo, False, COMPS)
    split(odd, x, 8, ob, oa, om)


def edge_kernel(odd_ref, base, moved, total, edge):
    odd = odd_ref[0]
    for c in range(3):
        for k in range(4):
            total[c, k] = base[c, k] + moved[c, k]
        for k in range(2):
            edge[c, k] = total[c, odd * 2 + k]


def last_kernel(
    odd_ref, hb, eb, ha, ea, em, source, a1, b1, cond, nu, field, x, y, held, f1, sems,
):
    odd = odd_ref[0]
    kept = copy_all(
        [
            (eb, field.at[0, :, pl.ds(odd * 8, 4)]),
            (ea, field.at[0, :, pl.ds((1 - odd) * 8, 4)]),
            (em, field.at[0, :, pl.ds(4, 4)]),
        ],
        sems,
    )
    extend_force(odd, source, 1, 1, (a1, b1), 6, f1)
    for c in range(3):
        for k in range(4):
            x[c, 4 + odd * 8 + k] = eb[c, k]
            x[c, 4 + (1 - odd) * 8 + k] = ea[c, k]
            x[c, 8 + k] = em[c, k]
        for k in range(2):
            x[c, 2 + odd * 14 + k] = hb[c, k]
            x[c, 2 + (1 - odd) * 14 + k] = ha[c, odd * 2 + k]
    fine_sweep(x, into(y), held, cond, nu, 3, 17, f1, 1)
    fine_sweep(y, into(x), held, cond, nu, 4, 10, None, 1)
    kept += copy_all([(x.at[:, pl.ds(4, 6)], field.at[1, :, pl.ds(0, 6)])], sems, 3)
    fine_sweep(y, into(x), held, cond, nu, 10, 16, None, 1)
    kept += copy_all([(x.at[:, pl.ds(10, 6)], field.at[1, :, pl.ds(6, 6)])], sems, 4)
    wait_all(kept)


def body(guess, source, regions, conductance, reluct):
    slices = lax.axis_size("tm")
    slabs = lax.axis_size("space")
    odd = (lax.axis_index("space") % 2).astype(jnp.int32).reshape(1)
    on_chip = [(i, i ^ 1) for i in range(slabs)]
    off_chip = [(i, i + 1) for i in range(1, slabs - 1, 2)]
    off_chip += [(j, i) for i, j in off_chip]
    fence = lax.optimization_barrier

    def from_a(x):
        return lax.ppermute(x, "space", on_chip)

    def from_b(x):
        return lax.ppermute(x, "space", off_chip)

    half = slices // 2

    def along(x, pairs):
        return lax.ppermute(x, "tm", pairs)

    def later(x, distance):
        return along(x, [(i, (i + distance) % slices) for i in range(slices)])

    def later_parts(x, distance):
        wrapping = [i for i in range(slices) if i % half + distance >= half]
        across = along(x, [(i, (i + half) % slices) for i in wrapping])
        around = along(across, [((i + half) % slices, (i + distance) % slices) for i in wrapping])
        plain = along(x, [(i, i + distance) for i in range(slices) if i not in wrapping])
        return around, plain

    tables = (conductance, reluct)
    sa1, sb1 = call(
        first_pack_kernel, "first_pack",
        (odd, guess[:1, :, :2], guess[:1, :, LX - 2:], source[1:, :, :1], source[1:, :, LX - 1:], regions[:1], regions[LX - 1:]),
        [planes(10), planes(10)], [],
    )
    b1 = from_b(sb1)
    a1 = from_a(sa1)
    um = call(
        first_middle_kernel, "first_middle", (*tables, guess, source, regions),
        planes(3, 4), [vmem(3, LX)] * 2 + [vmem(LX)] * 2,
    )
    sa2, sb2, sa3, sb3 = call(
        second_pack_kernel, "second_pack", (odd, source, regions),
        [planes(12), planes(12), planes(4), planes(4)], [pltpu.VMEM((LX, NY, NZ), jnp.int32)], 8, in_place=HBM,
    )
    vm = later_parts(um, 1)
    sb2, sa2, b1 = fence((sb2, sa2, b1))
    b2 = from_b(sb2)
    a2 = from_a(sa2)
    ua, ub = call(
        first_kernel, "first", (odd, *tables, guess, source, regions, a1, b1, um),
        [planes(3, 4), planes(3, 4)], [vmem(3, LX + 4)] * 4 + [vmem(LX + 4)] * 2,
    )
    vb = later(ub, 1)
    va = later(ua, 1)
    cond, nu, keep, spread = call(
        material_kernel, "material", (odd, *tables, regions, a2, b2), [planes(LX + 6)] * 4, [],
    )
    vb, cond = fence((vb, cond))
    hb = from_b(vb)
    va, *vm = fence((va, *vm))
    ha = from_a(va)
    n = LX + 8
    u0, ua, ub, um = call(
        second_kernel, "second",
        (odd, hb, vb, ha, va, *vm, source, a1, b1, a2, b2, cond, nu),
        [planes(3, LX + 4), planes(3, 4), planes(3, 4), planes(3, 4)], [vmem(3, n)] * 5,
    )
    sb3, sa3, ub = fence((sb3, sa3, ub))
    vb = later(ub, 1)
    va = later(ua, 1)
    around, plain = later_parts(um, 1)
    hb = from_b(vb)
    b3 = from_b(sb3)
    a3 = from_a(sa3)
    wide_keep, wide_spread = call(
        wide_kernel, "wide", (odd, *tables, keep, spread, a3, b3), [planes(LX + 14)] * 2, [],
    )
    va, around, wide_keep = fence((va, around, wide_keep))
    ha = from_a(va)
    residual, lb, la, lm, rb, ra, rm = call(
        residual_kernel, "residual",
        (odd, hb, vb, ha, va, around, plain, source, a2, b2, cond, nu, wide_keep, wide_spread, u0),
        [planes(1, 3, LX)] + [planes(3, 4)] * 6, [vmem(3, n)] * 4, 1, [ANY] + [VMEM] * 6,
    )
    sb = rb + later(lb, 1)
    hb = from_b(sb)
    around, plain = later_parts(lm, 1)
    moved, around = fence((later(la, 1), around))
    sa = ra + moved
    ha = from_a(sa)
    sm = rm + (around + plain)
    lb, la, lm = call(
        square_kernel, "square", (odd, hb, sb, ha, sa, sm, keep, spread),
        [planes(3, 4)] * 3, [vmem(3, n)] * 3,
    )
    tb = sb + later(lb, 2)
    near_b = from_b(tb)
    tm = sm + later(lm, 2)
    far_b = from_b(tm)
    around, plain = later_parts(la, 2)
    ta = sa + (around + plain)
    near_a = from_a(ta)
    far_a = from_a(tm)
    lb, la, lm, bb, ba, bm = call(
        fourth_kernel, "fourth",
        (odd, near_b, tb, far_b, tm, far_a, near_a, ta, u0, wide_keep, wide_spread),
        [planes(3, 4)] * 6, [vmem(3, LX + 16)] * 3,
    )
    eb, edge = call(
        edge_kernel, "edge", (odd, bb, later(lb, half)), [planes(3, 4), planes(3, 2)], [],
    )
    hb = from_b(edge)
    moved, hb = fence((later(la, half), hb))
    ea = ba + moved
    ha = from_a(ea)
    em = bm + later(lm, half)
    field = call(
        last_kernel, "last", (odd, hb, eb, ha, ea, em, source, a1, b1, cond, nu),
        planes(2, 3, LX), [vmem(3, n)] * 4, 5, ANY,
    )
    return field, residual


def solution(mesh):
    whole = P("tm", None, "space", None, None)
    return jax.shard_map(
        body, mesh=mesh, in_specs=(whole, whole, P("space", None, None), P(), P()),
        out_specs=(whole, whole), check_vma=False,
    )
```

```python
import jax
import jax.numpy as jnp
from jax import lax
from jax.experimental import pallas as pl
from jax.experimental.pallas import tpu as pltpu
from jax.sharding import PartitionSpec as P

LX, NY, NZ = 12, 64, 128
ROWS = pl.ds(8, NY)
F32 = jnp.float32
ANY = pl.BlockSpec(memory_space=pl.ANY)
HBM = pl.BlockSpec(memory_space=pltpu.HBM)
VMEM = pl.BlockSpec(memory_space=pltpu.VMEM)
SMEM = pl.BlockSpec(memory_space=pltpu.SMEM)


def planes(*lead):
    return jax.ShapeDtypeStruct(tuple(lead) + (NY, NZ), F32)


def vmem(*lead):
    return pltpu.VMEM(tuple(lead) + (NY, NZ), F32)


def padded(*lead):
    return pltpu.VMEM(tuple(lead) + (NY + 16, NZ), F32)


def clear(*bufs):
    zero = jnp.zeros((8, NZ), F32)

    def body(i, carry):
        for buf in bufs:
            for c in range(3):
                buf[c, i, pl.ds(0, 8)] = zero
                buf[c, i, pl.ds(NY + 8, 8)] = zero
        return carry

    lax.fori_loop(0, bufs[0].shape[1], body, 0)


def copy_all(pairs, sems, base=0):
    copies = [
        pltpu.make_async_copy(src, dst, sems.at[base + n]) for n, (src, dst) in enumerate(pairs)
    ]
    for copy in copies:
        copy.start()
    return copies


def wait_all(copies):
    for copy in copies:
        copy.wait()


def run_copies(pairs, sems, base=0):
    wait_all(copy_all(pairs, sems, base))


def call(kernel, name, args, outs, scratch, n_sems=0, out_specs=None, in_place=VMEM):
    in_specs = [SMEM if a.ndim == 1 else in_place for a in args]
    single = not isinstance(outs, (list, tuple))
    return pl.pallas_call(
        kernel,
        name=name,
        out_shape=outs,
        in_specs=in_specs,
        out_specs=out_specs or (VMEM if single else [VMEM] * len(outs)),
        scratch_shapes=list(scratch) + [pltpu.SemaphoreType.DMA((n_sems,))] * (n_sems > 0),
        compiler_params=pltpu.CompilerParams(vmem_limit_bytes=20 * 1024 * 1024),
        cost_estimate=pl.CostEstimate(flops=0, bytes_accessed=4 << 20, transcendentals=0),
    )(*args)


def over_layers(lo, hi, step, at_once):
    rounds = (hi - lo) // at_once

    def body(t, carry):
        for k in range(at_once):
            step(lo + t * at_once + k)
        return carry

    lax.fori_loop(0, rounds, body, 0)
    for i in range(lo + rounds * at_once, hi):
        step(i)


def neighbours(src, c, i):
    lane = lax.broadcasted_iota(jnp.int32, (NY, NZ), 1)
    zero = jnp.float32(0.0)
    if src.shape[-2] == NY:
        row = lax.broadcasted_iota(jnp.int32, (NY, NZ), 0)
        a = src[c, i]
        first = src[c, i + 1] + src[c, i - 1]
        up = jnp.where(row == 0, zero, pltpu.roll(a, 1, 0))
        down = jnp.where(row == NY - 1, zero, pltpu.roll(a, NY - 1, 0))
    else:
        a = src[c, i, ROWS]
        first = src[c, i + 1, ROWS] + src[c, i - 1, ROWS]
        up = src[c, i, pl.ds(7, NY)]
        down = src[c, i, pl.ds(9, NY)]
    left = jnp.where(lane == 0, zero, pltpu.roll(a, 1, 1))
    right = jnp.where(lane == NZ - 1, zero, pltpu.roll(a, NZ - 1, 1))
    return (first + (up + down)) + (left + right)


def layer(src, c, i):
    return src[c, i] if src.shape[-2] == NY else src[c, i, ROWS]


def fine_sweep(src, store, held, cond, nu, lo, hi, force=None, off=0):
    def step(i):
        state = [layer(src, c, i) for c in range(3)]
        square = state[0] * state[0] + state[1] * state[1] + state[2] * state[2]
        base = nu[i - off]
        weight = cond[i - off]
        grown = 1.0 + square
        strong = base * (1.0 + 1.5 * square)
        scale = 1.0 / (weight * grown + 6.0 * strong)
        keep = grown * scale
        spread = strong * scale
        for c in range(3):
            if force is not None:
                fixed = weight * state[c] + force[c, i]
                held[c, i] = fixed
            else:
                fixed = held[c, i]
            store(c, i, fixed * keep + neighbours(src, c, i) * spread)

    over_layers(lo, hi, step, 6)


def coarse_sweep(src, dst, held, keep, spread, off, lo, hi, first):
    def step(i):
        k = keep[i + off]
        s = spread[i + off]
        for c in range(3):
            if first:
                fixed = k * src[c, i, ROWS]
                held[c, i] = fixed
            else:
                fixed = held[c, i]
            dst[c, i, ROWS] = fixed + s * neighbours(src, c, i)

    over_layers(lo, hi, step, 6)


def lookup(code, table):
    first = jnp.where(code == 1, table[0], table[1])
    second = jnp.where(code == 3, table[2], table[3])
    return jnp.where(code <= 2, first, second)


def materials(code, cond_t, nu_t):
    outside = code == 0
    return (
        jnp.where(outside, jnp.float32(1.0), lookup(code, cond_t)),
        jnp.where(outside, jnp.float32(0.0), lookup(code, nu_t)),
    )


def into(buf):
    def store(c, i, value):
        buf[c, i, ROWS] = value
    return store


def edges(odd, n, width):
    return (1 - odd) * (n - width), odd * (n - width)


def first_pack_kernel(odd_ref, g_low, g_high, s_low, s_high, r_low, r_high, a1, b1):
    odd = odd_ref[0]

    def fill(low, high):
        for c in range(3):
            for k in range(2):
                low[2 * c + k] = g_low[0, c, k]
                high[2 * c + k] = g_high[0, c, k]
            low[6 + c] = s_low[0, c, 0]
            high[6 + c] = s_high[0, c, 0]
        low[9] = (r_low[0] + 1).astype(F32)
        high[9] = (r_high[0] + 1).astype(F32)

    @pl.when(odd == 0)
    def even_slab():
        fill(b1, a1)

    @pl.when(odd == 1)
    def odd_slab():
        fill(a1, b1)


def second_pack_kernel(odd_ref, source, regions, a2, b2):
    odd = odd_ref[0]
    for two, start in zip((a2, b2), edges(odd, LX, 3)):
        for c in range(3):
            for k in range(3):
                two[3 * c + k] = source[0, c, start + k]
    for two, start in zip((a2, b2), edges(odd, LX, 7)):
        for k in range(7):
            two[9 + k] = (regions[start + k] + 1).astype(F32)


def first_middle_kernel(cond_t, nu_t, guess, source, regions, after, out, y, held, cond, nu):
    def prepare(i):
        cond[i], nu[i] = materials(regions[i] + 1, cond_t, nu_t)

    over_layers(3, 9, prepare, 6)
    clear(y)
    fine_sweep(guess.at[0], into(y), held, cond, nu, 3, 9, source.at[1])

    def store(c, i, value):
        out[c, i - 4] = value

    fine_sweep(y, store, held, cond, nu, 4, 8)


def first_kernel(odd_ref, cond_t, nu_t, guess, source, regions, ra, rb, after, out_a, out_b, x, y, held, f, cond, nu):
    odd = odd_ref[0]
    clear(x, y)
    n = LX + 4
    for c in range(3):
        for i in (0, 1, 2, 3, 4, 5, 6, 7, 8, 9, 10, 11):
            x[c, i + 2, ROWS] = guess[0, c, i]
            f[c, i + 2] = source[1, c, i]
    for i in range(LX):
        cond[i + 2], nu[i + 2] = materials(regions[i] + 1, cond_t, nu_t)
    for pack, high in ((ra, 1 - odd), (rb, odd)):
        for c in range(3):
            for k in range(2):
                x[c, high * (n - 2) + k, ROWS] = pack[2 * c + k]
            f[c, 1 + high * (n - 3)] = pack[6 + c]
        cond[1 + high * (n - 3)], nu[1 + high * (n - 3)] = materials(pack[9], cond_t, nu_t)
    fine_sweep(x, into(y), held, cond, nu, 1, 7, f)
    fine_sweep(x, into(y), held, cond, nu, 9, n - 1, f)
    fine_sweep(y, into(x), held, cond, nu, 2, 6)
    fine_sweep(y, into(x), held, cond, nu, 10, 14)
    for c in range(3):
        for k in range(4):
            out_a[c, k] = x[c, 2 + (1 - odd) * 8 + k, ROWS]
            out_b[c, k] = x[c, 2 + odd * 8 + k, ROWS]


def material_kernel(odd_ref, cond_t, nu_t, regions, ra, rb, cond, nu, keep, spread):
    odd = odd_ref[0]

    def fill(at, code, near=True):
        cv, nv = materials(code, cond_t, nu_t)
        if near:
            cond[at - 4] = cv
            nu[at - 4] = nv
        half = 0.5 * cv
        scale = 1.0 / (half + 6.0 * nv)
        keep[at] = half * scale
        spread[at] = nv * scale

    for i in range(LX):
        fill(7 + i, regions[i] + 1)
    for k in range(7):
        from_on, from_off = ra[9 + k], rb[9 + k]
        fill(k, jnp.where(odd == 1, from_on, from_off), k >= 4)
        fill(LX + 7 + k, jnp.where(odd == 1, from_off, from_on), k < 3)


def extend(odd, pieces, halos, x):
    a, b, *m = pieces
    ha, hb = halos
    for c in range(3):
        for k in range(4):
            middle = m[0][c, k]
            for other in m[1:]:
                middle = middle + other[c, k]
            x[c, 8 + k, ROWS] = middle
            x[c, 4 + (1 - odd) * 8 + k, ROWS] = a[c, k]
            x[c, 4 + odd * 8 + k, ROWS] = b[c, k]
            x[c, (1 - odd) * 16 + k, ROWS] = ha[c, k]
            x[c, odd * 16 + k, ROWS] = hb[c, k]


def extend_force(odd, source, which, width, packs, start, f):
    for c in range(3):
        for i in range(LX):
            f[c, 4 + i] = source[which, c, i]
        for pack, high in ((packs[0], 1 - odd), (packs[1], odd)):
            for k in range(width):
                f[c, 4 - width + high * (LX + width) + k] = pack[start + width * c + k]


def second_kernel(
    odd_ref, hb, vb, ha, va, vm, source, a1, b1, a2, b2, cond, nu,
    u0, oa, ob, om, x, y, held, f0, f1,
):
    odd = odd_ref[0]
    clear(x, y)
    extend(odd, (va, vb, vm), (ha, hb), x)
    extend_force(odd, source, 0, 3, (a2, b2), 0, f0)
    extend_force(odd, source, 1, 1, (a1, b1), 6, f1)

    def keep_u0(c, i, value):
        x[c, i, ROWS] = value
        u0[c, i - 2] = value

    fine_sweep(x, into(y), held, cond, nu, 1, 19, f0, 1)
    fine_sweep(y, keep_u0, held, cond, nu, 2, 18, None, 1)
    fine_sweep(x, into(y), held, cond, nu, 3, 17, f1, 1)
    fine_sweep(y, into(x), held, cond, nu, 4, 16, None, 1)
    for c in range(3):
        for k in range(4):
            om[c, k] = x[c, 8 + k, ROWS]
            oa[c, k] = x[c, 4 + (1 - odd) * 8 + k, ROWS]
            ob[c, k] = x[c, 4 + odd * 8 + k, ROWS]


def split(odd, x, start, b, a, m):
    for c in range(3):
        for k in range(4):
            b[c, k] = x[c, start + odd * 8 + k, ROWS]
            a[c, k] = x[c, start + (1 - odd) * 8 + k, ROWS]
            m[c, k] = x[c, start + 4 + k, ROWS]


def residual_kernel(
    odd_ref, hb, vb, ha, va, vm, vn, source, a2, b2, cond, nu, keep, spread, u0,
    res_o, lb, la, lm, rb, ra, rm, x, y, held, f0, sems,
):
    odd = odd_ref[0]
    clear(x, y)
    extend(odd, (va, vb, vm, vn), (ha, hb), x)
    extend_force(odd, source, 0, 3, (a2, b2), 0, f0)

    def less(c, i, value):
        x[c, i, ROWS] = value - u0[c, i - 2]

    fine_sweep(x, into(y), held, cond, nu, 1, 19, f0, 1)
    fine_sweep(y, less, held, cond, nu, 2, 18, None, 1)
    kept = copy_all([(x.at[:, pl.ds(4, LX), ROWS], res_o.at[0])], sems)
    split(odd, x, 4, rb, ra, rm)
    coarse_sweep(x, y, held, keep, spread, 3, 3, 17, True)
    wait_all(kept)
    coarse_sweep(y, x, held, keep, spread, 3, 4, 16, False)
    split(odd, x, 4, lb, la, lm)


def square_kernel(odd_ref, hb, sb, ha, sa, sm, keep, spread, ob, oa, om, x, y, held):
    odd = odd_ref[0]
    clear(x, y)
    extend(odd, (sa, sb, sm), (ha, hb), x)
    for lo in (1, 3):
        coarse_sweep(x, y, held, keep, spread, 3, lo, 20 - lo, True)
        coarse_sweep(y, x, held, keep, spread, 3, lo + 1, 19 - lo, False)
    split(odd, x, 4, ob, oa, om)


def fourth_kernel(
    odd_ref, near_b, tb, far_b, tm, far_a, near_a, ta, u0, keep, spread,
    ob, oa, om, bb, ba, bm, x, y, held,
):
    odd = odd_ref[0]
    clear(x, y)
    for c in range(3):
        for k in range(4):
            x[c, 8 + odd * 8 + k, ROWS] = tb[c, k]
            x[c, 8 + (1 - odd) * 8 + k, ROWS] = ta[c, k]
            x[c, 12 + k, ROWS] = tm[c, k]
            x[c, 4 + odd * 16 + k, ROWS] = near_b[c, k]
            x[c, 4 + (1 - odd) * 16 + k, ROWS] = near_a[c, k]
            x[c, odd * 24 + k, ROWS] = far_b[c, k]
            x[c, (1 - odd) * 24 + k, ROWS] = far_a[c, k]
    for c in range(3):
        for k in range(4):
            bb[c, k] = tb[c, k] + u0[c, 2 + odd * 8 + k]
            ba[c, k] = ta[c, k] + u0[c, 2 + (1 - odd) * 8 + k]
            bm[c, k] = tm[c, k] + u0[c, 6 + k]
    for lo in (1, 3, 5, 7):
        coarse_sweep(x, y, held, keep, spread, -1, lo, 28 - lo, True)
        coarse_sweep(y, x, held, keep, spread, -1, lo + 1, 27 - lo, False)
    split(odd, x, 8, ob, oa, om)


def edge_kernel(odd_ref, base, moved, total, edge):
    odd = odd_ref[0]
    for c in range(3):
        for k in range(4):
            total[c, k] = base[c, k] + moved[c, k]
        for k in range(2):
            edge[c, k] = total[c, odd * 2 + k]


def last_kernel(
    odd_ref, hb, eb, ha, ea, em, source, a1, b1, cond, nu, field, x, y, held, f1, sems,
):
    odd = odd_ref[0]
    clear(x, y)
    kept = copy_all(
        [
            (eb, field.at[0, :, pl.ds(odd * 8, 4)]),
            (ea, field.at[0, :, pl.ds((1 - odd) * 8, 4)]),
            (em, field.at[0, :, pl.ds(4, 4)]),
        ],
        sems,
    )
    extend_force(odd, source, 1, 1, (a1, b1), 6, f1)
    for c in range(3):
        for k in range(4):
            x[c, 4 + odd * 8 + k, ROWS] = eb[c, k]
            x[c, 4 + (1 - odd) * 8 + k, ROWS] = ea[c, k]
            x[c, 8 + k, ROWS] = em[c, k]
        for k in range(2):
            x[c, 2 + odd * 14 + k, ROWS] = hb[c, k]
            x[c, 2 + (1 - odd) * 14 + k, ROWS] = ha[c, odd * 2 + k]
    fine_sweep(x, into(y), held, cond, nu, 3, 17, f1, 1)
    fine_sweep(y, into(x), held, cond, nu, 4, 10, None, 1)
    kept += copy_all([(x.at[:, pl.ds(4, 6), ROWS], field.at[1, :, pl.ds(0, 6)])], sems, 3)
    fine_sweep(y, into(x), held, cond, nu, 10, 16, None, 1)
    kept += copy_all([(x.at[:, pl.ds(10, 6), ROWS], field.at[1, :, pl.ds(6, 6)])], sems, 4)
    wait_all(kept)


def body(guess, source, regions, conductance, reluct):
    slices = lax.axis_size("tm")
    slabs = lax.axis_size("space")
    odd = (lax.axis_index("space") % 2).astype(jnp.int32).reshape(1)
    on_chip = [(i, i ^ 1) for i in range(slabs)]
    off_chip = [(i, i + 1) for i in range(1, slabs - 1, 2)]
    off_chip += [(j, i) for i, j in off_chip]
    fence = lax.optimization_barrier

    def from_a(x):
        return lax.ppermute(x, "space", on_chip)

    def from_b(x):
        return lax.ppermute(x, "space", off_chip)

    half = slices // 2

    def along(x, pairs):
        return lax.ppermute(x, "tm", pairs)

    def later(x, distance):
        return along(x, [(i, (i + distance) % slices) for i in range(slices)])

    def later_parts(x, distance):
        wrapping = [i for i in range(slices) if i % half + distance >= half]
        across = along(x, [(i, (i + half) % slices) for i in wrapping])
        around = along(across, [((i + half) % slices, (i + distance) % slices) for i in wrapping])
        plain = along(x, [(i, i + distance) for i in range(slices) if i not in wrapping])
        return around, plain

    tables = (conductance, reluct)
    sa1, sb1 = call(
        first_pack_kernel, "first_pack",
        (odd, guess[:1, :, :2], guess[:1, :, LX - 2:], source[1:, :, :1], source[1:, :, LX - 1:], regions[:1], regions[LX - 1:]),
        [planes(10), planes(10)], [],
    )
    b1 = from_b(sb1)
    a1 = from_a(sa1)
    um = call(
        first_middle_kernel, "first_middle", (*tables, guess, source, regions, sb1),
        planes(3, 4), [padded(3, LX), vmem(3, LX)] + [vmem(LX)] * 2,
    )
    sa2, sb2 = call(
        second_pack_kernel, "second_pack", (odd, source, regions), [planes(16), planes(16)], [],
    )
    vm = later(um, 1)
    sb2, sa2, b1 = fence((sb2, sa2, b1))
    b2 = from_b(sb2)
    a2 = from_a(sa2)
    ua, ub = call(
        first_kernel, "first", (odd, *tables, guess, source, regions, a1, b1, um),
        [planes(3, 4), planes(3, 4)], [padded(3, LX + 4)] * 2 + [vmem(3, LX + 4)] * 2 + [vmem(LX + 4)] * 2,
    )
    ub, vm = fence((ub, vm))
    vb = later(ub, 1)
    around, plain = later_parts(ua, 1)
    va = around + plain
    cond, nu, keep, spread = call(
        material_kernel, "material", (odd, *tables, regions, a2, b2),
        [planes(LX + 6)] * 2 + [planes(LX + 14)] * 2, [],
    )
    vb, cond = fence((vb, cond))
    hb = from_b(vb)
    ha = from_a(va)
    n = LX + 8
    u0, ua, ub, um = call(
        second_kernel, "second",
        (odd, hb, vb, ha, va, vm, source, a1, b1, a2, b2, cond, nu),
        [planes(3, LX + 4), planes(3, 4), planes(3, 4), planes(3, 4)], [padded(3, n)] * 2 + [vmem(3, n)] * 3,
    )
    vb = later(ub, 1)
    va = later(ua, 1)
    around, plain = later_parts(um, 1)
    hb = from_b(vb)
    va, around = fence((va, around))
    ha = from_a(va)
    residual, lb, la, lm, rb, ra, rm = call(
        residual_kernel, "residual",
        (odd, hb, vb, ha, va, around, plain, source, a2, b2, cond, nu, keep, spread, u0),
        [planes(1, 3, LX)] + [planes(3, 4)] * 6, [padded(3, n)] * 2 + [vmem(3, n)] * 2, 1, [ANY] + [VMEM] * 6,
    )
    sb = rb + later(lb, 1)
    hb = from_b(sb)
    around, plain = later_parts(lm, 1)
    moved, around = fence((later(la, 1), around))
    sa = ra + moved
    ha = from_a(sa)
    sm = rm + (around + plain)
    lb, la, lm = call(
        square_kernel, "square", (odd, hb, sb, ha, sa, sm, keep, spread),
        [planes(3, 4)] * 3, [padded(3, n)] * 2 + [vmem(3, n)],
    )
    tb = sb + later(lb, 2)
    near_b = from_b(tb)
    tm = sm + later(lm, 2)
    far_b = from_b(tm)
    around, plain = later_parts(la, 2)
    ta = sa + (around + plain)
    near_a = from_a(ta)
    far_a = from_a(tm)
    lb, la, lm, bb, ba, bm = call(
        fourth_kernel, "fourth",
        (odd, near_b, tb, far_b, tm, far_a, near_a, ta, u0, keep, spread),
        [planes(3, 4)] * 6, [padded(3, LX + 16)] * 2 + [vmem(3, LX + 16)],
    )
    eb, edge = call(
        edge_kernel, "edge", (odd, bb, later(lb, half)), [planes(3, 4), planes(3, 2)], [],
    )
    hb = from_b(edge)
    moved, hb = fence((later(la, half), hb))
    ea = ba + moved
    ha = from_a(ea)
    em = bm + later(lm, half)
    field = call(
        last_kernel, "last", (odd, hb, eb, ha, ea, em, source, a1, b1, cond, nu),
        planes(2, 3, LX), [padded(3, n)] * 2 + [vmem(3, n)] * 2, 5, ANY,
    )
    return field, residual


def solution(mesh):
    whole = P("tm", None, "space", None, None)
    return jax.shard_map(
        body, mesh=mesh, in_specs=(whole, whole, P("space", None, None), P(), P()),
        out_specs=(whole, whole), check_vma=False,
    )
```

```python
import jax
import jax.numpy as jnp
from jax import lax
from jax.experimental import pallas as pl
from jax.experimental.pallas import tpu as pltpu
from jax.sharding import PartitionSpec as P

LX, NY, NZ = 12, 64, 128
ROWS = pl.ds(8, NY)
F32 = jnp.float32
ANY = pl.BlockSpec(memory_space=pl.ANY)
HBM = pl.BlockSpec(memory_space=pltpu.HBM)
VMEM = pl.BlockSpec(memory_space=pltpu.VMEM)
SMEM = pl.BlockSpec(memory_space=pltpu.SMEM)


def planes(*lead):
    return jax.ShapeDtypeStruct(tuple(lead) + (NY, NZ), F32)


def vmem(*lead):
    return pltpu.VMEM(tuple(lead) + (NY, NZ), F32)


def padded(*lead):
    return pltpu.VMEM(tuple(lead) + (NY + 16, NZ), F32)


def clear(*bufs):
    zero = jnp.zeros((8, NZ), F32)

    def body(i, carry):
        for buf in bufs:
            for c in range(3):
                buf[c, i, pl.ds(0, 8)] = zero
                buf[c, i, pl.ds(NY + 8, 8)] = zero
        return carry

    lax.fori_loop(0, bufs[0].shape[1], body, 0)


def copy_all(pairs, sems, base=0):
    copies = [
        pltpu.make_async_copy(src, dst, sems.at[base + n]) for n, (src, dst) in enumerate(pairs)
    ]
    for copy in copies:
        copy.start()
    return copies


def wait_all(copies):
    for copy in copies:
        copy.wait()


def run_copies(pairs, sems, base=0):
    wait_all(copy_all(pairs, sems, base))


def call(kernel, name, args, outs, scratch, n_sems=0, out_specs=None, in_place=VMEM):
    in_specs = [SMEM if a.ndim == 1 else in_place for a in args]
    single = not isinstance(outs, (list, tuple))
    return pl.pallas_call(
        kernel,
        name=name,
        out_shape=outs,
        in_specs=in_specs,
        out_specs=out_specs or (VMEM if single else [VMEM] * len(outs)),
        scratch_shapes=list(scratch) + [pltpu.SemaphoreType.DMA((n_sems,))] * (n_sems > 0),
        compiler_params=pltpu.CompilerParams(vmem_limit_bytes=20 * 1024 * 1024),
        cost_estimate=pl.CostEstimate(flops=0, bytes_accessed=4 << 20, transcendentals=0),
    )(*args)


def over_layers(lo, hi, step, at_once):
    rounds = (hi - lo) // at_once

    def body(t, carry):
        for k in range(at_once):
            step(lo + t * at_once + k)
        return carry

    lax.fori_loop(0, rounds, body, 0)
    for i in range(lo + rounds * at_once, hi):
        step(i)


def neighbours(src, c, i):
    lane = lax.broadcasted_iota(jnp.int32, (NY, NZ), 1)
    zero = jnp.float32(0.0)
    if src.shape[-2] == NY:
        row = lax.broadcasted_iota(jnp.int32, (NY, NZ), 0)
        a = src[c, i]
        first = src[c, i + 1] + src[c, i - 1]
        up = jnp.where(row == 0, zero, pltpu.roll(a, 1, 0))
        down = jnp.where(row == NY - 1, zero, pltpu.roll(a, NY - 1, 0))
    else:
        a = src[c, i, ROWS]
        first = src[c, i + 1, ROWS] + src[c, i - 1, ROWS]
        up = src[c, i, pl.ds(7, NY)]
        down = src[c, i, pl.ds(9, NY)]
    left = jnp.where(lane == 0, zero, pltpu.roll(a, 1, 1))
    right = jnp.where(lane == NZ - 1, zero, pltpu.roll(a, NZ - 1, 1))
    return (first + (up + down)) + (left + right)


def layer(src, c, i):
    return src[c, i] if src.shape[-2] == NY else src[c, i, ROWS]


def fine_sweep(src, store, held, cond, nu, lo, hi, force=None, off=0):
    def step(i):
        state = [layer(src, c, i) for c in range(3)]
        square = state[0] * state[0] + state[1] * state[1] + state[2] * state[2]
        base = nu[i - off]
        weight = cond[i - off]
        grown = 1.0 + square
        strong = base * (1.0 + 1.5 * square)
        scale = 1.0 / (weight * grown + 6.0 * strong)
        keep = grown * scale
        spread = strong * scale
        for c in range(3):
            if force is not None:
                fixed = weight * state[c] + force[c, i]
                held[c, i] = fixed
            else:
                fixed = held[c, i]
            store(c, i, fixed * keep + neighbours(src, c, i) * spread)

    over_layers(lo, hi, step, 6)


def coarse_sweep(src, dst, held, keep, spread, off, lo, hi, first):
    def step(i):
        k = keep[i + off]
        s = spread[i + off]
        for c in range(3):
            if first:
                fixed = k * src[c, i, ROWS]
                held[c, i] = fixed
            else:
                fixed = held[c, i]
            dst[c, i, ROWS] = fixed + s * neighbours(src, c, i)

    over_layers(lo, hi, step, 6)


def lookup(code, table):
    first = jnp.where(code == 1, table[0], table[1])
    second = jnp.where(code == 3, table[2], table[3])
    return jnp.where(code <= 2, first, second)


def materials(code, cond_t, nu_t):
    outside = code == 0
    return (
        jnp.where(outside, jnp.float32(1.0), lookup(code, cond_t)),
        jnp.where(outside, jnp.float32(0.0), lookup(code, nu_t)),
    )


def into(buf):
    def store(c, i, value):
        buf[c, i, ROWS] = value
    return store


def edges(odd, n, width):
    return (1 - odd) * (n - width), odd * (n - width)


def pack_kernel(odd_ref, g_low, g_high, s_low, s_high, t_low, t_high, r_low, r_high, a1, b1):
    odd = odd_ref[0]

    def fill(low, high):
        for out, g, s, t, r in ((low, g_low, s_low, t_low, r_low), (high, g_high, s_high, t_high, r_high)):
            for c in range(3):
                for k in range(2):
                    out[2 * c + k] = g[0, c, k]
                out[6 + c] = s[0, c, 0]
                for k in range(3):
                    out[9 + 3 * c + k] = t[0, c, k]
            for k in range(7):
                out[18 + k] = (r[k] + 1).astype(F32)

    @pl.when(odd == 0)
    def even_slab():
        fill(b1, a1)

    @pl.when(odd == 1)
    def odd_slab():
        fill(a1, b1)


def first_middle_kernel(cond_t, nu_t, guess, source, regions, after, out, y, held, cond, nu):
    def prepare(i):
        cond[i], nu[i] = materials(regions[i] + 1, cond_t, nu_t)

    over_layers(3, 9, prepare, 6)
    clear(y)
    fine_sweep(guess.at[0], into(y), held, cond, nu, 3, 9, source.at[1])

    def store(c, i, value):
        out[c, i - 4] = value

    fine_sweep(y, store, held, cond, nu, 4, 8)


def first_kernel(odd_ref, cond_t, nu_t, guess, source, regions, ra, rb, after, out_a, out_b, x, y, held, f, cond, nu):
    odd = odd_ref[0]
    clear(x, y)
    n = LX + 4
    for c in range(3):
        for i in (0, 1, 2, 3, 4, 5, 6, 7, 8, 9, 10, 11):
            x[c, i + 2, ROWS] = guess[0, c, i]
            f[c, i + 2] = source[1, c, i]
    for i in range(LX):
        cond[i + 2], nu[i + 2] = materials(regions[i] + 1, cond_t, nu_t)
    for pack, high in ((ra, 1 - odd), (rb, odd)):
        for c in range(3):
            for k in range(2):
                x[c, high * (n - 2) + k, ROWS] = pack[2 * c + k]
            f[c, 1 + high * (n - 3)] = pack[6 + c]
        cond[1 + high * (n - 3)], nu[1 + high * (n - 3)] = materials(pack[24 - 6 * high], cond_t, nu_t)
    fine_sweep(x, into(y), held, cond, nu, 1, 7, f)
    fine_sweep(x, into(y), held, cond, nu, 9, n - 1, f)
    fine_sweep(y, into(x), held, cond, nu, 2, 6)
    fine_sweep(y, into(x), held, cond, nu, 10, 14)
    for c in range(3):
        for k in range(4):
            out_a[c, k] = x[c, 2 + (1 - odd) * 8 + k, ROWS]
            out_b[c, k] = x[c, 2 + odd * 8 + k, ROWS]


def material_kernel(odd_ref, cond_t, nu_t, regions, ra, rb, cond, nu, keep, spread):
    odd = odd_ref[0]

    def fill(at, code, near=True):
        cv, nv = materials(code, cond_t, nu_t)
        if near:
            cond[at - 4] = cv
            nu[at - 4] = nv
        half = 0.5 * cv
        scale = 1.0 / (half + 6.0 * nv)
        keep[at] = half * scale
        spread[at] = nv * scale

    for i in range(LX):
        fill(7 + i, regions[i] + 1)
    for k in range(7):
        from_on, from_off = ra[18 + k], rb[18 + k]
        fill(k, jnp.where(odd == 1, from_on, from_off), k >= 4)
        fill(LX + 7 + k, jnp.where(odd == 1, from_off, from_on), k < 3)


def extend(odd, pieces, halos, x):
    a, b, *m = pieces
    ha, hb = halos
    for c in range(3):
        for k in range(4):
            middle = m[0][c, k]
            for other in m[1:]:
                middle = middle + other[c, k]
            x[c, 8 + k, ROWS] = middle
            x[c, 4 + (1 - odd) * 8 + k, ROWS] = a[c, k]
            x[c, 4 + odd * 8 + k, ROWS] = b[c, k]
            x[c, (1 - odd) * 16 + k, ROWS] = ha[c, k]
            x[c, odd * 16 + k, ROWS] = hb[c, k]


def extend_force(odd, source, which, width, packs, start, f):
    for c in range(3):
        for i in range(LX):
            f[c, 4 + i] = source[which, c, i]
        for pack, high in ((packs[0], 1 - odd), (packs[1], odd)):
            for k in range(width):
                f[c, 4 - width + high * (LX + width) + k] = pack[start + width * c + k]


def second_kernel(
    odd_ref, hb, vb, ha, va, vm, vn, source, a1, b1, cond, nu,
    u0, oa, ob, om, x, y, held, f0, f1,
):
    odd = odd_ref[0]
    clear(x, y)
    extend(odd, (va, vb, vm, vn), (ha, hb), x)
    extend_force(odd, source, 0, 3, (a1, b1), 9, f0)
    extend_force(odd, source, 1, 1, (a1, b1), 6, f1)

    def keep_u0(c, i, value):
        x[c, i, ROWS] = value
        u0[c, i - 2] = value

    fine_sweep(x, into(y), held, cond, nu, 1, 19, f0, 1)
    fine_sweep(y, keep_u0, held, cond, nu, 2, 18, None, 1)
    fine_sweep(x, into(y), held, cond, nu, 3, 17, f1, 1)
    fine_sweep(y, into(x), held, cond, nu, 4, 16, None, 1)
    for c in range(3):
        for k in range(4):
            om[c, k] = x[c, 8 + k, ROWS]
            oa[c, k] = x[c, 4 + (1 - odd) * 8 + k, ROWS]
            ob[c, k] = x[c, 4 + odd * 8 + k, ROWS]


def split(odd, x, start, b, a, m):
    for c in range(3):
        for k in range(4):
            b[c, k] = x[c, start + odd * 8 + k, ROWS]
            a[c, k] = x[c, start + (1 - odd) * 8 + k, ROWS]
            m[c, k] = x[c, start + 4 + k, ROWS]


def residual_kernel(
    odd_ref, hb, vb, ha, va, vm, vn, source, a1, b1, cond, nu, keep, spread, u0,
    res_o, lb, la, lm, rb, ra, rm, x, y, held, f0, sems,
):
    odd = odd_ref[0]
    clear(x, y)
    extend(odd, (va, vb, vm, vn), (ha, hb), x)
    extend_force(odd, source, 0, 3, (a1, b1), 9, f0)

    def less(c, i, value):
        x[c, i, ROWS] = value - u0[c, i - 2]

    fine_sweep(x, into(y), held, cond, nu, 1, 19, f0, 1)
    fine_sweep(y, less, held, cond, nu, 2, 18, None, 1)
    kept = copy_all([(x.at[:, pl.ds(4, LX), ROWS], res_o.at[0])], sems)
    split(odd, x, 4, rb, ra, rm)
    coarse_sweep(x, y, held, keep, spread, 3, 3, 17, True)
    wait_all(kept)
    coarse_sweep(y, x, held, keep, spread, 3, 4, 16, False)
    split(odd, x, 4, lb, la, lm)


def square_kernel(odd_ref, hb, sb, ha, sa, sm, keep, spread, ob, oa, om, x, y, held):
    odd = odd_ref[0]
    clear(x, y)
    extend(odd, (sa, sb, sm), (ha, hb), x)
    for lo in (1, 3):
        coarse_sweep(x, y, held, keep, spread, 3, lo, 20 - lo, True)
        coarse_sweep(y, x, held, keep, spread, 3, lo + 1, 19 - lo, False)
    split(odd, x, 4, ob, oa, om)


def fourth_kernel(
    odd_ref, near_b, tb, far_b, tm, far_a, near_a, ta, u0, keep, spread,
    ob, oa, om, bb, ba, bm, x, y, held,
):
    odd = odd_ref[0]
    clear(x, y)
    for c in range(3):
        for k in range(4):
            x[c, 8 + odd * 8 + k, ROWS] = tb[c, k]
            x[c, 8 + (1 - odd) * 8 + k, ROWS] = ta[c, k]
            x[c, 12 + k, ROWS] = tm[c, k]
            x[c, 4 + odd * 16 + k, ROWS] = near_b[c, k]
            x[c, 4 + (1 - odd) * 16 + k, ROWS] = near_a[c, k]
            x[c, odd * 24 + k, ROWS] = far_b[c, k]
            x[c, (1 - odd) * 24 + k, ROWS] = far_a[c, k]
    for c in range(3):
        for k in range(4):
            bb[c, k] = tb[c, k] + u0[c, 2 + odd * 8 + k]
            ba[c, k] = ta[c, k] + u0[c, 2 + (1 - odd) * 8 + k]
            bm[c, k] = tm[c, k] + u0[c, 6 + k]
    for lo in (1, 3, 5, 7):
        coarse_sweep(x, y, held, keep, spread, -1, lo, 28 - lo, True)
        coarse_sweep(y, x, held, keep, spread, -1, lo + 1, 27 - lo, False)
    split(odd, x, 8, ob, oa, om)


def edge_kernel(odd_ref, base, moved, total, edge):
    odd = odd_ref[0]
    for c in range(3):
        for k in range(4):
            total[c, k] = base[c, k] + moved[c, k]
        for k in range(2):
            edge[c, k] = total[c, odd * 2 + k]


def last_kernel(
    odd_ref, hb, eb, ha, ea, em, source, a1, b1, cond, nu, field, x, y, held, f1, sems,
):
    odd = odd_ref[0]
    clear(x, y)
    kept = copy_all(
        [
            (eb, field.at[0, :, pl.ds(odd * 8, 4)]),
            (ea, field.at[0, :, pl.ds((1 - odd) * 8, 4)]),
            (em, field.at[0, :, pl.ds(4, 4)]),
        ],
        sems,
    )
    extend_force(odd, source, 1, 1, (a1, b1), 6, f1)
    for c in range(3):
        for k in range(4):
            x[c, 4 + odd * 8 + k, ROWS] = eb[c, k]
            x[c, 4 + (1 - odd) * 8 + k, ROWS] = ea[c, k]
            x[c, 8 + k, ROWS] = em[c, k]
        for k in range(2):
            x[c, 2 + odd * 14 + k, ROWS] = hb[c, k]
            x[c, 2 + (1 - odd) * 14 + k, ROWS] = ha[c, odd * 2 + k]
    fine_sweep(x, into(y), held, cond, nu, 3, 17, f1, 1)
    fine_sweep(y, into(x), held, cond, nu, 4, 10, None, 1)
    kept += copy_all([(x.at[:, pl.ds(4, 6), ROWS], field.at[1, :, pl.ds(0, 6)])], sems, 3)
    fine_sweep(y, into(x), held, cond, nu, 10, 16, None, 1)
    kept += copy_all([(x.at[:, pl.ds(10, 6), ROWS], field.at[1, :, pl.ds(6, 6)])], sems, 4)
    wait_all(kept)


def body(guess, source, regions, conductance, reluct):
    slices = lax.axis_size("tm")
    slabs = lax.axis_size("space")
    odd = (lax.axis_index("space") % 2).astype(jnp.int32).reshape(1)
    on_chip = [(i, i ^ 1) for i in range(slabs)]
    off_chip = [(i, i + 1) for i in range(1, slabs - 1, 2)]
    off_chip += [(j, i) for i, j in off_chip]
    fence = lax.optimization_barrier

    def from_a(x):
        return lax.ppermute(x, "space", on_chip)

    def from_b(x):
        return lax.ppermute(x, "space", off_chip)

    half = slices // 2

    def along(x, pairs):
        return lax.ppermute(x, "tm", pairs)

    def later(x, distance):
        return along(x, [(i, (i + distance) % slices) for i in range(slices)])

    def later_parts(x, distance):
        wrapping = [i for i in range(slices) if i % half + distance >= half]
        across = along(x, [(i, (i + half) % slices) for i in wrapping])
        around = along(across, [((i + half) % slices, (i + distance) % slices) for i in wrapping])
        plain = along(x, [(i, i + distance) for i in range(slices) if i not in wrapping])
        return around, plain

    def later_wrapped(x, distance):
        return later_parts(x, distance)[0]

    inside = [(i, i + 1) for i in range(slices - 1) if i % half < half - 1]

    tables = (conductance, reluct)
    sa1, sb1 = call(
        pack_kernel, "pack",
        (
            odd, guess[:1, :, :2], guess[:1, :, LX - 2:], source[1:, :, :1], source[1:, :, LX - 1:],
            source[:1, :, :3], source[:1, :, LX - 3:], regions[:7], regions[LX - 7:],
        ),
        [planes(25), planes(25)], [],
    )
    b1 = from_b(sb1)
    a1 = from_a(sa1)
    um = call(
        first_middle_kernel, "first_middle", (*tables, guess, source, regions, sb1),
        planes(3, 4), [padded(3, LX), vmem(3, LX)] + [vmem(LX)] * 2,
    )
    plain = along(um, inside)
    ua, ub = call(
        first_kernel, "first", (odd, *tables, guess, source, regions, a1, b1, um),
        [planes(3, 4), planes(3, 4)], [padded(3, LX + 4)] * 2 + [vmem(3, LX + 4)] * 2 + [vmem(LX + 4)] * 2,
    )
    ub, plain, um = fence((ub, plain, um))
    vb = later(ub, 1)
    va = later(ua, 1)
    around = later_wrapped(um, 1)
    cond, nu, keep, spread = call(
        material_kernel, "material", (odd, *tables, regions, a1, b1),
        [planes(LX + 6)] * 2 + [planes(LX + 14)] * 2, [],
    )
    hb = from_b(vb)
    ha = from_a(va)
    n = LX + 8
    u0, ua, ub, um = call(
        second_kernel, "second",
        (odd, hb, vb, ha, va, around, plain, source, a1, b1, cond, nu),
        [planes(3, LX + 4), planes(3, 4), planes(3, 4), planes(3, 4)], [padded(3, n)] * 2 + [vmem(3, n)] * 3,
    )
    vb = later(ub, 1)
    va = later(ua, 1)
    around, plain = later_parts(um, 1)
    hb = from_b(vb)
    va, around = fence((va, around))
    ha = from_a(va)
    residual, lb, la, lm, rb, ra, rm = call(
        residual_kernel, "residual",
        (odd, hb, vb, ha, va, around, plain, source, a1, b1, cond, nu, keep, spread, u0),
        [planes(1, 3, LX)] + [planes(3, 4)] * 6, [padded(3, n)] * 2 + [vmem(3, n)] * 2, 1, [ANY] + [VMEM] * 6,
    )
    sb = rb + later(lb, 1)
    hb = from_b(sb)
    around, plain = later_parts(lm, 1)
    moved, around = fence((later(la, 1), around))
    sa = ra + moved
    ha = from_a(sa)
    sm = rm + (around + plain)
    lb, la, lm = call(
        square_kernel, "square", (odd, hb, sb, ha, sa, sm, keep, spread),
        [planes(3, 4)] * 3, [padded(3, n)] * 2 + [vmem(3, n)],
    )
    tb = sb + later(lb, 2)
    near_b = from_b(tb)
    tm = sm + later(lm, 2)
    far_b = from_b(tm)
    around, plain = later_parts(la, 2)
    ta = sa + (around + plain)
    near_a = from_a(ta)
    far_a = from_a(tm)
    lb, la, lm, bb, ba, bm = call(
        fourth_kernel, "fourth",
        (odd, near_b, tb, far_b, tm, far_a, near_a, ta, u0, keep, spread),
        [planes(3, 4)] * 6, [padded(3, LX + 16)] * 2 + [vmem(3, LX + 16)],
    )
    eb, edge = call(
        edge_kernel, "edge", (odd, bb, later(lb, half)), [planes(3, 4), planes(3, 2)], [],
    )
    hb = from_b(edge)
    moved, hb = fence((later(la, half), hb))
    ea = ba + moved
    ha = from_a(ea)
    em = bm + later(lm, half)
    field = call(
        last_kernel, "last", (odd, hb, eb, ha, ea, em, source, a1, b1, cond, nu),
        planes(2, 3, LX), [padded(3, n)] * 2 + [vmem(3, n)] * 2, 5, ANY,
    )
    return field, residual


def solution(mesh):
    whole = P("tm", None, "space", None, None)
    return jax.shard_map(
        body, mesh=mesh, in_specs=(whole, whole, P("space", None, None), P(), P()),
        out_specs=(whole, whole), check_vma=False,
    )
```

```python
import jax
import jax.numpy as jnp
from jax import lax
from jax.experimental import pallas as pl
from jax.experimental.pallas import tpu as pltpu
from jax.sharding import PartitionSpec as P

LX, NY, NZ = 12, 64, 128
ROWS = pl.ds(8, NY)
F32 = jnp.float32
ANY = pl.BlockSpec(memory_space=pl.ANY)
HBM = pl.BlockSpec(memory_space=pltpu.HBM)
VMEM = pl.BlockSpec(memory_space=pltpu.VMEM)
SMEM = pl.BlockSpec(memory_space=pltpu.SMEM)


def planes(*lead):
    return jax.ShapeDtypeStruct(tuple(lead) + (NY, NZ), F32)


def vmem(*lead):
    return pltpu.VMEM(tuple(lead) + (NY, NZ), F32)


def padded(*lead):
    return pltpu.VMEM(tuple(lead) + (NY + 16, NZ), F32)


def clear(*bufs):
    zero = jnp.zeros((8, NZ), F32)

    def body(i, carry):
        for buf in bufs:
            for c in range(3):
                buf[c, i, pl.ds(0, 8)] = zero
                buf[c, i, pl.ds(NY + 8, 8)] = zero
        return carry

    lax.fori_loop(0, bufs[0].shape[1], body, 0)


def copy_all(pairs, sems, base=0):
    copies = [
        pltpu.make_async_copy(src, dst, sems.at[base + n]) for n, (src, dst) in enumerate(pairs)
    ]
    for copy in copies:
        copy.start()
    return copies


def wait_all(copies):
    for copy in copies:
        copy.wait()


def run_copies(pairs, sems, base=0):
    wait_all(copy_all(pairs, sems, base))


def call(kernel, name, args, outs, scratch, n_sems=0, out_specs=None, in_place=VMEM):
    in_specs = [SMEM if a.ndim == 1 else in_place for a in args]
    single = not isinstance(outs, (list, tuple))
    return pl.pallas_call(
        kernel,
        name=name,
        out_shape=outs,
        in_specs=in_specs,
        out_specs=out_specs or (VMEM if single else [VMEM] * len(outs)),
        scratch_shapes=list(scratch) + [pltpu.SemaphoreType.DMA((n_sems,))] * (n_sems > 0),
        compiler_params=pltpu.CompilerParams(vmem_limit_bytes=20 * 1024 * 1024),
        cost_estimate=pl.CostEstimate(flops=0, bytes_accessed=4 << 20, transcendentals=0),
    )(*args)


def over_layers(lo, hi, step, at_once):
    rounds = (hi - lo) // at_once

    def body(t, carry):
        for k in range(at_once):
            step(lo + t * at_once + k)
        return carry

    lax.fori_loop(0, rounds, body, 0)
    for i in range(lo + rounds * at_once, hi):
        step(i)


def neighbours(src, c, i):
    lane = lax.broadcasted_iota(jnp.int32, (NY, NZ), 1)
    zero = jnp.float32(0.0)
    if src.shape[-2] == NY:
        row = lax.broadcasted_iota(jnp.int32, (NY, NZ), 0)
        a = src[c, i]
        first = src[c, i + 1] + src[c, i - 1]
        up = jnp.where(row == 0, zero, pltpu.roll(a, 1, 0))
        down = jnp.where(row == NY - 1, zero, pltpu.roll(a, NY - 1, 0))
    else:
        a = src[c, i, ROWS]
        first = src[c, i + 1, ROWS] + src[c, i - 1, ROWS]
        up = src[c, i, pl.ds(7, NY)]
        down = src[c, i, pl.ds(9, NY)]
    left = jnp.where(lane == 0, zero, pltpu.roll(a, 1, 1))
    right = jnp.where(lane == NZ - 1, zero, pltpu.roll(a, NZ - 1, 1))
    return (first + (up + down)) + (left + right)


def layer(src, c, i):
    return src[c, i] if src.shape[-2] == NY else src[c, i, ROWS]


def fine_sweep(src, store, held, cond, nu, lo, hi, force=None, off=0):
    def step(i):
        state = [layer(src, c, i) for c in range(3)]
        square = state[0] * state[0] + state[1] * state[1] + state[2] * state[2]
        base = nu[i - off]
        weight = cond[i - off]
        grown = 1.0 + square
        strong = base * (1.0 + 1.5 * square)
        scale = 1.0 / (weight * grown + 6.0 * strong)
        keep = grown * scale
        spread = strong * scale
        for c in range(3):
            if force is not None:
                fixed = weight * state[c] + force[c, i]
                held[c, i] = fixed
            else:
                fixed = held[c, i]
            store(c, i, fixed * keep + neighbours(src, c, i) * spread)

    over_layers(lo, hi, step, 6)


def coarse_sweep(src, dst, held, keep, spread, off, lo, hi, first):
    def step(i):
        k = keep[i + off]
        s = spread[i + off]
        for c in range(3):
            if first:
                fixed = k * src[c, i, ROWS]
                held[c, i] = fixed
            else:
                fixed = held[c, i]
            dst[c, i, ROWS] = fixed + s * neighbours(src, c, i)

    over_layers(lo, hi, step, 6)


def lookup(code, table):
    first = jnp.where(code == 1, table[0], table[1])
    second = jnp.where(code == 3, table[2], table[3])
    return jnp.where(code <= 2, first, second)


def materials(code, cond_t, nu_t):
    outside = code == 0
    return (
        jnp.where(outside, jnp.float32(1.0), lookup(code, cond_t)),
        jnp.where(outside, jnp.float32(0.0), lookup(code, nu_t)),
    )


def into(buf):
    def store(c, i, value):
        buf[c, i, ROWS] = value
    return store


def edges(odd, n, width):
    return (1 - odd) * (n - width), odd * (n - width)


def first_pack_kernel(odd_ref, g_low, g_high, s_low, s_high, r_low, r_high, a1, b1):
    odd = odd_ref[0]

    def fill(low, high):
        for c in range(3):
            for k in range(2):
                low[2 * c + k] = g_low[0, c, k]
                high[2 * c + k] = g_high[0, c, k]
            low[6 + c] = s_low[0, c, 0]
            high[6 + c] = s_high[0, c, 0]
        low[9] = (r_low[0] + 1).astype(F32)
        high[9] = (r_high[0] + 1).astype(F32)

    @pl.when(odd == 0)
    def even_slab():
        fill(b1, a1)

    @pl.when(odd == 1)
    def odd_slab():
        fill(a1, b1)


def second_pack_kernel(odd_ref, source, regions, a2, b2):
    odd = odd_ref[0]
    for two, start in zip((a2, b2), edges(odd, LX, 3)):
        for c in range(3):
            for k in range(3):
                two[3 * c + k] = source[0, c, start + k]
    for two, start in zip((a2, b2), edges(odd, LX, 7)):
        for k in range(7):
            two[9 + k] = (regions[start + k] + 1).astype(F32)


def first_middle_kernel(cond_t, nu_t, guess, source, regions, out, y, held, cond, nu):
    def prepare(i):
        cond[i], nu[i] = materials(regions[i] + 1, cond_t, nu_t)

    over_layers(3, 9, prepare, 6)
    clear(y)
    fine_sweep(guess.at[0], into(y), held, cond, nu, 3, 9, source.at[1])

    def store(c, i, value):
        out[c, i - 4] = value

    fine_sweep(y, store, held, cond, nu, 4, 8)


def first_kernel(odd_ref, cond_t, nu_t, guess, source, regions, ra, rb, after, out_a, out_b, x, y, held, f, cond, nu):
    odd = odd_ref[0]
    clear(x, y)
    n = LX + 4
    for c in range(3):
        for i in (0, 1, 2, 3, 4, 5, 6, 7, 8, 9, 10, 11):
            x[c, i + 2, ROWS] = guess[0, c, i]
            f[c, i + 2] = source[1, c, i]
    for i in range(LX):
        cond[i + 2], nu[i + 2] = materials(regions[i] + 1, cond_t, nu_t)
    for pack, high in ((ra, 1 - odd), (rb, odd)):
        for c in range(3):
            for k in range(2):
                x[c, high * (n - 2) + k, ROWS] = pack[2 * c + k]
            f[c, 1 + high * (n - 3)] = pack[6 + c]
        cond[1 + high * (n - 3)], nu[1 + high * (n - 3)] = materials(pack[9], cond_t, nu_t)
    fine_sweep(x, into(y), held, cond, nu, 1, 7, f)
    fine_sweep(x, into(y), held, cond, nu, 9, n - 1, f)
    fine_sweep(y, into(x), held, cond, nu, 2, 6)
    fine_sweep(y, into(x), held, cond, nu, 10, 14)
    for c in range(3):
        for k in range(4):
            out_a[c, k] = x[c, 2 + (1 - odd) * 8 + k, ROWS]
            out_b[c, k] = x[c, 2 + odd * 8 + k, ROWS]


def material_kernel(odd_ref, cond_t, nu_t, regions, ra, rb, cond, nu, keep, spread):
    odd = odd_ref[0]

    def fill(at, code, near=True):
        cv, nv = materials(code, cond_t, nu_t)
        if near:
            cond[at - 4] = cv
            nu[at - 4] = nv
        half = 0.5 * cv
        scale = 1.0 / (half + 6.0 * nv)
        keep[at] = half * scale
        spread[at] = nv * scale

    for i in range(LX):
        fill(7 + i, regions[i] + 1)
    for k in range(7):
        from_on, from_off = ra[9 + k], rb[9 + k]
        fill(k, jnp.where(odd == 1, from_on, from_off), k >= 4)
        fill(LX + 7 + k, jnp.where(odd == 1, from_off, from_on), k < 3)


def extend(odd, pieces, halos, x):
    a, b, *m = pieces
    ha, hb = halos
    for c in range(3):
        for k in range(4):
            middle = m[0][c, k]
            for other in m[1:]:
                middle = middle + other[c, k]
            x[c, 8 + k, ROWS] = middle
            x[c, 4 + (1 - odd) * 8 + k, ROWS] = a[c, k]
            x[c, 4 + odd * 8 + k, ROWS] = b[c, k]
            x[c, (1 - odd) * 16 + k, ROWS] = ha[c, k]
            x[c, odd * 16 + k, ROWS] = hb[c, k]


def extend_force(odd, source, which, width, packs, start, f):
    for c in range(3):
        for i in range(LX):
            f[c, 4 + i] = source[which, c, i]
        for pack, high in ((packs[0], 1 - odd), (packs[1], odd)):
            for k in range(width):
                f[c, 4 - width + high * (LX + width) + k] = pack[start + width * c + k]


def second_kernel(
    odd_ref, hb, vb, ha, va, vm, vn, source, a1, b1, a2, b2, cond, nu,
    u0, oa, ob, om, x, y, held, f0, f1,
):
    odd = odd_ref[0]
    clear(x, y)
    extend(odd, (va, vb, vm, vn), (ha, hb), x)
    extend_force(odd, source, 0, 3, (a2, b2), 0, f0)
    extend_force(odd, source, 1, 1, (a1, b1), 6, f1)

    def keep_u0(c, i, value):
        x[c, i, ROWS] = value
        u0[c, i - 2] = value

    fine_sweep(x, into(y), held, cond, nu, 1, 19, f0, 1)
    fine_sweep(y, keep_u0, held, cond, nu, 2, 18, None, 1)
    fine_sweep(x, into(y), held, cond, nu, 3, 17, f1, 1)
    fine_sweep(y, into(x), held, cond, nu, 4, 16, None, 1)
    for c in range(3):
        for k in range(4):
            om[c, k] = x[c, 8 + k, ROWS]
            oa[c, k] = x[c, 4 + (1 - odd) * 8 + k, ROWS]
            ob[c, k] = x[c, 4 + odd * 8 + k, ROWS]


def split(odd, x, start, b, a, m):
    for c in range(3):
        for k in range(4):
            b[c, k] = x[c, start + odd * 8 + k, ROWS]
            a[c, k] = x[c, start + (1 - odd) * 8 + k, ROWS]
            m[c, k] = x[c, start + 4 + k, ROWS]


def residual_kernel(
    odd_ref, hb, vb, ha, va, vm, vn, source, a2, b2, cond, nu, keep, spread, u0,
    res_o, lb, la, lm, rb, ra, rm, x, y, held, f0, sems,
):
    odd = odd_ref[0]
    clear(x, y)
    extend(odd, (va, vb, vm, vn), (ha, hb), x)
    extend_force(odd, source, 0, 3, (a2, b2), 0, f0)

    def less(c, i, value):
        x[c, i, ROWS] = value - u0[c, i - 2]

    fine_sweep(x, into(y), held, cond, nu, 1, 19, f0, 1)
    fine_sweep(y, less, held, cond, nu, 2, 18, None, 1)
    kept = copy_all([(x.at[:, pl.ds(4, LX), ROWS], res_o.at[0])], sems)
    split(odd, x, 4, rb, ra, rm)
    coarse_sweep(x, y, held, keep, spread, 3, 3, 17, True)
    wait_all(kept)
    coarse_sweep(y, x, held, keep, spread, 3, 4, 16, False)
    split(odd, x, 4, lb, la, lm)


def square_kernel(odd_ref, hb, sb, ha, sa, sm, keep, spread, ob, oa, om, x, y, held):
    odd = odd_ref[0]
    clear(x, y)
    extend(odd, (sa, sb, sm), (ha, hb), x)
    for lo in (1, 3):
        coarse_sweep(x, y, held, keep, spread, 3, lo, 20 - lo, True)
        coarse_sweep(y, x, held, keep, spread, 3, lo + 1, 19 - lo, False)
    split(odd, x, 4, ob, oa, om)


def fourth_kernel(
    odd_ref, near_b, tb, far_b, tm, far_a, near_a, ta, u0, keep, spread,
    ob, oa, om, bb, ba, bm, x, y, held,
):
    odd = odd_ref[0]
    clear(x, y)
    for c in range(3):
        for k in range(4):
            x[c, 8 + odd * 8 + k, ROWS] = tb[c, k]
            x[c, 8 + (1 - odd) * 8 + k, ROWS] = ta[c, k]
            x[c, 12 + k, ROWS] = tm[c, k]
            x[c, 4 + odd * 16 + k, ROWS] = near_b[c, k]
            x[c, 4 + (1 - odd) * 16 + k, ROWS] = near_a[c, k]
            x[c, odd * 24 + k, ROWS] = far_b[c, k]
            x[c, (1 - odd) * 24 + k, ROWS] = far_a[c, k]
    for c in range(3):
        for k in range(4):
            bb[c, k] = tb[c, k] + u0[c, 2 + odd * 8 + k]
            ba[c, k] = ta[c, k] + u0[c, 2 + (1 - odd) * 8 + k]
            bm[c, k] = tm[c, k] + u0[c, 6 + k]
    for lo in (1, 3, 5, 7):
        coarse_sweep(x, y, held, keep, spread, -1, lo, 28 - lo, True)
        coarse_sweep(y, x, held, keep, spread, -1, lo + 1, 27 - lo, False)
    split(odd, x, 8, ob, oa, om)


def edge_kernel(odd_ref, base, moved, total, edge):
    odd = odd_ref[0]
    for c in range(3):
        for k in range(4):
            total[c, k] = base[c, k] + moved[c, k]
        for k in range(2):
            edge[c, k] = total[c, odd * 2 + k]


def last_kernel(
    odd_ref, hb, eb, ha, ea, em, source, a1, b1, cond, nu, field, x, y, held, f1, sems,
):
    odd = odd_ref[0]
    clear(x, y)
    kept = copy_all(
        [
            (eb, field.at[0, :, pl.ds(odd * 8, 4)]),
            (ea, field.at[0, :, pl.ds((1 - odd) * 8, 4)]),
            (em, field.at[0, :, pl.ds(4, 4)]),
        ],
        sems,
    )
    extend_force(odd, source, 1, 1, (a1, b1), 6, f1)
    for c in range(3):
        for k in range(4):
            x[c, 4 + odd * 8 + k, ROWS] = eb[c, k]
            x[c, 4 + (1 - odd) * 8 + k, ROWS] = ea[c, k]
            x[c, 8 + k, ROWS] = em[c, k]
        for k in range(2):
            x[c, 2 + odd * 14 + k, ROWS] = hb[c, k]
            x[c, 2 + (1 - odd) * 14 + k, ROWS] = ha[c, odd * 2 + k]
    fine_sweep(x, into(y), held, cond, nu, 3, 17, f1, 1)
    fine_sweep(y, into(x), held, cond, nu, 4, 10, None, 1)
    kept += copy_all([(x.at[:, pl.ds(4, 6), ROWS], field.at[1, :, pl.ds(0, 6)])], sems, 3)
    fine_sweep(y, into(x), held, cond, nu, 10, 16, None, 1)
    kept += copy_all([(x.at[:, pl.ds(10, 6), ROWS], field.at[1, :, pl.ds(6, 6)])], sems, 4)
    wait_all(kept)


def body(guess, source, regions, conductance, reluct):
    slices = lax.axis_size("tm")
    slabs = lax.axis_size("space")
    odd = (lax.axis_index("space") % 2).astype(jnp.int32).reshape(1)
    on_chip = [(i, i ^ 1) for i in range(slabs)]
    off_chip = [(i, i + 1) for i in range(1, slabs - 1, 2)]
    off_chip += [(j, i) for i, j in off_chip]
    fence = lax.optimization_barrier

    def from_a(x):
        return lax.ppermute(x, "space", on_chip)

    def from_b(x):
        return lax.ppermute(x, "space", off_chip)

    half = slices // 2

    def along(x, pairs):
        return lax.ppermute(x, "tm", pairs)

    def later(x, distance):
        return along(x, [(i, (i + distance) % slices) for i in range(slices)])

    def later_parts(x, distance):
        wrapping = [i for i in range(slices) if i % half + distance >= half]
        across = along(x, [(i, (i + half) % slices) for i in wrapping])
        around = along(across, [((i + half) % slices, (i + distance) % slices) for i in wrapping])
        plain = along(x, [(i, i + distance) for i in range(slices) if i not in wrapping])
        return around, plain

    tables = (conductance, reluct)
    sa1, sb1 = call(
        first_pack_kernel, "first_pack",
        (odd, guess[:1, :, :2], guess[:1, :, LX - 2:], source[1:, :, :1], source[1:, :, LX - 1:], regions[:1], regions[LX - 1:]),
        [planes(10), planes(10)], [],
    )
    b1 = from_b(sb1)
    a1 = from_a(sa1)
    um = call(
        first_middle_kernel, "first_middle", (*tables, guess, source, regions),
        planes(3, 4), [padded(3, LX), vmem(3, LX)] + [vmem(LX)] * 2,
    )
    sa2, sb2 = call(
        second_pack_kernel, "second_pack", (odd, source, regions), [planes(16), planes(16)], [],
    )
    vm = later_parts(um, 1)
    sb2, sa2, b1 = fence((sb2, sa2, b1))
    b2 = from_b(sb2)
    a2 = from_a(sa2)
    ua, ub = call(
        first_kernel, "first", (odd, *tables, guess, source, regions, a1, b1, um),
        [planes(3, 4), planes(3, 4)], [padded(3, LX + 4)] * 2 + [vmem(3, LX + 4)] * 2 + [vmem(LX + 4)] * 2,
    )
    vb = later(ub, 1)
    va = later(ua, 1)
    cond, nu, keep, spread = call(
        material_kernel, "material", (odd, *tables, regions, a2, b2),
        [planes(LX + 6)] * 2 + [planes(LX + 14)] * 2, [],
    )
    vb, cond = fence((vb, cond))
    hb = from_b(vb)
    va, *vm = fence((va, *vm))
    ha = from_a(va)
    n = LX + 8
    u0, ua, ub, um = call(
        second_kernel, "second",
        (odd, hb, vb, ha, va, *vm, source, a1, b1, a2, b2, cond, nu),
        [planes(3, LX + 4), planes(3, 4), planes(3, 4), planes(3, 4)], [padded(3, n)] * 2 + [vmem(3, n)] * 3,
    )
    vb = later(ub, 1)
    va = later(ua, 1)
    around, plain = later_parts(um, 1)
    hb = from_b(vb)
    va, around = fence((va, around))
    ha = from_a(va)
    residual, lb, la, lm, rb, ra, rm = call(
        residual_kernel, "residual",
        (odd, hb, vb, ha, va, around, plain, source, a2, b2, cond, nu, keep, spread, u0),
        [planes(1, 3, LX)] + [planes(3, 4)] * 6, [padded(3, n)] * 2 + [vmem(3, n)] * 2, 1, [ANY] + [VMEM] * 6,
    )
    sb = rb + later(lb, 1)
    hb = from_b(sb)
    around, plain = later_parts(lm, 1)
    moved, around = fence((later(la, 1), around))
    sa = ra + moved
    ha = from_a(sa)
    sm = rm + (around + plain)
    lb, la, lm = call(
        square_kernel, "square", (odd, hb, sb, ha, sa, sm, keep, spread),
        [planes(3, 4)] * 3, [padded(3, n)] * 2 + [vmem(3, n)],
    )
    tb = sb + later(lb, 2)
    near_b = from_b(tb)
    tm = sm + later(lm, 2)
    far_b = from_b(tm)
    around, plain = later_parts(la, 2)
    ta = sa + (around + plain)
    near_a = from_a(ta)
    far_a = from_a(tm)
    lb, la, lm, bb, ba, bm = call(
        fourth_kernel, "fourth",
        (odd, near_b, tb, far_b, tm, far_a, near_a, ta, u0, keep, spread),
        [planes(3, 4)] * 6, [padded(3, LX + 16)] * 2 + [vmem(3, LX + 16)],
    )
    eb, edge = call(
        edge_kernel, "edge", (odd, bb, later(lb, half)), [planes(3, 4), planes(3, 2)], [],
    )
    hb = from_b(edge)
    moved, hb = fence((later(la, half), hb))
    ea = ba + moved
    ha = from_a(ea)
    em = bm + later(lm, half)
    field = call(
        last_kernel, "last", (odd, hb, eb, ha, ea, em, source, a1, b1, cond, nu),
        planes(2, 3, LX), [padded(3, n)] * 2 + [vmem(3, n)] * 2, 5, ANY,
    )
    return field, residual


def solution(mesh):
    whole = P("tm", None, "space", None, None)
    return jax.shard_map(
        body, mesh=mesh, in_specs=(whole, whole, P("space", None, None), P(), P()),
        out_specs=(whole, whole), check_vma=False,
    )
```

```python
import jax
import jax.numpy as jnp
from jax import lax
from jax.experimental import pallas as pl
from jax.experimental.pallas import tpu as pltpu
from jax.sharding import PartitionSpec as P

LX, NY, NZ = 12, 64, 128
ROWS = pl.ds(8, NY)
F32 = jnp.float32
ANY = pl.BlockSpec(memory_space=pl.ANY)
HBM = pl.BlockSpec(memory_space=pltpu.HBM)
VMEM = pl.BlockSpec(memory_space=pltpu.VMEM)
SMEM = pl.BlockSpec(memory_space=pltpu.SMEM)


def planes(*lead):
    return jax.ShapeDtypeStruct(tuple(lead) + (NY, NZ), F32)


def vmem(*lead):
    return pltpu.VMEM(tuple(lead) + (NY, NZ), F32)


def padded(*lead):
    return pltpu.VMEM(tuple(lead) + (NY + 16, NZ), F32)


def clear(*bufs):
    zero = jnp.zeros((8, NZ), F32)

    def body(i, carry):
        for buf in bufs:
            for c in range(3):
                buf[c, i, pl.ds(0, 8)] = zero
                buf[c, i, pl.ds(NY + 8, 8)] = zero
        return carry

    lax.fori_loop(0, bufs[0].shape[1], body, 0)


def copy_all(pairs, sems, base=0):
    copies = [
        pltpu.make_async_copy(src, dst, sems.at[base + n]) for n, (src, dst) in enumerate(pairs)
    ]
    for copy in copies:
        copy.start()
    return copies


def wait_all(copies):
    for copy in copies:
        copy.wait()


def run_copies(pairs, sems, base=0):
    wait_all(copy_all(pairs, sems, base))


def call(kernel, name, args, outs, scratch, n_sems=0, out_specs=None, in_place=VMEM):
    in_specs = [SMEM if a.ndim == 1 else in_place for a in args]
    single = not isinstance(outs, (list, tuple))
    return pl.pallas_call(
        kernel,
        name=name,
        out_shape=outs,
        in_specs=in_specs,
        out_specs=out_specs or (VMEM if single else [VMEM] * len(outs)),
        scratch_shapes=list(scratch) + [pltpu.SemaphoreType.DMA((n_sems,))] * (n_sems > 0),
        compiler_params=pltpu.CompilerParams(vmem_limit_bytes=20 * 1024 * 1024),
        cost_estimate=pl.CostEstimate(flops=0, bytes_accessed=4 << 20, transcendentals=0),
    )(*args)


def over_layers(lo, hi, step, at_once):
    rounds = (hi - lo) // at_once

    def body(t, carry):
        for k in range(at_once):
            step(lo + t * at_once + k)
        return carry

    lax.fori_loop(0, rounds, body, 0)
    for i in range(lo + rounds * at_once, hi):
        step(i)


def neighbours(src, c, i):
    lane = lax.broadcasted_iota(jnp.int32, (NY, NZ), 1)
    zero = jnp.float32(0.0)
    if src.shape[-2] == NY:
        row = lax.broadcasted_iota(jnp.int32, (NY, NZ), 0)
        a = src[c, i]
        first = src[c, i + 1] + src[c, i - 1]
        up = jnp.where(row == 0, zero, pltpu.roll(a, 1, 0))
        down = jnp.where(row == NY - 1, zero, pltpu.roll(a, NY - 1, 0))
    else:
        a = src[c, i, ROWS]
        first = src[c, i + 1, ROWS] + src[c, i - 1, ROWS]
        up = src[c, i, pl.ds(7, NY)]
        down = src[c, i, pl.ds(9, NY)]
    left = jnp.where(lane == 0, zero, pltpu.roll(a, 1, 1))
    right = jnp.where(lane == NZ - 1, zero, pltpu.roll(a, NZ - 1, 1))
    return (first + (up + down)) + (left + right)


def layer(src, c, i):
    return src[c, i] if src.shape[-2] == NY else src[c, i, ROWS]


def fine_sweep(src, store, held, cond, nu, lo, hi, force=None, off=0):
    def step(i):
        state = [layer(src, c, i) for c in range(3)]
        square = state[0] * state[0] + state[1] * state[1] + state[2] * state[2]
        base = nu[i - off]
        weight = cond[i - off]
        grown = 1.0 + square
        strong = base * (1.0 + 1.5 * square)
        scale = 1.0 / (weight * grown + 6.0 * strong)
        keep = grown * scale
        spread = strong * scale
        for c in range(3):
            if force is not None:
                fixed = weight * state[c] + force[c, i]
                held[c, i] = fixed
            else:
                fixed = held[c, i]
            store(c, i, fixed * keep + neighbours(src, c, i) * spread)

    over_layers(lo, hi, step, 6)


def coarse_sweep(src, dst, held, keep, spread, off, lo, hi, first):
    def step(i):
        k = keep[i + off]
        s = spread[i + off]
        for c in range(3):
            if first:
                fixed = k * src[c, i, ROWS]
                held[c, i] = fixed
            else:
                fixed = held[c, i]
            dst[c, i, ROWS] = fixed + s * neighbours(src, c, i)

    over_layers(lo, hi, step, 6)


def lookup(code, table):
    first = jnp.where(code == 1, table[0], table[1])
    second = jnp.where(code == 3, table[2], table[3])
    return jnp.where(code <= 2, first, second)


def materials(code, cond_t, nu_t):
    outside = code == 0
    return (
        jnp.where(outside, jnp.float32(1.0), lookup(code, cond_t)),
        jnp.where(outside, jnp.float32(0.0), lookup(code, nu_t)),
    )


def into(buf):
    def store(c, i, value):
        buf[c, i, ROWS] = value
    return store


def edges(odd, n, width):
    return (1 - odd) * (n - width), odd * (n - width)


def first_pack_kernel(odd_ref, g_low, g_high, s_low, s_high, r_low, r_high, a1, b1):
    odd = odd_ref[0]

    def fill(low, high):
        for c in range(3):
            for k in range(2):
                low[2 * c + k] = g_low[0, c, k]
                high[2 * c + k] = g_high[0, c, k]
            low[6 + c] = s_low[0, c, 0]
            high[6 + c] = s_high[0, c, 0]
        low[9] = (r_low[0] + 1).astype(F32)
        high[9] = (r_high[0] + 1).astype(F32)

    @pl.when(odd == 0)
    def even_slab():
        fill(b1, a1)

    @pl.when(odd == 1)
    def odd_slab():
        fill(a1, b1)


def second_pack_kernel(odd_ref, source, regions, a2, b2, a3, b3, reg, sems):
    odd = odd_ref[0]
    pairs = [(regions, reg)]
    for two, start in zip((a2, b2), edges(odd, LX, 3)):
        for c in range(3):
            pairs.append((source.at[0, c, pl.ds(start, 3)], two.at[pl.ds(3 * c, 3)]))
    run_copies(pairs, sems)
    for two, start in zip((a2, b2), edges(odd, LX, 3)):
        for k in range(3):
            two[9 + k] = (reg[start + k] + 1).astype(F32)
    for three, high in ((a3, 1 - odd), (b3, odd)):
        for k in range(4):
            three[k] = (reg[high * (LX - 7) + (1 - high) * 3 + k] + 1).astype(F32)


def first_middle_kernel(cond_t, nu_t, guess, source, regions, out, y, held, cond, nu):
    def prepare(i):
        cond[i], nu[i] = materials(regions[i] + 1, cond_t, nu_t)

    over_layers(3, 9, prepare, 6)
    clear(y)
    fine_sweep(guess.at[0], into(y), held, cond, nu, 3, 9, source.at[1])

    def store(c, i, value):
        out[c, i - 4] = value

    fine_sweep(y, store, held, cond, nu, 4, 8)


def first_kernel(odd_ref, cond_t, nu_t, guess, source, regions, ra, rb, after, out_a, out_b, x, y, held, f, cond, nu):
    odd = odd_ref[0]
    clear(x, y)
    n = LX + 4
    for c in range(3):
        for i in (0, 1, 2, 3, 4, 5, 6, 7, 8, 9, 10, 11):
            x[c, i + 2, ROWS] = guess[0, c, i]
            f[c, i + 2] = source[1, c, i]
    for i in range(LX):
        cond[i + 2], nu[i + 2] = materials(regions[i] + 1, cond_t, nu_t)
    for pack, high in ((ra, 1 - odd), (rb, odd)):
        for c in range(3):
            for k in range(2):
                x[c, high * (n - 2) + k, ROWS] = pack[2 * c + k]
            f[c, 1 + high * (n - 3)] = pack[6 + c]
        cond[1 + high * (n - 3)], nu[1 + high * (n - 3)] = materials(pack[9], cond_t, nu_t)
    fine_sweep(x, into(y), held, cond, nu, 1, 7, f)
    fine_sweep(x, into(y), held, cond, nu, 9, n - 1, f)
    fine_sweep(y, into(x), held, cond, nu, 2, 6)
    fine_sweep(y, into(x), held, cond, nu, 10, 14)
    for c in range(3):
        for k in range(4):
            out_a[c, k] = x[c, 2 + (1 - odd) * 8 + k, ROWS]
            out_b[c, k] = x[c, 2 + odd * 8 + k, ROWS]


def material_kernel(odd_ref, cond_t, nu_t, regions, ra, rb, cond, nu, keep, spread):
    odd = odd_ref[0]

    def fill(at, code):
        cv, nv = materials(code, cond_t, nu_t)
        cond[at] = cv
        nu[at] = nv
        half = 0.5 * cv
        scale = 1.0 / (half + 6.0 * nv)
        keep[at] = half * scale
        spread[at] = nv * scale

    for i in range(LX):
        fill(3 + i, regions[i] + 1)
    for pack, high in ((ra, 1 - odd), (rb, odd)):
        for k in range(3):
            fill(high * (LX + 3) + k, pack[9 + k])


def wide_kernel(odd_ref, cond_t, nu_t, keep_i, spread_i, ra, rb, keep, spread):
    odd = odd_ref[0]
    for i in range(LX + 6):
        keep[i + 4] = keep_i[i]
        spread[i + 4] = spread_i[i]
    for pack, high in ((ra, 1 - odd), (rb, odd)):
        for k in range(4):
            at = high * (LX + 10) + k
            cv, nv = materials(pack[k], cond_t, nu_t)
            half = 0.5 * cv
            scale = 1.0 / (half + 6.0 * nv)
            keep[at] = half * scale
            spread[at] = nv * scale


def extend(odd, pieces, halos, x):
    a, b, *m = pieces
    ha, hb = halos
    for c in range(3):
        for k in range(4):
            middle = m[0][c, k]
            for other in m[1:]:
                middle = middle + other[c, k]
            x[c, 8 + k, ROWS] = middle
            x[c, 4 + (1 - odd) * 8 + k, ROWS] = a[c, k]
            x[c, 4 + odd * 8 + k, ROWS] = b[c, k]
            x[c, (1 - odd) * 16 + k, ROWS] = ha[c, k]
            x[c, odd * 16 + k, ROWS] = hb[c, k]


def extend_force(odd, source, which, width, packs, start, f):
    for c in range(3):
        for i in range(LX):
            f[c, 4 + i] = source[which, c, i]
        for pack, high in ((packs[0], 1 - odd), (packs[1], odd)):
            for k in range(width):
                f[c, 4 - width + high * (LX + width) + k] = pack[start + width * c + k]


def second_kernel(
    odd_ref, hb, vb, ha, va, vm, vn, source, a1, b1, a2, b2, cond, nu,
    u0, oa, ob, om, x, y, held, f0, f1,
):
    odd = odd_ref[0]
    clear(x, y)
    extend(odd, (va, vb, vm, vn), (ha, hb), x)
    extend_force(odd, source, 0, 3, (a2, b2), 0, f0)
    extend_force(odd, source, 1, 1, (a1, b1), 6, f1)

    def keep_u0(c, i, value):
        x[c, i, ROWS] = value
        u0[c, i - 2] = value

    fine_sweep(x, into(y), held, cond, nu, 1, 19, f0, 1)
    fine_sweep(y, keep_u0, held, cond, nu, 2, 18, None, 1)
    fine_sweep(x, into(y), held, cond, nu, 3, 17, f1, 1)
    fine_sweep(y, into(x), held, cond, nu, 4, 16, None, 1)
    for c in range(3):
        for k in range(4):
            om[c, k] = x[c, 8 + k, ROWS]
            oa[c, k] = x[c, 4 + (1 - odd) * 8 + k, ROWS]
            ob[c, k] = x[c, 4 + odd * 8 + k, ROWS]


def split(odd, x, start, b, a, m):
    for c in range(3):
        for k in range(4):
            b[c, k] = x[c, start + odd * 8 + k, ROWS]
            a[c, k] = x[c, start + (1 - odd) * 8 + k, ROWS]
            m[c, k] = x[c, start + 4 + k, ROWS]


def residual_kernel(
    odd_ref, hb, vb, ha, va, vm, vn, source, a2, b2, cond, nu, keep, spread, u0,
    res_o, lb, la, lm, rb, ra, rm, x, y, held, f0, sems,
):
    odd = odd_ref[0]
    clear(x, y)
    extend(odd, (va, vb, vm, vn), (ha, hb), x)
    extend_force(odd, source, 0, 3, (a2, b2), 0, f0)

    def less(c, i, value):
        x[c, i, ROWS] = value - u0[c, i - 2]

    fine_sweep(x, into(y), held, cond, nu, 1, 19, f0, 1)
    fine_sweep(y, less, held, cond, nu, 2, 18, None, 1)
    kept = copy_all([(x.at[:, pl.ds(4, LX), ROWS], res_o.at[0])], sems)
    split(odd, x, 4, rb, ra, rm)
    coarse_sweep(x, y, held, keep, spread, 3, 3, 17, True)
    wait_all(kept)
    coarse_sweep(y, x, held, keep, spread, 3, 4, 16, False)
    split(odd, x, 4, lb, la, lm)


def square_kernel(odd_ref, hb, sb, ha, sa, sm, keep, spread, ob, oa, om, x, y, held):
    odd = odd_ref[0]
    clear(x, y)
    extend(odd, (sa, sb, sm), (ha, hb), x)
    for lo in (1, 3):
        coarse_sweep(x, y, held, keep, spread, -1, lo, 20 - lo, True)
        coarse_sweep(y, x, held, keep, spread, -1, lo + 1, 19 - lo, False)
    split(odd, x, 4, ob, oa, om)


def fourth_kernel(
    odd_ref, near_b, tb, far_b, tm, far_a, near_a, ta, u0, keep, spread,
    ob, oa, om, bb, ba, bm, x, y, held,
):
    odd = odd_ref[0]
    clear(x, y)
    for c in range(3):
        for k in range(4):
            x[c, 8 + odd * 8 + k, ROWS] = tb[c, k]
            x[c, 8 + (1 - odd) * 8 + k, ROWS] = ta[c, k]
            x[c, 12 + k, ROWS] = tm[c, k]
            x[c, 4 + odd * 16 + k, ROWS] = near_b[c, k]
            x[c, 4 + (1 - odd) * 16 + k, ROWS] = near_a[c, k]
            x[c, odd * 24 + k, ROWS] = far_b[c, k]
            x[c, (1 - odd) * 24 + k, ROWS] = far_a[c, k]
    for c in range(3):
        for k in range(4):
            bb[c, k] = tb[c, k] + u0[c, 2 + odd * 8 + k]
            ba[c, k] = ta[c, k] + u0[c, 2 + (1 - odd) * 8 + k]
            bm[c, k] = tm[c, k] + u0[c, 6 + k]
    for lo in (1, 3, 5, 7):
        coarse_sweep(x, y, held, keep, spread, -1, lo, 28 - lo, True)
        coarse_sweep(y, x, held, keep, spread, -1, lo + 1, 27 - lo, False)
    split(odd, x, 8, ob, oa, om)


def edge_kernel(odd_ref, base, moved, total, edge):
    odd = odd_ref[0]
    for c in range(3):
        for k in range(4):
            total[c, k] = base[c, k] + moved[c, k]
        for k in range(2):
            edge[c, k] = total[c, odd * 2 + k]


def last_kernel(
    odd_ref, hb, eb, ha, ea, em, source, a1, b1, cond, nu, field, x, y, held, f1, sems,
):
    odd = odd_ref[0]
    clear(x, y)
    kept = copy_all(
        [
            (eb, field.at[0, :, pl.ds(odd * 8, 4)]),
            (ea, field.at[0, :, pl.ds((1 - odd) * 8, 4)]),
            (em, field.at[0, :, pl.ds(4, 4)]),
        ],
        sems,
    )
    extend_force(odd, source, 1, 1, (a1, b1), 6, f1)
    for c in range(3):
        for k in range(4):
            x[c, 4 + odd * 8 + k, ROWS] = eb[c, k]
            x[c, 4 + (1 - odd) * 8 + k, ROWS] = ea[c, k]
            x[c, 8 + k, ROWS] = em[c, k]
        for k in range(2):
            x[c, 2 + odd * 14 + k, ROWS] = hb[c, k]
            x[c, 2 + (1 - odd) * 14 + k, ROWS] = ha[c, odd * 2 + k]
    fine_sweep(x, into(y), held, cond, nu, 3, 17, f1, 1)
    fine_sweep(y, into(x), held, cond, nu, 4, 10, None, 1)
    kept += copy_all([(x.at[:, pl.ds(4, 6), ROWS], field.at[1, :, pl.ds(0, 6)])], sems, 3)
    fine_sweep(y, into(x), held, cond, nu, 10, 16, None, 1)
    kept += copy_all([(x.at[:, pl.ds(10, 6), ROWS], field.at[1, :, pl.ds(6, 6)])], sems, 4)
    wait_all(kept)


def body(guess, source, regions, conductance, reluct):
    slices = lax.axis_size("tm")
    slabs = lax.axis_size("space")
    odd = (lax.axis_index("space") % 2).astype(jnp.int32).reshape(1)
    on_chip = [(i, i ^ 1) for i in range(slabs)]
    off_chip = [(i, i + 1) for i in range(1, slabs - 1, 2)]
    off_chip += [(j, i) for i, j in off_chip]
    fence = lax.optimization_barrier

    def from_a(x):
        return lax.ppermute(x, "space", on_chip)

    def from_b(x):
        return lax.ppermute(x, "space", off_chip)

    half = slices // 2

    def along(x, pairs):
        return lax.ppermute(x, "tm", pairs)

    def later(x, distance):
        return along(x, [(i, (i + distance) % slices) for i in range(slices)])

    def later_parts(x, distance):
        wrapping = [i for i in range(slices) if i % half + distance >= half]
        across = along(x, [(i, (i + half) % slices) for i in wrapping])
        around = along(across, [((i + half) % slices, (i + distance) % slices) for i in wrapping])
        plain = along(x, [(i, i + distance) for i in range(slices) if i not in wrapping])
        return around, plain

    tables = (conductance, reluct)
    sa1, sb1 = call(
        first_pack_kernel, "first_pack",
        (odd, guess[:1, :, :2], guess[:1, :, LX - 2:], source[1:, :, :1], source[1:, :, LX - 1:], regions[:1], regions[LX - 1:]),
        [planes(10), planes(10)], [],
    )
    b1 = from_b(sb1)
    a1 = from_a(sa1)
    um = call(
        first_middle_kernel, "first_middle", (*tables, guess, source, regions),
        planes(3, 4), [padded(3, LX), vmem(3, LX)] + [vmem(LX)] * 2,
    )
    sa2, sb2, sa3, sb3 = call(
        second_pack_kernel, "second_pack", (odd, source, regions),
        [planes(12), planes(12), planes(4), planes(4)], [pltpu.VMEM((LX, NY, NZ), jnp.int32)], 8, in_place=HBM,
    )
    vm = later_parts(um, 1)
    sb2, sa2, b1 = fence((sb2, sa2, b1))
    b2 = from_b(sb2)
    a2 = from_a(sa2)
    ua, ub = call(
        first_kernel, "first", (odd, *tables, guess, source, regions, a1, b1, um),
        [planes(3, 4), planes(3, 4)], [padded(3, LX + 4)] * 2 + [vmem(3, LX + 4)] * 2 + [vmem(LX + 4)] * 2,
    )
    vb = later(ub, 1)
    va = later(ua, 1)
    cond, nu, keep, spread = call(
        material_kernel, "material", (odd, *tables, regions, a2, b2), [planes(LX + 6)] * 4, [],
    )
    vb, cond = fence((vb, cond))
    hb = from_b(vb)
    va, *vm = fence((va, *vm))
    ha = from_a(va)
    n = LX + 8
    u0, ua, ub, um = call(
        second_kernel, "second",
        (odd, hb, vb, ha, va, *vm, source, a1, b1, a2, b2, cond, nu),
        [planes(3, LX + 4), planes(3, 4), planes(3, 4), planes(3, 4)], [padded(3, n)] * 2 + [vmem(3, n)] * 3,
    )
    sb3, sa3, ub = fence((sb3, sa3, ub))
    vb = later(ub, 1)
    va = later(ua, 1)
    around, plain = later_parts(um, 1)
    hb = from_b(vb)
    b3 = from_b(sb3)
    a3 = from_a(sa3)
    wide_keep, wide_spread = call(
        wide_kernel, "wide", (odd, *tables, keep, spread, a3, b3), [planes(LX + 14)] * 2, [],
    )
    va, around = fence((va, around))
    ha = from_a(va)
    residual, lb, la, lm, rb, ra, rm = call(
        residual_kernel, "residual",
        (odd, hb, vb, ha, va, around, plain, source, a2, b2, cond, nu, wide_keep, wide_spread, u0),
        [planes(1, 3, LX)] + [planes(3, 4)] * 6, [padded(3, n)] * 2 + [vmem(3, n)] * 2, 1, [ANY] + [VMEM] * 6,
    )
    sb = rb + later(lb, 1)
    hb = from_b(sb)
    around, plain = later_parts(lm, 1)
    moved, around = fence((later(la, 1), around))
    sa = ra + moved
    ha = from_a(sa)
    sm = rm + (around + plain)
    lb, la, lm = call(
        square_kernel, "square", (odd, hb, sb, ha, sa, sm, keep, spread),
        [planes(3, 4)] * 3, [padded(3, n)] * 2 + [vmem(3, n)],
    )
    tb = sb + later(lb, 2)
    near_b = from_b(tb)
    tm = sm + later(lm, 2)
    far_b = from_b(tm)
    around, plain = later_parts(la, 2)
    ta = sa + (around + plain)
    near_a = from_a(ta)
    far_a = from_a(tm)
    lb, la, lm, bb, ba, bm = call(
        fourth_kernel, "fourth",
        (odd, near_b, tb, far_b, tm, far_a, near_a, ta, u0, wide_keep, wide_spread),
        [planes(3, 4)] * 6, [padded(3, LX + 16)] * 2 + [vmem(3, LX + 16)],
    )
    eb, edge = call(
        edge_kernel, "edge", (odd, bb, later(lb, half)), [planes(3, 4), planes(3, 2)], [],
    )
    hb = from_b(edge)
    moved, hb = fence((later(la, half), hb))
    ea = ba + moved
    ha = from_a(ea)
    em = bm + later(lm, half)
    field = call(
        last_kernel, "last", (odd, hb, eb, ha, ea, em, source, a1, b1, cond, nu),
        planes(2, 3, LX), [padded(3, n)] * 2 + [vmem(3, n)] * 2, 5, ANY,
    )
    return field, residual


def solution(mesh):
    whole = P("tm", None, "space", None, None)
    return jax.shard_map(
        body, mesh=mesh, in_specs=(whole, whole, P("space", None, None), P(), P()),
        out_specs=(whole, whole), check_vma=False,
    )
```

```python
import jax
import jax.numpy as jnp
from jax import lax
from jax.experimental import pallas as pl
from jax.experimental.pallas import tpu as pltpu
from jax.sharding import PartitionSpec as P

LX, NY, NZ = 12, 64, 128
ROWS = pl.ds(8, NY)
F32 = jnp.float32
ANY = pl.BlockSpec(memory_space=pl.ANY)
HBM = pl.BlockSpec(memory_space=pltpu.HBM)
VMEM = pl.BlockSpec(memory_space=pltpu.VMEM)
SMEM = pl.BlockSpec(memory_space=pltpu.SMEM)


def planes(*lead):
    return jax.ShapeDtypeStruct(tuple(lead) + (NY, NZ), F32)


def vmem(*lead):
    return pltpu.VMEM(tuple(lead) + (NY, NZ), F32)


def padded(*lead):
    return pltpu.VMEM(tuple(lead) + (NY + 16, NZ), F32)


def clear(*bufs):
    zero = jnp.zeros((8, NZ), F32)

    def body(i, carry):
        for buf in bufs:
            for c in range(3):
                buf[c, i, pl.ds(0, 8)] = zero
                buf[c, i, pl.ds(NY + 8, 8)] = zero
        return carry

    lax.fori_loop(0, bufs[0].shape[1], body, 0)


def copy_all(pairs, sems, base=0):
    copies = [
        pltpu.make_async_copy(src, dst, sems.at[base + n]) for n, (src, dst) in enumerate(pairs)
    ]
    for copy in copies:
        copy.start()
    return copies


def wait_all(copies):
    for copy in copies:
        copy.wait()


def run_copies(pairs, sems, base=0):
    wait_all(copy_all(pairs, sems, base))


def call(kernel, name, args, outs, scratch, n_sems=0, out_specs=None, in_place=VMEM):
    in_specs = [SMEM if a.ndim == 1 else in_place for a in args]
    single = not isinstance(outs, (list, tuple))
    return pl.pallas_call(
        kernel,
        name=name,
        out_shape=outs,
        in_specs=in_specs,
        out_specs=out_specs or (VMEM if single else [VMEM] * len(outs)),
        scratch_shapes=list(scratch) + [pltpu.SemaphoreType.DMA((n_sems,))] * (n_sems > 0),
        compiler_params=pltpu.CompilerParams(vmem_limit_bytes=20 * 1024 * 1024),
        cost_estimate=pl.CostEstimate(flops=0, bytes_accessed=4 << 20, transcendentals=0),
    )(*args)


def over_layers(lo, hi, step, at_once):
    rounds = (hi - lo) // at_once

    def body(t, carry):
        for k in range(at_once):
            step(lo + t * at_once + k)
        return carry

    lax.fori_loop(0, rounds, body, 0)
    for i in range(lo + rounds * at_once, hi):
        step(i)


def neighbours(src, c, i):
    lane = lax.broadcasted_iota(jnp.int32, (NY, NZ), 1)
    zero = jnp.float32(0.0)
    if src.shape[-2] == NY:
        row = lax.broadcasted_iota(jnp.int32, (NY, NZ), 0)
        a = src[c, i]
        first = src[c, i + 1] + src[c, i - 1]
        up = jnp.where(row == 0, zero, pltpu.roll(a, 1, 0))
        down = jnp.where(row == NY - 1, zero, pltpu.roll(a, NY - 1, 0))
    else:
        a = src[c, i, ROWS]
        first = src[c, i + 1, ROWS] + src[c, i - 1, ROWS]
        up = src[c, i, pl.ds(7, NY)]
        down = src[c, i, pl.ds(9, NY)]
    left = jnp.where(lane == 0, zero, pltpu.roll(a, 1, 1))
    right = jnp.where(lane == NZ - 1, zero, pltpu.roll(a, NZ - 1, 1))
    return (first + (up + down)) + (left + right)


def layer(src, c, i):
    return src[c, i] if src.shape[-2] == NY else src[c, i, ROWS]


def fine_sweep(src, store, held, cond, nu, lo, hi, force=None, off=0):
    def step(i):
        state = [layer(src, c, i) for c in range(3)]
        square = state[0] * state[0] + state[1] * state[1] + state[2] * state[2]
        base = nu[i - off]
        weight = cond[i - off]
        grown = 1.0 + square
        strong = base * (1.0 + 1.5 * square)
        scale = 1.0 / (weight * grown + 6.0 * strong)
        keep = grown * scale
        spread = strong * scale
        for c in range(3):
            if force is not None:
                fixed = weight * state[c] + force[c, i]
                held[c, i] = fixed
            else:
                fixed = held[c, i]
            store(c, i, fixed * keep + neighbours(src, c, i) * spread)

    over_layers(lo, hi, step, 6)


def coarse_sweep(src, dst, held, keep, spread, off, lo, hi, first):
    def step(i):
        k = keep[i + off]
        s = spread[i + off]
        for c in range(3):
            if first:
                fixed = k * src[c, i, ROWS]
                held[c, i] = fixed
            else:
                fixed = held[c, i]
            dst[c, i, ROWS] = fixed + s * neighbours(src, c, i)

    over_layers(lo, hi, step, 6)


def lookup(code, table):
    first = jnp.where(code == 1, table[0], table[1])
    second = jnp.where(code == 3, table[2], table[3])
    return jnp.where(code <= 2, first, second)


def materials(code, cond_t, nu_t):
    outside = code == 0
    return (
        jnp.where(outside, jnp.float32(1.0), lookup(code, cond_t)),
        jnp.where(outside, jnp.float32(0.0), lookup(code, nu_t)),
    )


def into(buf):
    def store(c, i, value):
        buf[c, i, ROWS] = value
    return store


def edges(odd, n, width):
    return (1 - odd) * (n - width), odd * (n - width)


def first_pack_kernel(odd_ref, g_low, g_high, s_low, s_high, r_low, r_high, a1, b1):
    odd = odd_ref[0]

    def fill(low, high):
        for c in range(3):
            for k in range(2):
                low[2 * c + k] = g_low[0, c, k]
                high[2 * c + k] = g_high[0, c, k]
            low[6 + c] = s_low[0, c, 0]
            high[6 + c] = s_high[0, c, 0]
        low[9] = (r_low[0] + 1).astype(F32)
        high[9] = (r_high[0] + 1).astype(F32)

    @pl.when(odd == 0)
    def even_slab():
        fill(b1, a1)

    @pl.when(odd == 1)
    def odd_slab():
        fill(a1, b1)


def second_pack_kernel(odd_ref, source, regions, a2, b2, a3, b3, reg, sems):
    odd = odd_ref[0]
    pairs = [(regions, reg)]
    for two, start in zip((a2, b2), edges(odd, LX, 3)):
        for c in range(3):
            pairs.append((source.at[0, c, pl.ds(start, 3)], two.at[pl.ds(3 * c, 3)]))
    run_copies(pairs, sems)
    for two, start in zip((a2, b2), edges(odd, LX, 3)):
        for k in range(3):
            two[9 + k] = (reg[start + k] + 1).astype(F32)
    for three, high in ((a3, 1 - odd), (b3, odd)):
        for k in range(4):
            three[k] = (reg[high * (LX - 7) + (1 - high) * 3 + k] + 1).astype(F32)


def first_middle_kernel(cond_t, nu_t, guess, source, regions, out, y, held, cond, nu):
    def prepare(i):
        cond[i], nu[i] = materials(regions[i] + 1, cond_t, nu_t)

    over_layers(3, 9, prepare, 6)
    clear(y)
    fine_sweep(guess.at[0], into(y), held, cond, nu, 3, 9, source.at[1])

    def store(c, i, value):
        out[c, i - 4] = value

    fine_sweep(y, store, held, cond, nu, 4, 8)


def first_kernel(odd_ref, cond_t, nu_t, guess, source, regions, ra, rb, after, out_a, out_b, x, y, held, f, cond, nu):
    odd = odd_ref[0]
    clear(x, y)
    n = LX + 4
    for c in range(3):
        for i in (0, 1, 2, 3, 4, 5, 6, 7, 8, 9, 10, 11):
            x[c, i + 2, ROWS] = guess[0, c, i]
            f[c, i + 2] = source[1, c, i]
    for i in range(LX):
        cond[i + 2], nu[i + 2] = materials(regions[i] + 1, cond_t, nu_t)
    for pack, high in ((ra, 1 - odd), (rb, odd)):
        for c in range(3):
            for k in range(2):
                x[c, high * (n - 2) + k, ROWS] = pack[2 * c + k]
            f[c, 1 + high * (n - 3)] = pack[6 + c]
        cond[1 + high * (n - 3)], nu[1 + high * (n - 3)] = materials(pack[9], cond_t, nu_t)
    fine_sweep(x, into(y), held, cond, nu, 1, 7, f)
    fine_sweep(x, into(y), held, cond, nu, 9, n - 1, f)
    fine_sweep(y, into(x), held, cond, nu, 2, 6)
    fine_sweep(y, into(x), held, cond, nu, 10, 14)
    for c in range(3):
        for k in range(4):
            out_a[c, k] = x[c, 2 + (1 - odd) * 8 + k, ROWS]
            out_b[c, k] = x[c, 2 + odd * 8 + k, ROWS]


def material_kernel(odd_ref, cond_t, nu_t, regions, ra, rb, cond, nu, keep, spread):
    odd = odd_ref[0]

    def fill(at, code):
        cv, nv = materials(code, cond_t, nu_t)
        cond[at] = cv
        nu[at] = nv
        half = 0.5 * cv
        scale = 1.0 / (half + 6.0 * nv)
        keep[at] = half * scale
        spread[at] = nv * scale

    for i in range(LX):
        fill(3 + i, regions[i] + 1)
    for pack, high in ((ra, 1 - odd), (rb, odd)):
        for k in range(3):
            fill(high * (LX + 3) + k, pack[9 + k])


def wide_kernel(odd_ref, cond_t, nu_t, keep_i, spread_i, ra, rb, keep, spread):
    odd = odd_ref[0]
    for i in range(LX + 6):
        keep[i + 4] = keep_i[i]
        spread[i + 4] = spread_i[i]
    for pack, start, high in ((ra, 0, 1 - odd), (rb, 12, odd)):
        for k in range(4):
            at = high * (LX + 10) + k
            cv, nv = materials(pack[start + k], cond_t, nu_t)
            half = 0.5 * cv
            scale = 1.0 / (half + 6.0 * nv)
            keep[at] = half * scale
            spread[at] = nv * scale


def extend(odd, pieces, halos, x):
    a, b, *m = pieces
    ha, hb = halos
    for c in range(3):
        for k in range(4):
            middle = m[0][c, k]
            for other in m[1:]:
                middle = middle + other[c, k]
            x[c, 8 + k, ROWS] = middle
            x[c, 4 + (1 - odd) * 8 + k, ROWS] = a[c, k]
            x[c, 4 + odd * 8 + k, ROWS] = b[c, k]
            x[c, (1 - odd) * 16 + k, ROWS] = ha[c, k]
            x[c, odd * 16 + k, ROWS] = hb[c, k] if len(hb.shape) == 4 else hb[4 * c + k]


def extend_force(odd, source, which, width, packs, start, f):
    for c in range(3):
        for i in range(LX):
            f[c, 4 + i] = source[which, c, i]
        for pack, high in ((packs[0], 1 - odd), (packs[1], odd)):
            for k in range(width):
                f[c, 4 - width + high * (LX + width) + k] = pack[start + width * c + k]


def second_kernel(
    odd_ref, hb, vb, ha, va, vm, vn, source, a1, b1, a2, b2, cond, nu,
    u0, oa, ob, om, x, y, held, f0, f1,
):
    odd = odd_ref[0]
    clear(x, y)
    extend(odd, (va, vb, vm, vn), (ha, hb), x)
    extend_force(odd, source, 0, 3, (a2, b2), 0, f0)
    extend_force(odd, source, 1, 1, (a1, b1), 6, f1)

    def keep_u0(c, i, value):
        x[c, i, ROWS] = value
        u0[c, i - 2] = value

    fine_sweep(x, into(y), held, cond, nu, 1, 19, f0, 1)
    fine_sweep(y, keep_u0, held, cond, nu, 2, 18, None, 1)
    fine_sweep(x, into(y), held, cond, nu, 3, 17, f1, 1)
    fine_sweep(y, into(x), held, cond, nu, 4, 16, None, 1)
    for c in range(3):
        for k in range(4):
            om[c, k] = x[c, 8 + k, ROWS]
            oa[c, k] = x[c, 4 + (1 - odd) * 8 + k, ROWS]
            ob[c, k] = x[c, 4 + odd * 8 + k, ROWS]


def split(odd, x, start, b, a, m):
    for c in range(3):
        for k in range(4):
            b[c, k] = x[c, start + odd * 8 + k, ROWS]
            a[c, k] = x[c, start + (1 - odd) * 8 + k, ROWS]
            m[c, k] = x[c, start + 4 + k, ROWS]


def residual_kernel(
    odd_ref, hb, vb, ha, va, vm, vn, source, a2, b2, cond, nu, keep, spread, u0,
    res_o, lb, la, lm, rb, ra, rm, x, y, held, f0, sems,
):
    odd = odd_ref[0]
    clear(x, y)
    extend(odd, (va, vb, vm, vn), (ha, hb), x)
    extend_force(odd, source, 0, 3, (a2, b2), 0, f0)

    def less(c, i, value):
        x[c, i, ROWS] = value - u0[c, i - 2]

    fine_sweep(x, into(y), held, cond, nu, 1, 19, f0, 1)
    fine_sweep(y, less, held, cond, nu, 2, 18, None, 1)
    kept = copy_all([(x.at[:, pl.ds(4, LX), ROWS], res_o.at[0])], sems)
    split(odd, x, 4, rb, ra, rm)
    coarse_sweep(x, y, held, keep, spread, -1, 3, 17, True)
    wait_all(kept)
    coarse_sweep(y, x, held, keep, spread, -1, 4, 16, False)
    split(odd, x, 4, lb, la, lm)


def square_kernel(odd_ref, hb, sb, ha, sa, sm, keep, spread, ob, oa, om, x, y, held):
    odd = odd_ref[0]
    clear(x, y)
    extend(odd, (sa, sb, sm), (ha, hb), x)
    for lo in (1, 3):
        coarse_sweep(x, y, held, keep, spread, -1, lo, 20 - lo, True)
        coarse_sweep(y, x, held, keep, spread, -1, lo + 1, 19 - lo, False)
    split(odd, x, 4, ob, oa, om)


def fourth_kernel(
    odd_ref, near_b, tb, far_b, tm, far_a, near_a, ta, u0, keep, spread,
    ob, oa, om, bb, ba, bm, x, y, held,
):
    odd = odd_ref[0]
    clear(x, y)
    for c in range(3):
        for k in range(4):
            x[c, 8 + odd * 8 + k, ROWS] = tb[c, k]
            x[c, 8 + (1 - odd) * 8 + k, ROWS] = ta[c, k]
            x[c, 12 + k, ROWS] = tm[c, k]
            x[c, 4 + odd * 16 + k, ROWS] = near_b[c, k]
            x[c, 4 + (1 - odd) * 16 + k, ROWS] = near_a[c, k]
            x[c, odd * 24 + k, ROWS] = far_b[c, k]
            x[c, (1 - odd) * 24 + k, ROWS] = far_a[c, k]
    for c in range(3):
        for k in range(4):
            bb[c, k] = tb[c, k] + u0[c, 2 + odd * 8 + k]
            ba[c, k] = ta[c, k] + u0[c, 2 + (1 - odd) * 8 + k]
            bm[c, k] = tm[c, k] + u0[c, 6 + k]
    for lo in (1, 3, 5, 7):
        coarse_sweep(x, y, held, keep, spread, -1, lo, 28 - lo, True)
        coarse_sweep(y, x, held, keep, spread, -1, lo + 1, 27 - lo, False)
    split(odd, x, 8, ob, oa, om)


def edge_kernel(odd_ref, base, moved, total, edge):
    odd = odd_ref[0]
    for c in range(3):
        for k in range(4):
            total[c, k] = base[c, k] + moved[c, k]
        for k in range(2):
            edge[c, k] = total[c, odd * 2 + k]


def last_kernel(
    odd_ref, hb, eb, ha, ea, em, source, a1, b1, cond, nu, field, x, y, held, f1, sems,
):
    odd = odd_ref[0]
    clear(x, y)
    kept = copy_all(
        [
            (eb, field.at[0, :, pl.ds(odd * 8, 4)]),
            (ea, field.at[0, :, pl.ds((1 - odd) * 8, 4)]),
            (em, field.at[0, :, pl.ds(4, 4)]),
        ],
        sems,
    )
    extend_force(odd, source, 1, 1, (a1, b1), 6, f1)
    for c in range(3):
        for k in range(4):
            x[c, 4 + odd * 8 + k, ROWS] = eb[c, k]
            x[c, 4 + (1 - odd) * 8 + k, ROWS] = ea[c, k]
            x[c, 8 + k, ROWS] = em[c, k]
        for k in range(2):
            x[c, 2 + odd * 14 + k, ROWS] = hb[c, k]
            x[c, 2 + (1 - odd) * 14 + k, ROWS] = ha[c, odd * 2 + k]
    fine_sweep(x, into(y), held, cond, nu, 3, 17, f1, 1)
    fine_sweep(y, into(x), held, cond, nu, 4, 10, None, 1)
    kept += copy_all([(x.at[:, pl.ds(4, 6), ROWS], field.at[1, :, pl.ds(0, 6)])], sems, 3)
    fine_sweep(y, into(x), held, cond, nu, 10, 16, None, 1)
    kept += copy_all([(x.at[:, pl.ds(10, 6), ROWS], field.at[1, :, pl.ds(6, 6)])], sems, 4)
    wait_all(kept)


def body(guess, source, regions, conductance, reluct):
    slices = lax.axis_size("tm")
    slabs = lax.axis_size("space")
    odd = (lax.axis_index("space") % 2).astype(jnp.int32).reshape(1)
    on_chip = [(i, i ^ 1) for i in range(slabs)]
    off_chip = [(i, i + 1) for i in range(1, slabs - 1, 2)]
    off_chip += [(j, i) for i, j in off_chip]
    fence = lax.optimization_barrier

    def from_a(x):
        return lax.ppermute(x, "space", on_chip)

    def from_b(x):
        return lax.ppermute(x, "space", off_chip)

    half = slices // 2

    def along(x, pairs):
        return lax.ppermute(x, "tm", pairs)

    def later(x, distance):
        return along(x, [(i, (i + distance) % slices) for i in range(slices)])

    def later_parts(x, distance):
        wrapping = [i for i in range(slices) if i % half + distance >= half]
        across = along(x, [(i, (i + half) % slices) for i in wrapping])
        around = along(across, [((i + half) % slices, (i + distance) % slices) for i in wrapping])
        plain = along(x, [(i, i + distance) for i in range(slices) if i not in wrapping])
        return around, plain

    tables = (conductance, reluct)
    sa1, sb1 = call(
        first_pack_kernel, "first_pack",
        (odd, guess[:1, :, :2], guess[:1, :, LX - 2:], source[1:, :, :1], source[1:, :, LX - 1:], regions[:1], regions[LX - 1:]),
        [planes(10), planes(10)], [],
    )
    b1 = from_b(sb1)
    a1 = from_a(sa1)
    um = call(
        first_middle_kernel, "first_middle", (*tables, guess, source, regions),
        planes(3, 4), [padded(3, LX), vmem(3, LX)] + [vmem(LX)] * 2,
    )
    sa2, sb2, sa3, sb3 = call(
        second_pack_kernel, "second_pack", (odd, source, regions),
        [planes(12), planes(12), planes(4), planes(4)], [pltpu.VMEM((LX, NY, NZ), jnp.int32)], 8, in_place=HBM,
    )
    vm = later_parts(um, 1)
    sb2, sa2, b1 = fence((sb2, sa2, b1))
    b2 = from_b(sb2)
    a2 = from_a(sa2)
    ua, ub = call(
        first_kernel, "first", (odd, *tables, guess, source, regions, a1, b1, um),
        [planes(3, 4), planes(3, 4)], [padded(3, LX + 4)] * 2 + [vmem(3, LX + 4)] * 2 + [vmem(LX + 4)] * 2,
    )
    vb = later(ub, 1)
    va = later(ua, 1)
    cond, nu, keep, spread = call(
        material_kernel, "material", (odd, *tables, regions, a2, b2), [planes(LX + 6)] * 4, [],
    )
    vb, cond = fence((vb, cond))
    hb = from_b(vb)
    va, *vm = fence((va, *vm))
    ha = from_a(va)
    n = LX + 8
    u0, ua, ub, um = call(
        second_kernel, "second",
        (odd, hb, vb, ha, va, *vm, source, a1, b1, a2, b2, cond, nu),
        [planes(3, LX + 4), planes(3, 4), planes(3, 4), planes(3, 4)], [padded(3, n)] * 2 + [vmem(3, n)] * 3,
    )
    vb = later(ub, 1)
    va = later(ua, 1)
    around, plain = later_parts(um, 1)
    hb = from_b(vb)
    va, around = fence((va, around))
    ha = from_a(va)
    residual, lb, la, lm, rb, ra, rm = call(
        residual_kernel, "residual",
        (odd, hb, vb, ha, va, around, plain, source, a2, b2, cond, nu, keep, spread, u0),
        [planes(1, 3, LX)] + [planes(3, 4)] * 6, [padded(3, n)] * 2 + [vmem(3, n)] * 2, 1, [ANY] + [VMEM] * 6,
    )
    sb = rb + later(lb, 1)
    hb = from_b(jnp.concatenate([sb.reshape(12, NY, NZ), sb3], axis=0))
    sa3, sb = fence((sa3, sb))
    a3 = from_a(sa3)
    wide_keep, wide_spread = call(
        wide_kernel, "wide", (odd, *tables, keep, spread, a3, hb), [planes(LX + 14)] * 2, [],
    )
    around, plain = later_parts(lm, 1)
    moved, around = fence((later(la, 1), around))
    sa = ra + moved
    ha = from_a(sa)
    sm = rm + (around + plain)
    lb, la, lm = call(
        square_kernel, "square", (odd, hb, sb, ha, sa, sm, keep, spread),
        [planes(3, 4)] * 3, [padded(3, n)] * 2 + [vmem(3, n)],
    )
    tb = sb + later(lb, 2)
    near_b = from_b(tb)
    tm = sm + later(lm, 2)
    far_b = from_b(tm)
    around, plain = later_parts(la, 2)
    ta = sa + (around + plain)
    near_a = from_a(ta)
    far_a = from_a(tm)
    lb, la, lm, bb, ba, bm = call(
        fourth_kernel, "fourth",
        (odd, near_b, tb, far_b, tm, far_a, near_a, ta, u0, wide_keep, wide_spread),
        [planes(3, 4)] * 6, [padded(3, LX + 16)] * 2 + [vmem(3, LX + 16)],
    )
    eb, edge = call(
        edge_kernel, "edge", (odd, bb, later(lb, half)), [planes(3, 4), planes(3, 2)], [],
    )
    hb = from_b(edge)
    moved, hb = fence((later(la, half), hb))
    ea = ba + moved
    ha = from_a(ea)
    em = bm + later(lm, half)
    field = call(
        last_kernel, "last", (odd, hb, eb, ha, ea, em, source, a1, b1, cond, nu),
        planes(2, 3, LX), [padded(3, n)] * 2 + [vmem(3, n)] * 2, 5, ANY,
    )
    return field, residual


def solution(mesh):
    whole = P("tm", None, "space", None, None)
    return jax.shard_map(
        body, mesh=mesh, in_specs=(whole, whole, P("space", None, None), P(), P()),
        out_specs=(whole, whole), check_vma=False,
    )
```

```python
import jax
import jax.numpy as jnp
from jax import lax
from jax.experimental import pallas as pl
from jax.experimental.pallas import tpu as pltpu
from jax.sharding import PartitionSpec as P

LX, NY, NZ = 12, 64, 128
ROWS = pl.ds(8, NY)
F32 = jnp.float32
ANY = pl.BlockSpec(memory_space=pl.ANY)
HBM = pl.BlockSpec(memory_space=pltpu.HBM)
VMEM = pl.BlockSpec(memory_space=pltpu.VMEM)
SMEM = pl.BlockSpec(memory_space=pltpu.SMEM)


def planes(*lead):
    return jax.ShapeDtypeStruct(tuple(lead) + (NY, NZ), F32)


def vmem(*lead):
    return pltpu.VMEM(tuple(lead) + (NY, NZ), F32)


def padded(*lead):
    return pltpu.VMEM(tuple(lead) + (NY + 16, NZ), F32)


def clear(*bufs):
    zero = jnp.zeros((8, NZ), F32)

    def body(i, carry):
        for buf in bufs:
            for c in range(3):
                buf[c, i, pl.ds(0, 8)] = zero
                buf[c, i, pl.ds(NY + 8, 8)] = zero
        return carry

    lax.fori_loop(0, bufs[0].shape[1], body, 0)


def copy_all(pairs, sems, base=0):
    copies = [
        pltpu.make_async_copy(src, dst, sems.at[base + n]) for n, (src, dst) in enumerate(pairs)
    ]
    for copy in copies:
        copy.start()
    return copies


def wait_all(copies):
    for copy in copies:
        copy.wait()


def run_copies(pairs, sems, base=0):
    wait_all(copy_all(pairs, sems, base))


def call(kernel, name, args, outs, scratch, n_sems=0, out_specs=None, in_place=VMEM):
    in_specs = [SMEM if a.ndim == 1 else in_place for a in args]
    single = not isinstance(outs, (list, tuple))
    return pl.pallas_call(
        kernel,
        name=name,
        out_shape=outs,
        in_specs=in_specs,
        out_specs=out_specs or (VMEM if single else [VMEM] * len(outs)),
        scratch_shapes=list(scratch) + [pltpu.SemaphoreType.DMA((n_sems,))] * (n_sems > 0),
        compiler_params=pltpu.CompilerParams(vmem_limit_bytes=20 * 1024 * 1024),
        cost_estimate=pl.CostEstimate(flops=0, bytes_accessed=4 << 20, transcendentals=0),
    )(*args)


def over_layers(lo, hi, step, at_once):
    rounds = (hi - lo) // at_once

    def body(t, carry):
        for k in range(at_once):
            step(lo + t * at_once + k)
        return carry

    lax.fori_loop(0, rounds, body, 0)
    for i in range(lo + rounds * at_once, hi):
        step(i)


def neighbours(src, c, i):
    lane = lax.broadcasted_iota(jnp.int32, (NY, NZ), 1)
    zero = jnp.float32(0.0)
    if src.shape[-2] == NY:
        row = lax.broadcasted_iota(jnp.int32, (NY, NZ), 0)
        a = src[c, i]
        first = src[c, i + 1] + src[c, i - 1]
        up = jnp.where(row == 0, zero, pltpu.roll(a, 1, 0))
        down = jnp.where(row == NY - 1, zero, pltpu.roll(a, NY - 1, 0))
    else:
        a = src[c, i, ROWS]
        first = src[c, i + 1, ROWS] + src[c, i - 1, ROWS]
        up = src[c, i, pl.ds(7, NY)]
        down = src[c, i, pl.ds(9, NY)]
    left = jnp.where(lane == 0, zero, pltpu.roll(a, 1, 1))
    right = jnp.where(lane == NZ - 1, zero, pltpu.roll(a, NZ - 1, 1))
    return (first + (up + down)) + (left + right)


def layer(src, c, i):
    return src[c, i] if src.shape[-2] == NY else src[c, i, ROWS]


def fine_sweep(src, store, held, cond, nu, lo, hi, force=None, off=0):
    def step(i):
        state = [layer(src, c, i) for c in range(3)]
        square = state[0] * state[0] + state[1] * state[1] + state[2] * state[2]
        base = nu[i - off]
        weight = cond[i - off]
        grown = 1.0 + square
        strong = base * (1.0 + 1.5 * square)
        scale = 1.0 / (weight * grown + 6.0 * strong)
        keep = grown * scale
        spread = strong * scale
        for c in range(3):
            if force is not None:
                fixed = weight * state[c] + force[c, i]
                held[c, i] = fixed
            else:
                fixed = held[c, i]
            store(c, i, fixed * keep + neighbours(src, c, i) * spread)

    over_layers(lo, hi, step, (hi - lo) // 2 if hi - lo >= 12 else 6)


def coarse_sweep(src, dst, held, keep, spread, off, lo, hi, first):
    def step(i):
        k = keep[i + off]
        s = spread[i + off]
        for c in range(3):
            if first:
                fixed = k * src[c, i, ROWS]
                held[c, i] = fixed
            else:
                fixed = held[c, i]
            dst[c, i, ROWS] = fixed + s * neighbours(src, c, i)

    over_layers(lo, hi, step, (hi - lo) // 2 if hi - lo >= 12 else 6)


def lookup(code, table):
    first = jnp.where(code == 1, table[0], table[1])
    second = jnp.where(code == 3, table[2], table[3])
    return jnp.where(code <= 2, first, second)


def materials(code, cond_t, nu_t):
    outside = code == 0
    return (
        jnp.where(outside, jnp.float32(1.0), lookup(code, cond_t)),
        jnp.where(outside, jnp.float32(0.0), lookup(code, nu_t)),
    )


def into(buf):
    def store(c, i, value):
        buf[c, i, ROWS] = value
    return store


def edges(odd, n, width):
    return (1 - odd) * (n - width), odd * (n - width)


def first_pack_kernel(odd_ref, g_low, g_high, s_low, s_high, r_low, r_high, a1, b1):
    odd = odd_ref[0]

    def fill(low, high):
        for c in range(3):
            for k in range(2):
                low[2 * c + k] = g_low[0, c, k]
                high[2 * c + k] = g_high[0, c, k]
            low[6 + c] = s_low[0, c, 0]
            high[6 + c] = s_high[0, c, 0]
        low[9] = (r_low[0] + 1).astype(F32)
        high[9] = (r_high[0] + 1).astype(F32)

    @pl.when(odd == 0)
    def even_slab():
        fill(b1, a1)

    @pl.when(odd == 1)
    def odd_slab():
        fill(a1, b1)


def second_pack_kernel(odd_ref, source, regions, a2, b2, a3, b3, reg, sems):
    odd = odd_ref[0]
    pairs = [(regions, reg)]
    for two, start in zip((a2, b2), edges(odd, LX, 3)):
        for c in range(3):
            pairs.append((source.at[0, c, pl.ds(start, 3)], two.at[pl.ds(3 * c, 3)]))
    run_copies(pairs, sems)
    for two, start in zip((a2, b2), edges(odd, LX, 3)):
        for k in range(3):
            two[9 + k] = (reg[start + k] + 1).astype(F32)
    for three, high in ((a3, 1 - odd), (b3, odd)):
        for k in range(4):
            three[k] = (reg[high * (LX - 7) + (1 - high) * 3 + k] + 1).astype(F32)


def first_middle_kernel(cond_t, nu_t, guess, source, regions, out, y, held, cond, nu):
    def prepare(i):
        cond[i], nu[i] = materials(regions[i] + 1, cond_t, nu_t)

    over_layers(3, 9, prepare, 6)
    clear(y)
    fine_sweep(guess.at[0], into(y), held, cond, nu, 3, 9, source.at[1])

    def store(c, i, value):
        out[c, i - 4] = value

    fine_sweep(y, store, held, cond, nu, 4, 8)


def first_kernel(odd_ref, cond_t, nu_t, guess, source, regions, ra, rb, after, out_a, out_b, x, y, held, f, cond, nu):
    odd = odd_ref[0]
    clear(x, y)
    n = LX + 4
    for c in range(3):
        for i in (0, 1, 2, 3, 4, 5, 6, 7, 8, 9, 10, 11):
            x[c, i + 2, ROWS] = guess[0, c, i]
            f[c, i + 2] = source[1, c, i]
    for i in range(LX):
        cond[i + 2], nu[i + 2] = materials(regions[i] + 1, cond_t, nu_t)
    for pack, high in ((ra, 1 - odd), (rb, odd)):
        for c in range(3):
            for k in range(2):
                x[c, high * (n - 2) + k, ROWS] = pack[2 * c + k]
            f[c, 1 + high * (n - 3)] = pack[6 + c]
        cond[1 + high * (n - 3)], nu[1 + high * (n - 3)] = materials(pack[9], cond_t, nu_t)
    fine_sweep(x, into(y), held, cond, nu, 1, 7, f)
    fine_sweep(x, into(y), held, cond, nu, 9, n - 1, f)
    fine_sweep(y, into(x), held, cond, nu, 2, 6)
    fine_sweep(y, into(x), held, cond, nu, 10, 14)
    for c in range(3):
        for k in range(4):
            out_a[c, k] = x[c, 2 + (1 - odd) * 8 + k, ROWS]
            out_b[c, k] = x[c, 2 + odd * 8 + k, ROWS]


def material_kernel(odd_ref, cond_t, nu_t, regions, ra, rb, cond, nu, keep, spread):
    odd = odd_ref[0]

    def fill(at, code):
        cv, nv = materials(code, cond_t, nu_t)
        cond[at] = cv
        nu[at] = nv
        half = 0.5 * cv
        scale = 1.0 / (half + 6.0 * nv)
        keep[at] = half * scale
        spread[at] = nv * scale

    for i in range(LX):
        fill(3 + i, regions[i] + 1)
    for pack, high in ((ra, 1 - odd), (rb, odd)):
        for k in range(3):
            fill(high * (LX + 3) + k, pack[9 + k])


def wide_kernel(odd_ref, cond_t, nu_t, keep_i, spread_i, ra, rb, keep, spread):
    odd = odd_ref[0]
    for i in range(LX + 6):
        keep[i + 4] = keep_i[i]
        spread[i + 4] = spread_i[i]
    for pack, start, high in ((ra, 0, 1 - odd), (rb, 12, odd)):
        for k in range(4):
            at = high * (LX + 10) + k
            cv, nv = materials(pack[start + k], cond_t, nu_t)
            half = 0.5 * cv
            scale = 1.0 / (half + 6.0 * nv)
            keep[at] = half * scale
            spread[at] = nv * scale


def extend(odd, pieces, halos, x):
    a, b, *m = pieces
    ha, hb = halos
    for c in range(3):
        for k in range(4):
            middle = m[0][c, k]
            for other in m[1:]:
                middle = middle + other[c, k]
            x[c, 8 + k, ROWS] = middle
            x[c, 4 + (1 - odd) * 8 + k, ROWS] = a[c, k]
            x[c, 4 + odd * 8 + k, ROWS] = b[c, k]
            x[c, (1 - odd) * 16 + k, ROWS] = ha[c, k]
            x[c, odd * 16 + k, ROWS] = hb[c, k] if len(hb.shape) == 4 else hb[4 * c + k]


def extend_force(odd, source, which, width, packs, start, f):
    for c in range(3):
        for i in range(LX):
            f[c, 4 + i] = source[which, c, i]
        for pack, high in ((packs[0], 1 - odd), (packs[1], odd)):
            for k in range(width):
                f[c, 4 - width + high * (LX + width) + k] = pack[start + width * c + k]


def second_kernel(
    odd_ref, hb, vb, ha, va, vm, vn, source, a1, b1, a2, b2, cond, nu,
    u0, oa, ob, om, x, y, held, f0, f1,
):
    odd = odd_ref[0]
    clear(x, y)
    extend(odd, (va, vb, vm, vn), (ha, hb), x)
    extend_force(odd, source, 0, 3, (a2, b2), 0, f0)
    extend_force(odd, source, 1, 1, (a1, b1), 6, f1)

    def keep_u0(c, i, value):
        x[c, i, ROWS] = value
        u0[c, i - 2] = value

    fine_sweep(x, into(y), held, cond, nu, 1, 19, f0, 1)
    fine_sweep(y, keep_u0, held, cond, nu, 2, 18, None, 1)
    fine_sweep(x, into(y), held, cond, nu, 3, 17, f1, 1)
    fine_sweep(y, into(x), held, cond, nu, 4, 16, None, 1)
    for c in range(3):
        for k in range(4):
            om[c, k] = x[c, 8 + k, ROWS]
            oa[c, k] = x[c, 4 + (1 - odd) * 8 + k, ROWS]
            ob[c, k] = x[c, 4 + odd * 8 + k, ROWS]


def split(odd, x, start, b, a, m):
    for c in range(3):
        for k in range(4):
            b[c, k] = x[c, start + odd * 8 + k, ROWS]
            a[c, k] = x[c, start + (1 - odd) * 8 + k, ROWS]
            m[c, k] = x[c, start + 4 + k, ROWS]


def residual_kernel(
    odd_ref, hb, vb, ha, va, vm, vn, source, a2, b2, cond, nu, keep, spread, u0,
    res_o, lb, la, lm, rb, ra, rm, x, y, held, f0, sems,
):
    odd = odd_ref[0]
    clear(x, y)
    extend(odd, (va, vb, vm, vn), (ha, hb), x)
    extend_force(odd, source, 0, 3, (a2, b2), 0, f0)

    def less(c, i, value):
        x[c, i, ROWS] = value - u0[c, i - 2]

    fine_sweep(x, into(y), held, cond, nu, 1, 19, f0, 1)
    fine_sweep(y, less, held, cond, nu, 2, 18, None, 1)
    kept = copy_all([(x.at[:, pl.ds(4, LX), ROWS], res_o.at[0])], sems)
    split(odd, x, 4, rb, ra, rm)
    coarse_sweep(x, y, held, keep, spread, -1, 3, 17, True)
    wait_all(kept)
    coarse_sweep(y, x, held, keep, spread, -1, 4, 16, False)
    split(odd, x, 4, lb, la, lm)


def square_kernel(odd_ref, hb, sb, ha, sa, sm, keep, spread, ob, oa, om, x, y, held):
    odd = odd_ref[0]
    clear(x, y)
    extend(odd, (sa, sb, sm), (ha, hb), x)
    for lo in (1, 3):
        coarse_sweep(x, y, held, keep, spread, -1, lo, 20 - lo, True)
        coarse_sweep(y, x, held, keep, spread, -1, lo + 1, 19 - lo, False)
    split(odd, x, 4, ob, oa, om)


def fourth_kernel(
    odd_ref, near_b, tb, far_b, tm, far_a, near_a, ta, u0, keep, spread,
    ob, oa, om, bb, ba, bm, x, y, held,
):
    odd = odd_ref[0]
    clear(x, y)
    for c in range(3):
        for k in range(4):
            x[c, 8 + odd * 8 + k, ROWS] = tb[c, k]
            x[c, 8 + (1 - odd) * 8 + k, ROWS] = ta[c, k]
            x[c, 12 + k, ROWS] = tm[c, k]
            x[c, 4 + odd * 16 + k, ROWS] = near_b[c, k]
            x[c, 4 + (1 - odd) * 16 + k, ROWS] = near_a[c, k]
            x[c, odd * 24 + k, ROWS] = far_b[c, k]
            x[c, (1 - odd) * 24 + k, ROWS] = far_a[c, k]
    for c in range(3):
        for k in range(4):
            bb[c, k] = tb[c, k] + u0[c, 2 + odd * 8 + k]
            ba[c, k] = ta[c, k] + u0[c, 2 + (1 - odd) * 8 + k]
            bm[c, k] = tm[c, k] + u0[c, 6 + k]
    for lo in (1, 3, 5, 7):
        coarse_sweep(x, y, held, keep, spread, -1, lo, 28 - lo, True)
        coarse_sweep(y, x, held, keep, spread, -1, lo + 1, 27 - lo, False)
    split(odd, x, 8, ob, oa, om)


def edge_kernel(odd_ref, base, moved, total, edge):
    odd = odd_ref[0]
    for c in range(3):
        for k in range(4):
            total[c, k] = base[c, k] + moved[c, k]
        for k in range(2):
            edge[c, k] = total[c, odd * 2 + k]


def last_kernel(
    odd_ref, hb, eb, ha, ea, em, source, a1, b1, cond, nu, field, x, y, held, f1, sems,
):
    odd = odd_ref[0]
    clear(x, y)
    kept = copy_all(
        [
            (eb, field.at[0, :, pl.ds(odd * 8, 4)]),
            (ea, field.at[0, :, pl.ds((1 - odd) * 8, 4)]),
            (em, field.at[0, :, pl.ds(4, 4)]),
        ],
        sems,
    )
    extend_force(odd, source, 1, 1, (a1, b1), 6, f1)
    for c in range(3):
        for k in range(4):
            x[c, 4 + odd * 8 + k, ROWS] = eb[c, k]
            x[c, 4 + (1 - odd) * 8 + k, ROWS] = ea[c, k]
            x[c, 8 + k, ROWS] = em[c, k]
        for k in range(2):
            x[c, 2 + odd * 14 + k, ROWS] = hb[c, k]
            x[c, 2 + (1 - odd) * 14 + k, ROWS] = ha[c, odd * 2 + k]
    fine_sweep(x, into(y), held, cond, nu, 3, 17, f1, 1)
    fine_sweep(y, into(x), held, cond, nu, 4, 10, None, 1)
    kept += copy_all([(x.at[:, pl.ds(4, 6), ROWS], field.at[1, :, pl.ds(0, 6)])], sems, 3)
    fine_sweep(y, into(x), held, cond, nu, 10, 16, None, 1)
    kept += copy_all([(x.at[:, pl.ds(10, 6), ROWS], field.at[1, :, pl.ds(6, 6)])], sems, 4)
    wait_all(kept)


def body(guess, source, regions, conductance, reluct):
    slices = lax.axis_size("tm")
    slabs = lax.axis_size("space")
    odd = (lax.axis_index("space") % 2).astype(jnp.int32).reshape(1)
    on_chip = [(i, i ^ 1) for i in range(slabs)]
    off_chip = [(i, i + 1) for i in range(1, slabs - 1, 2)]
    off_chip += [(j, i) for i, j in off_chip]
    fence = lax.optimization_barrier

    def from_a(x):
        return lax.ppermute(x, "space", on_chip)

    def from_b(x):
        return lax.ppermute(x, "space", off_chip)

    half = slices // 2

    def along(x, pairs):
        return lax.ppermute(x, "tm", pairs)

    def later(x, distance):
        return along(x, [(i, (i + distance) % slices) for i in range(slices)])

    def later_parts(x, distance):
        wrapping = [i for i in range(slices) if i % half + distance >= half]
        across = along(x, [(i, (i + half) % slices) for i in wrapping])
        around = along(across, [((i + half) % slices, (i + distance) % slices) for i in wrapping])
        plain = along(x, [(i, i + distance) for i in range(slices) if i not in wrapping])
        return around, plain

    tables = (conductance, reluct)
    sa1, sb1 = call(
        first_pack_kernel, "first_pack",
        (odd, guess[:1, :, :2], guess[:1, :, LX - 2:], source[1:, :, :1], source[1:, :, LX - 1:], regions[:1], regions[LX - 1:]),
        [planes(10), planes(10)], [],
    )
    b1 = from_b(sb1)
    a1 = from_a(sa1)
    um = call(
        first_middle_kernel, "first_middle", (*tables, guess, source, regions),
        planes(3, 4), [padded(3, LX), vmem(3, LX)] + [vmem(LX)] * 2,
    )
    sa2, sb2, sa3, sb3 = call(
        second_pack_kernel, "second_pack", (odd, source, regions),
        [planes(12), planes(12), planes(4), planes(4)], [pltpu.VMEM((LX, NY, NZ), jnp.int32)], 8, in_place=HBM,
    )
    vm = later_parts(um, 1)
    sb2, sa2, b1 = fence((sb2, sa2, b1))
    b2 = from_b(sb2)
    a2 = from_a(sa2)
    ua, ub = call(
        first_kernel, "first", (odd, *tables, guess, source, regions, a1, b1, um),
        [planes(3, 4), planes(3, 4)], [padded(3, LX + 4)] * 2 + [vmem(3, LX + 4)] * 2 + [vmem(LX + 4)] * 2,
    )
    vb = later(ub, 1)
    va = later(ua, 1)
    cond, nu, keep, spread = call(
        material_kernel, "material", (odd, *tables, regions, a2, b2), [planes(LX + 6)] * 4, [],
    )
    vb, cond = fence((vb, cond))
    hb = from_b(vb)
    va, *vm = fence((va, *vm))
    ha = from_a(va)
    n = LX + 8
    u0, ua, ub, um = call(
        second_kernel, "second",
        (odd, hb, vb, ha, va, *vm, source, a1, b1, a2, b2, cond, nu),
        [planes(3, LX + 4), planes(3, 4), planes(3, 4), planes(3, 4)], [padded(3, n)] * 2 + [vmem(3, n)] * 3,
    )
    vb = later(ub, 1)
    va = later(ua, 1)
    around, plain = later_parts(um, 1)
    hb = from_b(vb)
    va, around = fence((va, around))
    ha = from_a(va)
    residual, lb, la, lm, rb, ra, rm = call(
        residual_kernel, "residual",
        (odd, hb, vb, ha, va, around, plain, source, a2, b2, cond, nu, keep, spread, u0),
        [planes(1, 3, LX)] + [planes(3, 4)] * 6, [padded(3, n)] * 2 + [vmem(3, n)] * 2, 1, [ANY] + [VMEM] * 6,
    )
    sb = rb + later(lb, 1)
    hb = from_b(jnp.concatenate([sb.reshape(12, NY, NZ), sb3], axis=0))
    sa3, sb = fence((sa3, sb))
    a3 = from_a(sa3)
    wide_keep, wide_spread = call(
        wide_kernel, "wide", (odd, *tables, keep, spread, a3, hb), [planes(LX + 14)] * 2, [],
    )
    around, plain = later_parts(lm, 1)
    moved, around = fence((later(la, 1), around))
    sa = ra + moved
    ha = from_a(sa)
    sm = rm + (around + plain)
    lb, la, lm = call(
        square_kernel, "square", (odd, hb, sb, ha, sa, sm, keep, spread),
        [planes(3, 4)] * 3, [padded(3, n)] * 2 + [vmem(3, n)],
    )
    tb = sb + later(lb, 2)
    near_b = from_b(tb)
    tm = sm + later(lm, 2)
    far_b = from_b(tm)
    around, plain = later_parts(la, 2)
    ta = sa + (around + plain)
    near_a = from_a(ta)
    far_a = from_a(tm)
    lb, la, lm, bb, ba, bm = call(
        fourth_kernel, "fourth",
        (odd, near_b, tb, far_b, tm, far_a, near_a, ta, u0, wide_keep, wide_spread),
        [planes(3, 4)] * 6, [padded(3, LX + 16)] * 2 + [vmem(3, LX + 16)],
    )
    eb, edge = call(
        edge_kernel, "edge", (odd, bb, later(lb, half)), [planes(3, 4), planes(3, 2)], [],
    )
    hb = from_b(edge)
    moved, hb = fence((later(la, half), hb))
    ea = ba + moved
    ha = from_a(ea)
    em = bm + later(lm, half)
    field = call(
        last_kernel, "last", (odd, hb, eb, ha, ea, em, source, a1, b1, cond, nu),
        planes(2, 3, LX), [padded(3, n)] * 2 + [vmem(3, n)] * 2, 5, ANY,
    )
    return field, residual


def solution(mesh):
    whole = P("tm", None, "space", None, None)
    return jax.shard_map(
        body, mesh=mesh, in_specs=(whole, whole, P("space", None, None), P(), P()),
        out_specs=(whole, whole), check_vma=False,
    )
```

```python
import jax
import jax.numpy as jnp
from jax import lax
from jax.experimental import pallas as pl
from jax.experimental.pallas import tpu as pltpu
from jax.sharding import PartitionSpec as P

LX, NY, NZ = 12, 64, 128
ROWS = pl.ds(8, NY)
F32 = jnp.float32
ANY = pl.BlockSpec(memory_space=pl.ANY)
HBM = pl.BlockSpec(memory_space=pltpu.HBM)
VMEM = pl.BlockSpec(memory_space=pltpu.VMEM)
SMEM = pl.BlockSpec(memory_space=pltpu.SMEM)


def planes(*lead):
    return jax.ShapeDtypeStruct(tuple(lead) + (NY, NZ), F32)


def vmem(*lead):
    return pltpu.VMEM(tuple(lead) + (NY, NZ), F32)


def padded(*lead):
    return pltpu.VMEM(tuple(lead) + (NY + 16, NZ), F32)


def clear(*bufs):
    zero = jnp.zeros((8, NZ), F32)

    def body(i, carry):
        for buf in bufs:
            for c in range(3):
                buf[c, i, pl.ds(0, 8)] = zero
                buf[c, i, pl.ds(NY + 8, 8)] = zero
        return carry

    lax.fori_loop(0, bufs[0].shape[1], body, 0)


def copy_all(pairs, sems, base=0):
    copies = [
        pltpu.make_async_copy(src, dst, sems.at[base + n]) for n, (src, dst) in enumerate(pairs)
    ]
    for copy in copies:
        copy.start()
    return copies


def wait_all(copies):
    for copy in copies:
        copy.wait()


def run_copies(pairs, sems, base=0):
    wait_all(copy_all(pairs, sems, base))


def call(kernel, name, args, outs, scratch, n_sems=0, out_specs=None, in_place=VMEM):
    in_specs = [SMEM if a.ndim == 1 else in_place for a in args]
    single = not isinstance(outs, (list, tuple))
    return pl.pallas_call(
        kernel,
        name=name,
        out_shape=outs,
        in_specs=in_specs,
        out_specs=out_specs or (VMEM if single else [VMEM] * len(outs)),
        scratch_shapes=list(scratch) + [pltpu.SemaphoreType.DMA((n_sems,))] * (n_sems > 0),
        compiler_params=pltpu.CompilerParams(vmem_limit_bytes=20 * 1024 * 1024),
        cost_estimate=pl.CostEstimate(flops=0, bytes_accessed=4 << 20, transcendentals=0),
    )(*args)


def over_layers(lo, hi, step, at_once):
    rounds = (hi - lo) // at_once

    def body(t, carry):
        for k in range(at_once):
            step(lo + t * at_once + k)
        return carry

    lax.fori_loop(0, rounds, body, 0)
    for i in range(lo + rounds * at_once, hi):
        step(i)


def neighbours(src, c, i):
    lane = lax.broadcasted_iota(jnp.int32, (NY, NZ), 1)
    zero = jnp.float32(0.0)
    if src.shape[-2] == NY:
        row = lax.broadcasted_iota(jnp.int32, (NY, NZ), 0)
        a = src[c, i]
        first = src[c, i + 1] + src[c, i - 1]
        up = jnp.where(row == 0, zero, pltpu.roll(a, 1, 0))
        down = jnp.where(row == NY - 1, zero, pltpu.roll(a, NY - 1, 0))
    else:
        a = src[c, i, ROWS]
        first = src[c, i + 1, ROWS] + src[c, i - 1, ROWS]
        up = src[c, i, pl.ds(7, NY)]
        down = src[c, i, pl.ds(9, NY)]
    left = jnp.where(lane == 0, zero, pltpu.roll(a, 1, 1))
    right = jnp.where(lane == NZ - 1, zero, pltpu.roll(a, NZ - 1, 1))
    return (first + (up + down)) + (left + right)


def layer(src, c, i):
    return src[c, i] if src.shape[-2] == NY else src[c, i, ROWS]


def fine_sweep(src, store, held, cond, nu, lo, hi, force=None, off=0):
    def step(i):
        state = [layer(src, c, i) for c in range(3)]
        square = state[0] * state[0] + state[1] * state[1] + state[2] * state[2]
        base = nu[i - off]
        weight = cond[i - off]
        grown = 1.0 + square
        strong = base * (1.0 + 1.5 * square)
        scale = 1.0 / (weight * grown + 6.0 * strong)
        keep = grown * scale
        spread = strong * scale
        for c in range(3):
            if force is not None:
                fixed = weight * state[c] + force[c, i]
                held[c, i] = fixed
            else:
                fixed = held[c, i]
            store(c, i, fixed * keep + neighbours(src, c, i) * spread)

    over_layers(lo, hi, step, (hi - lo) // 2 if hi - lo >= 12 else 6)


def coarse_sweep(src, dst, held, keep, spread, off, lo, hi, first):
    def step(i):
        k = keep[i + off]
        s = spread[i + off]
        for c in range(3):
            if first:
                fixed = k * src[c, i, ROWS]
                held[c, i] = fixed
            else:
                fixed = held[c, i]
            dst[c, i, ROWS] = fixed + s * neighbours(src, c, i)

    over_layers(lo, hi, step, (hi - lo) // 2 if hi - lo >= 12 else 6)


def lookup(code, table):
    first = jnp.where(code == 1, table[0], table[1])
    second = jnp.where(code == 3, table[2], table[3])
    return jnp.where(code <= 2, first, second)


def materials(code, cond_t, nu_t):
    outside = code == 0
    return (
        jnp.where(outside, jnp.float32(1.0), lookup(code, cond_t)),
        jnp.where(outside, jnp.float32(0.0), lookup(code, nu_t)),
    )


def into(buf):
    def store(c, i, value):
        buf[c, i, ROWS] = value
    return store


def edges(odd, n, width):
    return (1 - odd) * (n - width), odd * (n - width)


def first_pack_kernel(odd_ref, g_low, g_high, s_low, s_high, r_low, r_high, a1, b1):
    odd = odd_ref[0]

    def fill(low, high):
        for c in range(3):
            for k in range(2):
                low[2 * c + k] = g_low[0, c, k]
                high[2 * c + k] = g_high[0, c, k]
            low[6 + c] = s_low[0, c, 0]
            high[6 + c] = s_high[0, c, 0]
        low[9] = (r_low[0] + 1).astype(F32)
        high[9] = (r_high[0] + 1).astype(F32)

    @pl.when(odd == 0)
    def even_slab():
        fill(b1, a1)

    @pl.when(odd == 1)
    def odd_slab():
        fill(a1, b1)


def second_pack_kernel(odd_ref, source, regions, a2, b2, a3, b3, reg, sems):
    odd = odd_ref[0]
    pairs = [(regions, reg)]
    for two, start in zip((a2, b2), edges(odd, LX, 3)):
        for c in range(3):
            pairs.append((source.at[0, c, pl.ds(start, 3)], two.at[pl.ds(3 * c, 3)]))
    run_copies(pairs, sems)
    for two, start in zip((a2, b2), edges(odd, LX, 3)):
        for k in range(3):
            two[9 + k] = (reg[start + k] + 1).astype(F32)
    for three, high in ((a3, 1 - odd), (b3, odd)):
        for k in range(4):
            three[k] = (reg[high * (LX - 7) + (1 - high) * 3 + k] + 1).astype(F32)


def first_middle_kernel(cond_t, nu_t, guess, source, regions, out, y, held, cond, nu):
    def prepare(i):
        cond[i], nu[i] = materials(regions[i] + 1, cond_t, nu_t)

    over_layers(3, 9, prepare, 6)
    clear(y)
    fine_sweep(guess.at[0], into(y), held, cond, nu, 3, 9, source.at[1])

    def store(c, i, value):
        out[c, i - 4] = value

    fine_sweep(y, store, held, cond, nu, 4, 8)


def first_kernel(odd_ref, cond_t, nu_t, guess, source, regions, ra, rb, after, out_a, out_b, x, y, held, f, cond, nu):
    odd = odd_ref[0]
    clear(x, y)
    n = LX + 4
    for c in range(3):
        for i in (0, 1, 2, 3, 4, 5, 6, 7, 8, 9, 10, 11):
            x[c, i + 2, ROWS] = guess[0, c, i]
            f[c, i + 2] = source[1, c, i]
    for i in range(LX):
        cond[i + 2], nu[i + 2] = materials(regions[i] + 1, cond_t, nu_t)
    for pack, high in ((ra, 1 - odd), (rb, odd)):
        for c in range(3):
            for k in range(2):
                x[c, high * (n - 2) + k, ROWS] = pack[2 * c + k]
            f[c, 1 + high * (n - 3)] = pack[6 + c]
        cond[1 + high * (n - 3)], nu[1 + high * (n - 3)] = materials(pack[9], cond_t, nu_t)
    fine_sweep(x, into(y), held, cond, nu, 1, 7, f)
    fine_sweep(x, into(y), held, cond, nu, 9, n - 1, f)
    fine_sweep(y, into(x), held, cond, nu, 2, 6)
    fine_sweep(y, into(x), held, cond, nu, 10, 14)
    for c in range(3):
        for k in range(4):
            out_a[c, k] = x[c, 2 + (1 - odd) * 8 + k, ROWS]
            out_b[c, k] = x[c, 2 + odd * 8 + k, ROWS]


def material_kernel(odd_ref, cond_t, nu_t, regions, ra, rb, cond, nu, keep, spread):
    odd = odd_ref[0]

    def fill(at, code):
        cv, nv = materials(code, cond_t, nu_t)
        cond[at] = cv
        nu[at] = nv
        half = 0.5 * cv
        scale = 1.0 / (half + 6.0 * nv)
        keep[at] = half * scale
        spread[at] = nv * scale

    for i in range(LX):
        fill(3 + i, regions[i] + 1)
    for pack, high in ((ra, 1 - odd), (rb, odd)):
        for k in range(3):
            fill(high * (LX + 3) + k, pack[9 + k])


def wide_kernel(odd_ref, cond_t, nu_t, keep_i, spread_i, ra, rb, keep, spread):
    odd = odd_ref[0]
    for i in range(LX + 6):
        keep[i + 4] = keep_i[i]
        spread[i + 4] = spread_i[i]
    for pack, start, high in ((ra, 0, 1 - odd), (rb, 12, odd)):
        for k in range(4):
            at = high * (LX + 10) + k
            cv, nv = materials(pack[start + k], cond_t, nu_t)
            half = 0.5 * cv
            scale = 1.0 / (half + 6.0 * nv)
            keep[at] = half * scale
            spread[at] = nv * scale


def extend(odd, pieces, halos, x):
    a, b, *m = pieces
    ha, hb = halos
    for c in range(3):
        for k in range(4):
            middle = m[0][c, k]
            for other in m[1:]:
                middle = middle + other[c, k]
            x[c, 8 + k, ROWS] = middle
            x[c, 4 + (1 - odd) * 8 + k, ROWS] = a[c, k]
            x[c, 4 + odd * 8 + k, ROWS] = b[c, k]
            x[c, (1 - odd) * 16 + k, ROWS] = ha[c, k]
            x[c, odd * 16 + k, ROWS] = hb[c, k] if len(hb.shape) == 4 else hb[4 * c + k]


def extend_force(odd, source, which, width, packs, start, f):
    for c in range(3):
        for i in range(LX):
            f[c, 4 + i] = source[which, c, i]
        for pack, high in ((packs[0], 1 - odd), (packs[1], odd)):
            for k in range(width):
                f[c, 4 - width + high * (LX + width) + k] = pack[start + width * c + k]


def second_kernel(
    odd_ref, hb, vb, ha, va, vm, vn, source, a1, b1, a2, b2, cond, nu,
    u0, oa, ob, om, x, y, held, f0, f1,
):
    odd = odd_ref[0]
    clear(x, y)
    extend(odd, (va, vb, vm, vn), (ha, hb), x)
    extend_force(odd, source, 0, 3, (a2, b2), 0, f0)
    extend_force(odd, source, 1, 1, (a1, b1), 6, f1)

    def keep_u0(c, i, value):
        x[c, i, ROWS] = value
        u0[c, i - 2] = value

    fine_sweep(x, into(y), held, cond, nu, 1, 19, f0, 1)
    fine_sweep(y, keep_u0, held, cond, nu, 2, 18, None, 1)
    fine_sweep(x, into(y), held, cond, nu, 3, 17, f1, 1)
    fine_sweep(y, into(x), held, cond, nu, 4, 16, None, 1)
    for c in range(3):
        for k in range(4):
            om[c, k] = x[c, 8 + k, ROWS]
            oa[c, k] = x[c, 4 + (1 - odd) * 8 + k, ROWS]
            ob[c, k] = x[c, 4 + odd * 8 + k, ROWS]


def split(odd, x, start, b, a, m):
    for c in range(3):
        for k in range(4):
            b[c, k] = x[c, start + odd * 8 + k, ROWS]
            a[c, k] = x[c, start + (1 - odd) * 8 + k, ROWS]
            m[c, k] = x[c, start + 4 + k, ROWS]


def residual_kernel(
    odd_ref, hb, vb, ha, va, vm, vn, source, a2, b2, cond, nu, keep, spread, u0,
    res_o, lb, la, lm, rb, ra, rm, x, y, held, f0, sems,
):
    odd = odd_ref[0]
    clear(x, y)
    extend(odd, (va, vb, vm, vn), (ha, hb), x)
    extend_force(odd, source, 0, 3, (a2, b2), 0, f0)

    def less(c, i, value):
        x[c, i, ROWS] = value - u0[c, i - 2]

    fine_sweep(x, into(y), held, cond, nu, 1, 19, f0, 1)
    fine_sweep(y, less, held, cond, nu, 2, 18, None, 1)
    kept = copy_all([(x.at[:, pl.ds(4, LX), ROWS], res_o.at[0])], sems)
    split(odd, x, 4, rb, ra, rm)
    coarse_sweep(x, y, held, keep, spread, -1, 3, 17, True)
    wait_all(kept)
    coarse_sweep(y, x, held, keep, spread, -1, 4, 16, False)
    split(odd, x, 4, lb, la, lm)


def square_kernel(odd_ref, hb, sb, ha, sa, sm, keep, spread, ob, oa, om, x, y, held):
    odd = odd_ref[0]
    clear(x, y)
    extend(odd, (sa, sb, sm), (ha, hb), x)
    for lo in (1, 3):
        coarse_sweep(x, y, held, keep, spread, -1, lo, 20 - lo, True)
        coarse_sweep(y, x, held, keep, spread, -1, lo + 1, 19 - lo, False)
    split(odd, x, 4, ob, oa, om)


def fourth_kernel(
    odd_ref, near_b, tb, far_b, tm, far_a, near_a, ta, u0, keep, spread,
    ob, oa, om, bb, ba, bm, x, y, held,
):
    odd = odd_ref[0]
    clear(x, y)
    for c in range(3):
        for k in range(4):
            x[c, 8 + odd * 8 + k, ROWS] = tb[c, k]
            x[c, 8 + (1 - odd) * 8 + k, ROWS] = ta[c, k]
            x[c, 12 + k, ROWS] = tm[c, k]
            x[c, 4 + odd * 16 + k, ROWS] = near_b[c, k]
            x[c, 4 + (1 - odd) * 16 + k, ROWS] = near_a[c, k]
            x[c, odd * 24 + k, ROWS] = far_b[c, k]
            x[c, (1 - odd) * 24 + k, ROWS] = far_a[c, k]
    for c in range(3):
        for k in range(4):
            bb[c, k] = tb[c, k] + u0[c, 2 + odd * 8 + k]
            ba[c, k] = ta[c, k] + u0[c, 2 + (1 - odd) * 8 + k]
            bm[c, k] = tm[c, k] + u0[c, 6 + k]
    for lo in (1, 3, 5, 7):
        coarse_sweep(x, y, held, keep, spread, -1, lo, 28 - lo, True)
        coarse_sweep(y, x, held, keep, spread, -1, lo + 1, 27 - lo, False)
    split(odd, x, 8, ob, oa, om)


def edge_kernel(odd_ref, base, moved, total, edge):
    odd = odd_ref[0]
    for c in range(3):
        for k in range(4):
            total[c, k] = base[c, k] + moved[c, k]
        for k in range(2):
            edge[c, k] = total[c, odd * 2 + k]


def last_kernel(
    odd_ref, hb, eb, ha, ea, em, source, a1, b1, cond, nu, field, x, y, held, f1, sems,
):
    odd = odd_ref[0]
    clear(x, y)
    kept = copy_all(
        [
            (eb, field.at[0, :, pl.ds(odd * 8, 4)]),
            (ea, field.at[0, :, pl.ds((1 - odd) * 8, 4)]),
            (em, field.at[0, :, pl.ds(4, 4)]),
        ],
        sems,
    )
    extend_force(odd, source, 1, 1, (a1, b1), 6, f1)
    for c in range(3):
        for k in range(4):
            x[c, 4 + odd * 8 + k, ROWS] = eb[c, k]
            x[c, 4 + (1 - odd) * 8 + k, ROWS] = ea[c, k]
            x[c, 8 + k, ROWS] = em[c, k]
        for k in range(2):
            x[c, 2 + odd * 14 + k, ROWS] = hb[c, k]
            x[c, 2 + (1 - odd) * 14 + k, ROWS] = ha[c, odd * 2 + k]
    fine_sweep(x, into(y), held, cond, nu, 3, 17, f1, 1)
    fine_sweep(y, into(x), held, cond, nu, 4, 10, None, 1)
    kept += copy_all([(x.at[:, pl.ds(4, 6), ROWS], field.at[1, :, pl.ds(0, 6)])], sems, 3)
    fine_sweep(y, into(x), held, cond, nu, 10, 16, None, 1)
    kept += copy_all([(x.at[:, pl.ds(10, 6), ROWS], field.at[1, :, pl.ds(6, 6)])], sems, 4)
    wait_all(kept)


def body(guess, source, regions, conductance, reluct):
    slices = lax.axis_size("tm")
    slabs = lax.axis_size("space")
    odd = (lax.axis_index("space") % 2).astype(jnp.int32).reshape(1)
    on_chip = [(i, i ^ 1) for i in range(slabs)]
    off_chip = [(i, i + 1) for i in range(1, slabs - 1, 2)]
    off_chip += [(j, i) for i, j in off_chip]
    fence = lax.optimization_barrier

    def from_a(x):
        return lax.ppermute(x, "space", on_chip)

    def from_b(x):
        return lax.ppermute(x, "space", off_chip)

    half = slices // 2

    def along(x, pairs):
        return lax.ppermute(x, "tm", pairs)

    def later(x, distance):
        return along(x, [(i, (i + distance) % slices) for i in range(slices)])

    def later_parts(x, distance):
        wrapping = [i for i in range(slices) if i % half + distance >= half]
        across = along(x, [(i, (i + half) % slices) for i in wrapping])
        around = along(across, [((i + half) % slices, (i + distance) % slices) for i in wrapping])
        plain = along(x, [(i, i + distance) for i in range(slices) if i not in wrapping])
        return around, plain

    tables = (conductance, reluct)
    sa1, sb1 = call(
        first_pack_kernel, "first_pack",
        (odd, guess[:1, :, :2], guess[:1, :, LX - 2:], source[1:, :, :1], source[1:, :, LX - 1:], regions[:1], regions[LX - 1:]),
        [planes(10), planes(10)], [],
    )
    b1 = from_b(sb1)
    a1 = from_a(sa1)
    um = call(
        first_middle_kernel, "first_middle", (*tables, guess, source, regions),
        planes(3, 4), [padded(3, LX), vmem(3, LX)] + [vmem(LX)] * 2,
    )
    sa2, sb2, sa3, sb3 = call(
        second_pack_kernel, "second_pack", (odd, source, regions),
        [planes(12), planes(12), planes(4), planes(4)], [pltpu.VMEM((LX, NY, NZ), jnp.int32)], 8, in_place=HBM,
    )
    vm = later_parts(um, 1)
    sb2, sa2, b1 = fence((sb2, sa2, b1))
    b2 = from_b(sb2)
    a2 = from_a(sa2)
    ua, ub = call(
        first_kernel, "first", (odd, *tables, guess, source, regions, a1, b1, um),
        [planes(3, 4), planes(3, 4)], [padded(3, LX + 4)] * 2 + [vmem(3, LX + 4)] * 2 + [vmem(LX + 4)] * 2,
    )
    vb = later(ub, 1)
    va = later(ua, 1)
    cond, nu, keep, spread = call(
        material_kernel, "material", (odd, *tables, regions, a2, b2), [planes(LX + 6)] * 4, [],
    )
    vb, cond = fence((vb, cond))
    hb = from_b(vb)
    va, *vm = fence((va, *vm))
    ha = from_a(va)
    n = LX + 8
    u0, ua, ub, um = call(
        second_kernel, "second",
        (odd, hb, vb, ha, va, *vm, source, a1, b1, a2, b2, cond, nu),
        [planes(3, LX + 4), planes(3, 4), planes(3, 4), planes(3, 4)], [padded(3, n)] * 2 + [vmem(3, n)] * 3,
    )
    vb = later(ub, 1)
    va = later(ua, 1)
    around, plain = later_parts(um, 1)
    hb = from_b(vb)
    va, around = fence((va, around))
    ha = from_a(va)
    residual, lb, la, lm, rb, ra, rm = call(
        residual_kernel, "residual",
        (odd, hb, vb, ha, va, around, plain, source, a2, b2, cond, nu, keep, spread, u0),
        [planes(1, 3, LX)] + [planes(3, 4)] * 6, [padded(3, n)] * 2 + [vmem(3, n)] * 2, 1, [ANY] + [VMEM] * 6,
    )
    sb = rb + later(lb, 1)
    hb = from_b(jnp.concatenate([sb.reshape(12, NY, NZ), sb3], axis=0))
    sa3, sb = fence((sa3, sb))
    a3 = from_a(sa3)
    wide_keep, wide_spread = call(
        wide_kernel, "wide", (odd, *tables, keep, spread, a3, hb), [planes(LX + 14)] * 2, [],
    )
    around, plain = later_parts(lm, 1)
    moved, around = fence((later(la, 1), around))
    sa = ra + moved
    ha = from_a(sa)
    sm = rm + (around + plain)
    lb, la, lm = call(
        square_kernel, "square", (odd, hb, sb, ha, sa, sm, keep, spread),
        [planes(3, 4)] * 3, [padded(3, n)] * 2 + [vmem(3, n)],
    )
    tb = sb + later(lb, 2)
    near_b = from_b(tb)
    tm = sm + later(lm, 2)
    far_b = from_b(tm)
    ta = sa + later(la, 2)
    near_a = from_a(ta)
    far_a = from_a(tm)
    lb, la, lm, bb, ba, bm = call(
        fourth_kernel, "fourth",
        (odd, near_b, tb, far_b, tm, far_a, near_a, ta, u0, wide_keep, wide_spread),
        [planes(3, 4)] * 6, [padded(3, LX + 16)] * 2 + [vmem(3, LX + 16)],
    )
    eb, edge = call(
        edge_kernel, "edge", (odd, bb, later(lb, half)), [planes(3, 4), planes(3, 2)], [],
    )
    hb = from_b(edge)
    moved, hb = fence((later(la, half), hb))
    ea = ba + moved
    ha = from_a(ea)
    em = bm + later(lm, half)
    field = call(
        last_kernel, "last", (odd, hb, eb, ha, ea, em, source, a1, b1, cond, nu),
        planes(2, 3, LX), [padded(3, n)] * 2 + [vmem(3, n)] * 2, 5, ANY,
    )
    return field, residual


def solution(mesh):
    whole = P("tm", None, "space", None, None)
    return jax.shard_map(
        body, mesh=mesh, in_specs=(whole, whole, P("space", None, None), P(), P()),
        out_specs=(whole, whole), check_vma=False,
    )
```
